32 devices in a mesh: context: 4 (over y, x), expert: 8 (over z, core).
Axes of the slice: x: 2, y: 2, z: 4, core: 2. Of those that a mesh axis runs over, the one named last changes fastest.
Arguments:
- tokens: bfloat16 [8, 512, 2048], P('expert', 'context'), may hold values from -6 to 6
- span_order: int32 [8, 8], P('expert'), may hold values from 0 to 7, each once within a row
- expert_ids: int32 [8, 512, 8], P('expert', 'context'), may hold values from 0 to 31, all different within a row; in each aligned block of 128 rows (0 to 127, 128 to 255, ..., all dimensions but the last counted through in order) at most 64 rows name the same one
- norm_gain: float32 [2048], replicated, may hold values from 0.3 to 3
- w_query: bfloat16 [2048, 4096], P(('context', 'expert')), may hold values from -0.125 to 0.125
- key_projection_weight: bfloat16 [2048, 512], P(('context', 'expert')), may hold values from -0.125 to 0.125
- value_projection_weight: bfloat16 [2048, 512], P(('context', 'expert')), may hold values from -0.125 to 0.125
- query_gain: float32 [128], replicated, may hold values from 0.5 to 2
- key_gain: float32 [128], replicated, may hold values from 0.5 to 2
- w_out: bfloat16 [4096, 2048], P(('context', 'expert')), may hold values from -0.75 to 0.75
- post_gain: float32 [2048], replicated, may hold values from 0.3 to 3
- w_router: bfloat16 [2048, 32], P(('context', 'expert')), may hold values from -0.044189453 to 0.044189453
- w_gate: bfloat16 [32, 2048, 768], P(('context', 'expert')), may hold values from -0.125 to 0.125
- w_up: bfloat16 [32, 2048, 768], P(('context', 'expert')), may hold values from -0.125 to 0.125
- w_down: bfloat16 [32, 768, 2048], P(('context', 'expert')), may hold values from -0.875 to 0.875
- cotangent: bfloat16 [8, 512, 2048], P('expert', 'context'), may hold values from -6 to 6
Outputs:
- out: bfloat16 [8, 512, 2048], P('expert', 'context')
- grad_tokens: float32 [8, 512, 2048], P('expert', 'context')
- grad_norm_gain: float32 [2048], replicated
- grad_w_query: float32 [2048, 4096], P(('context', 'expert'))
- grad_w_key: float32 [2048, 512], P(('context', 'expert'))
- grad_w_value: float32 [2048, 512], P(('context', 'expert'))
- grad_query_gain: float32 [128], replicated
- grad_key_gain: float32 [128], replicated
- grad_w_out: float32 [4096, 2048], P(('context', 'expert'))
- grad_post_gain: float32 [2048], replicated
- grad_w_router: float32 [2048, 32], P(('context', 'expert'))
- grad_w_gate: float32 [32, 2048, 768], P(('context', 'expert'))
- grad_w_up: float32 [32, 2048, 768], P(('context', 'expert'))
- grad_w_down: float32 [32, 768, 2048], P(('context', 'expert'))
The draws below stay inside these ranges and needn't reach their ends.
Inputs may be any that keep to these rules, and one draw needn't show every extreme that they name: Each row is a permutation: stored block c of a sequence holds positions span_order[c] * 64 to span_order[c] * 64 + 63. `expert_ids`: each token names 8 different experts. Among the 128 tokens of one device (aligned blocks along a sequence) no expert is named more than 64 times, and on some device some expert is named exactly 64 times.
All inputs are finite; a program needn't handle non-finite values.
Results may differ from the reference program's by a relative error of at most 0.024.
Values may be sent and summed in bfloat16 or wider, within the bound.
No kernel may reach another device: no remote copies, remote signals or barrier semaphores. Data moves between devices by JAX's collectives and lax.ppermute only.
A program may use at most 256 MiB of HBM per device.

```python
import math
import jax
import jax.numpy as jnp
import numpy as np
from jax import lax

MODEL_DIM = 2048
QUERY_HEADS = 32
KEY_VALUE_HEADS = 4
HEAD_DIM = 128
FFE = 768
TOPK = 8
TOK_DEV = 128
EXPERTS = 32
SEQUENCE_LENGTH = 512
SEQUENCE_COUNT = 8
CAP = 64
N_CONTEXT = 4
N_EXPERT = 8


def steps_of(own_key, extent, shards, low, high):
    def one(axis_at, blocks):
        draws = jax.random.uniform(jax.random.fold_in(jax.random.fold_in(own_key, 6), axis_at), (blocks,), jnp.float32, low / len(shards), high / len(shards))
        return jnp.repeat(jnp.exp(draws), extent[axis_at] // blocks).reshape((-1,) + (1,) * (len(extent) - axis_at - 1))

    factor_of = one(*shards[0])
    for cut in shards[1:]:
        factor_of = factor_of * one(*cut)
    return factor_of


def shared_out(own_key, own, number, rows, count, top, limit, slope):
    sequence = jax.random.permutation(own_key, count)
    heavy_load, usual = shares(count, rows * top, limit, slope, True), shares(count, rows * top, limit, slope, False)
    places = jnp.arange(count)

    def named(sizes, rotation):
        used = int((sizes > 0).sum())
        fixed = max(1, used // 4)
        passed = fixed + (places - fixed + rotation * (used - fixed)) % max(1, count - fixed)
        return jnp.zeros((count,), jnp.int32).at[sequence[jnp.where(places < fixed, places, passed)]].set(jnp.asarray(sizes, jnp.int32))

    sizes = jnp.where(number % 4 == 0, named(heavy_load, number // 4), named(usual, number - number // 4 - 1))
    mixed = jax.random.permutation(jax.random.fold_in(own, 3), count)
    donor, receiver = mixed[0:count // 2 * 2:2], mixed[1:count // 2 * 2:2]
    room = jnp.minimum(sizes[donor] - 1, limit - sizes[receiver]) // 2
    room = jnp.where((donor == sequence[0]) | (receiver == sequence[0]) | (sizes[receiver] == 0), 0, jnp.maximum(room, 0))
    passed = jax.random.randint(jax.random.fold_in(own, 4), (count // 2,), 0, 1 << 20) % (room + 1)
    sizes = sizes.at[donor].add(-passed).at[receiver].add(passed)
    items = jnp.searchsorted(jnp.cumsum(sizes), jnp.arange(rows * top), side="right").astype(jnp.int32)
    listing = items.reshape(top, rows).T
    listing = listing[jax.random.permutation(jax.random.fold_in(own, 1), rows)]
    rotation = jax.random.randint(jax.random.fold_in(own, 2), (rows, 1), 0, top)
    return jnp.take_along_axis(listing, (jnp.arange(top)[None, :] + rotation) % top, axis=1)


def shares(amount, total, most, skew, full):
    portions = [(1 << 20) // math.isqrt(rank ** skew) + 1 for rank in range(1, amount + 1)]
    largest = most if full else min(most, max(-(-total // amount), total * portions[0] // sum(portions)))
    least = 1 if total - largest >= amount - 1 else 0
    given, rest = [largest] + [least] * (amount - 1), total - largest - least * (amount - 1)
    while rest > 0:
        movable = [i for i in range(1, amount) if given[i] < largest] or [i for i in range(1, amount) if given[i] < most]
        whole, budget = sum([portions[i] for i in movable]), rest
        for i in movable:
            extra = min(most - given[i], max(1, budget * portions[i] // whole), rest)
            given[i] = given[i] + extra
            rest = rest - extra
    return np.array(given)


def noise(stream_key, shape, spread, bound, cuts=(), kind=jnp.bfloat16):
    entries = jax.random.normal(stream_key, shape, jnp.float32) * spread
    if len(cuts) > 0:
        entries = steps_of(stream_key, shape, cuts, -0.22, 0.18) * entries
    return jnp.clip(entries, min=-bound, max=bound).astype(kind)


def setup_inputs(seed: int = 0) -> dict:
    splits = jax.random.split(jax.random.key(seed), 17)
    tokens = noise(splits[0], (SEQUENCE_COUNT, SEQUENCE_LENGTH, MODEL_DIM), 1.0, 6.0, ((0, 8), (1, 4)))
    span_order = jax.vmap(lambda own: jax.random.permutation(own, 2 * N_CONTEXT))(jax.random.split(splits[1], SEQUENCE_COUNT)).reshape((SEQUENCE_COUNT, 2 * N_CONTEXT)).astype(jnp.int32)
    expert_ids_keys = jax.random.split(jax.random.fold_in(splits[2], 1), SEQUENCE_COUNT * SEQUENCE_LENGTH // TOK_DEV)
    expert_ids_turns = jax.random.permutation(jax.random.fold_in(splits[2], 3), SEQUENCE_COUNT * SEQUENCE_LENGTH // TOK_DEV)
    expert_ids = jax.vmap(lambda own, number: shared_out(jax.random.fold_in(splits[2], 2), own, number, TOK_DEV, EXPERTS, TOPK, CAP, 2))(expert_ids_keys, expert_ids_turns).reshape((SEQUENCE_COUNT, SEQUENCE_LENGTH, TOPK))
    norm_gain = jnp.clip(jnp.exp(jax.random.uniform(splits[3], (MODEL_DIM,), jnp.float32, math.log(0.3), math.log(3.0))), 0.3, 3.0)
    w_query = noise(splits[4], (MODEL_DIM, QUERY_HEADS * HEAD_DIM), MODEL_DIM ** -0.5, 0.125, ((0, 32),))
    key_projection_weight = noise(splits[5], (MODEL_DIM, KEY_VALUE_HEADS * HEAD_DIM), MODEL_DIM ** -0.5, 0.125, ((0, 32),))
    value_projection_weight = noise(splits[6], (MODEL_DIM, KEY_VALUE_HEADS * HEAD_DIM), MODEL_DIM ** -0.5, 0.125, ((0, 32),))
    query_gain = jnp.clip(jnp.exp(jax.random.uniform(splits[7], (HEAD_DIM,), jnp.float32, math.log(0.5), math.log(2.0))), 0.5, 2.0)
    key_gain = jnp.clip(jnp.exp(jax.random.uniform(splits[8], (HEAD_DIM,), jnp.float32, math.log(0.5), math.log(2.0))), 0.5, 2.0)
    w_out = noise(splits[9], (QUERY_HEADS * HEAD_DIM, MODEL_DIM), (QUERY_HEADS * HEAD_DIM // 64) ** -0.5, 0.75, ((0, 32),))
    post_gain = jnp.clip(jnp.exp(jax.random.uniform(splits[10], (MODEL_DIM,), jnp.float32, math.log(0.3), math.log(3.0))), 0.3, 3.0)
    w_router = noise(splits[11], (MODEL_DIM, EXPERTS), (0.36 / MODEL_DIM ** 0.5), 0.044189453, ((0, 32),))
    w_gate = noise(splits[12], (EXPERTS, MODEL_DIM, FFE), MODEL_DIM ** -0.5, 0.125, ((0, 32),))
    w_up = noise(splits[13], (EXPERTS, MODEL_DIM, FFE), MODEL_DIM ** -0.5, 0.125, ((0, 32),))
    w_down = noise(splits[14], (EXPERTS, FFE, MODEL_DIM), (FFE // 16) ** -0.5, 0.875, ((0, 32),))
    cotangent = noise(splits[15], (SEQUENCE_COUNT, SEQUENCE_LENGTH, MODEL_DIM), 1.0, 6.0, ((0, 8), (1, 4)))
    return {"tokens": tokens, "span_order": span_order, "expert_ids": expert_ids, "norm_gain": norm_gain, "w_query": w_query, "key_projection_weight": key_projection_weight, "value_projection_weight": value_projection_weight, "query_gain": query_gain, "key_gain": key_gain, "w_out": w_out, "post_gain": post_gain, "w_router": w_router, "w_gate": w_gate, "w_up": w_up, "w_down": w_down, "cotangent": cotangent}


highest_precision = lax.Precision.HIGHEST
epsilon = 1e-06
rotary_base = 1000000.0
very_negative = -1e+30

@jax.custom_vjp
def low(v):
    return lax.optimization_barrier(v.astype(jnp.bfloat16)).astype(jnp.float32)

@jax.custom_vjp
def low_back(v):
    return v

def low_keep(v):
    return (low(v), None)

def low_pass(kept, grad):
    return (grad,)

def back_keep(v):
    return (v, None)

def back_low(kept, grad):
    return (low(grad),)
low.defvjp(low_keep, low_pass)
low_back.defvjp(back_keep, back_low)

def rms_norm(values, scale_gain):
    return values * lax.rsqrt(lax.optimization_barrier(jnp.mean(values * values, axis=-1, keepdims=True)) + epsilon) * scale_gain

def rotary_tables(token_positions, head_width):
    half_width = head_width // 2
    frequency = rotary_base ** (-jnp.arange(half_width, dtype=jnp.float32) * 2.0 / head_width)
    angles = token_positions.astype(jnp.float32)[:, None] * frequency[None, :]
    return (jnp.cos(angles)[:, None, :], jnp.sin(angles)[:, None, :])

def rotate(values, cosine_table, sine_table, direction):
    half_width = values.shape[-1] // 2
    first_half = values[..., :half_width]
    second_half = values[..., half_width:]
    return jnp.concatenate([first_half * cosine_table - direction * second_half * sine_table, second_half * cosine_table + direction * first_half * sine_table], axis=-1)

def attend_heads(packed):
    query_rows, key_rows, values, token_positions = packed
    query_group_count = QUERY_HEADS // KEY_VALUE_HEADS
    grouped_queries = query_rows.reshape(SEQUENCE_LENGTH, KEY_VALUE_HEADS, query_group_count, HEAD_DIM)
    block_rows = min(512, SEQUENCE_LENGTH)

    def one_block(first_row):
        block_queries = lax.dynamic_slice_in_dim(grouped_queries, first_row, block_rows, 0)
        block_places = lax.dynamic_slice_in_dim(token_positions, first_row, block_rows, 0)
        scores = low_back(jnp.einsum('qhgd,khd->hgqk', block_queries, key_rows, precision=highest_precision) * HEAD_DIM ** (-0.5))
        visible = block_places[:, None] >= token_positions[None, :]
        scores = jnp.where(visible[None, None], scores, very_negative)
        weights = jax.nn.softmax(scores, axis=-1)
        return jnp.einsum('hgqk,khd->qhgd', low(weights), values, precision=highest_precision)
    firsts = jnp.arange(SEQUENCE_LENGTH // block_rows, dtype=jnp.int32) * block_rows
    result = lax.map(jax.checkpoint(one_block), firsts)
    return result.reshape(SEQUENCE_LENGTH, QUERY_HEADS, HEAD_DIM)

def layer(inputs, norm_gain, w_query, key_projection_weight, value_projection_weight, query_gain, key_gain, w_out, post_gain, w_router, w_gate, w_up, w_down, token_positions, gather_rows, pair_place, expert_ids):
    token_rows = inputs.reshape(SEQUENCE_COUNT * SEQUENCE_LENGTH, MODEL_DIM)
    activation_output = low(rms_norm(token_rows, norm_gain))
    query_raw = low_back(jnp.dot(activation_output, w_query, precision=highest_precision)).reshape(SEQUENCE_COUNT * SEQUENCE_LENGTH, QUERY_HEADS, HEAD_DIM)
    key_unrotated = low_back(jnp.dot(activation_output, key_projection_weight, precision=highest_precision)).reshape(SEQUENCE_COUNT * SEQUENCE_LENGTH, KEY_VALUE_HEADS, HEAD_DIM)
    value_prepared = low(low_back(jnp.dot(activation_output, value_projection_weight, precision=highest_precision))).reshape(SEQUENCE_COUNT, SEQUENCE_LENGTH, KEY_VALUE_HEADS, HEAD_DIM)
    cosine_table, sine_table = rotary_tables(token_positions.reshape(-1), HEAD_DIM)
    query_prepared = low(low_back(rotate(rms_norm(query_raw, query_gain), cosine_table, sine_table, 1.0)))
    key_prepared = low(low_back(rotate(rms_norm(key_unrotated, key_gain), cosine_table, sine_table, 1.0)))
    attended_output = lax.map(attend_heads, (query_prepared.reshape(SEQUENCE_COUNT, SEQUENCE_LENGTH, QUERY_HEADS, HEAD_DIM), key_prepared.reshape(SEQUENCE_COUNT, SEQUENCE_LENGTH, KEY_VALUE_HEADS, HEAD_DIM), value_prepared, token_positions))
    attn_rows = low(low_back(attended_output.reshape(SEQUENCE_COUNT * SEQUENCE_LENGTH, QUERY_HEADS * HEAD_DIM)))
    residual = token_rows + low_back(jnp.dot(attn_rows, w_out, precision=highest_precision))
    mixed = low(rms_norm(residual, post_gain))
    logits = low_back(jnp.dot(mixed, w_router, precision=highest_precision))
    chosen = jnp.take_along_axis(logits, expert_ids.reshape(SEQUENCE_COUNT * SEQUENCE_LENGTH, TOPK), axis=1)
    gates = jax.nn.softmax(chosen, axis=-1)
    padded = jnp.concatenate([mixed, jnp.zeros((1, MODEL_DIM), mixed.dtype)], axis=0)

    def expert_block(packed):
        picks, gate_weight, up_weight, down_weight = packed
        rows_in = low_back(padded[picks])
        gate_pre = low_back(jnp.dot(rows_in, gate_weight, precision=highest_precision))
        up_pre = low_back(jnp.dot(rows_in, up_weight, precision=highest_precision))
        hidden = low(jax.nn.silu(gate_pre) * up_pre)
        return low(low_back(jnp.dot(hidden, down_weight, precision=highest_precision)))
    expert_rows_out = lax.map(jax.checkpoint(expert_block), (gather_rows, w_gate, w_up, w_down))
    pair_out = expert_rows_out.reshape(-1, MODEL_DIM)[pair_place].reshape(SEQUENCE_COUNT * SEQUENCE_LENGTH, TOPK, MODEL_DIM)
    final = residual + lax.optimization_barrier(jnp.sum(gates[:, :, None] * pair_out, axis=1))
    return final.reshape(SEQUENCE_COUNT, SEQUENCE_LENGTH, MODEL_DIM)

def reference(tokens, span_order, expert_ids, norm_gain, w_query, key_projection_weight, value_projection_weight, query_gain, key_gain, w_out, post_gain, w_router, w_gate, w_up, w_down, cotangent):
    span_rows = SEQUENCE_LENGTH // (2 * N_CONTEXT)
    storage = jnp.arange(SEQUENCE_LENGTH, dtype=jnp.int32)
    token_positions = (jnp.take(span_order, storage // span_rows, axis=1) * span_rows + storage % span_rows).astype(jnp.int32)
    flat_ids = expert_ids.reshape(-1).astype(jnp.int32)
    pair_count = SEQUENCE_COUNT * SEQUENCE_LENGTH * TOPK
    per_expert = N_CONTEXT * N_EXPERT * CAP
    sorted_order = jnp.argsort(flat_ids, stable=True).astype(jnp.int32)
    counts = lax.optimization_barrier(jnp.sum((flat_ids[:, None] == jnp.arange(EXPERTS, dtype=jnp.int32)[None, :]).astype(jnp.int32), axis=0))
    starts = (jnp.cumsum(counts) - counts).astype(jnp.int32)
    sorted_ids = flat_ids[sorted_order]
    ranks = (jnp.arange(pair_count, dtype=jnp.int32) - starts[sorted_ids]).astype(jnp.int32)
    targets = (sorted_ids * per_expert + ranks).astype(jnp.int32)
    table = jnp.full((EXPERTS * per_expert,), pair_count, jnp.int32).at[targets].set(sorted_order)
    gather_rows = (table // TOPK).astype(jnp.int32).reshape(EXPERTS, per_expert)
    pair_place = jnp.zeros((pair_count,), jnp.int32).at[sorted_order].set(targets)
    float_args = tuple((array_in.astype(jnp.float32) for array_in in (tokens, norm_gain, w_query, key_projection_weight, value_projection_weight, query_gain, key_gain, w_out, post_gain, w_router, w_gate, w_up, w_down)))

    def forward(*params):
        return layer(*params, token_positions, gather_rows, pair_place, expert_ids)
    final, pullback = jax.vjp(forward, *float_args)
    gradients = pullback(cotangent.astype(jnp.float32))
    return (final.astype(jnp.bfloat16), gradients[0], gradients[1], gradients[2], gradients[3], gradients[4], gradients[5], gradients[6], gradients[7], gradients[8], gradients[9], gradients[10], gradients[11], gradients[12])
```

```python
import jax
import jax.numpy as jnp
from jax import lax
from jax.sharding import PartitionSpec as P

epsilon = 1e-06
rotary_base = 1000000.0
very_negative = -1e30


def norm_forward(values, scale_gain):
    inverse = lax.rsqrt(jnp.mean(values * values, axis=-1, keepdims=True) + epsilon)
    return (values * inverse * scale_gain, inverse)


def norm_backward(values, inverse, scale_gain, upstream):
    normed = values * inverse
    weighted = upstream * scale_gain
    inner = jnp.mean(weighted * normed, axis=-1, keepdims=True)
    return (inverse * (weighted - normed * inner), upstream * normed)


def rotary_tables(token_positions, head_width):
    half_width = head_width // 2
    frequency = rotary_base ** (-jnp.arange(half_width, dtype=jnp.float32) * 2.0 / head_width)
    angles = token_positions.astype(jnp.float32)[:, None] * frequency[None, :]
    return (jnp.cos(angles)[:, None, :], jnp.sin(angles)[:, None, :])


def rotate(values, cosine_table, sine_table, direction):
    half_width = values.shape[-1] // 2
    first_half = values[..., :half_width]
    second_half = values[..., half_width:]
    return jnp.concatenate(
        [
            first_half * cosine_table - direction * second_half * sine_table,
            second_half * cosine_table + direction * first_half * sine_table,
        ],
        axis=-1,
    )


def head_rows(array_in, kv_heads, query_group_count):
    row_total = array_in.shape[0]
    return (
        array_in.reshape(row_total, kv_heads, query_group_count, -1)
        .transpose(1, 2, 0, 3)
        .reshape(kv_heads, query_group_count * row_total, -1)
    )


def token_rows_of(array_in, kv_heads, query_group_count, tok_rows):
    return (
        array_in.reshape(kv_heads, query_group_count, tok_rows, -1)
        .transpose(2, 0, 1, 3)
        .reshape(tok_rows, -1)
    )


def dense_ranks(mask):
    width = mask.shape[-1]
    before = (
        jnp.arange(width, dtype=jnp.int32)[:, None] < jnp.arange(width, dtype=jnp.int32)[None, :]
    )
    return jnp.dot(
        mask.astype(jnp.bfloat16), before.astype(jnp.bfloat16), preferred_element_type=jnp.float32
    ).astype(jnp.int32)


def grouped(
    tokens,
    span_order,
    expert_ids,
    norm_gain,
    w_query,
    key_projection_weight,
    value_projection_weight,
    query_gain,
    key_gain,
    w_out,
    post_gain,
    w_router,
    w_gate,
    w_up,
    w_down,
    cotangent,
):
    tok_rows = tokens.shape[1]
    model_width = tokens.shape[2]
    head_size = query_gain.shape[0]
    top_count = expert_ids.shape[2]
    query_heads = w_query.shape[1] // head_size
    kv_heads = key_projection_weight.shape[1] // head_size
    group = query_heads // kv_heads
    context_size = lax.axis_size("context")
    expert_size = lax.axis_size("expert")
    both = ("context", "expert")
    device_count = context_size * expert_size
    me = lax.axis_index("context") * expert_size + lax.axis_index("expert")
    capacity = 2 * tok_rows * top_count // device_count
    seq_len = tok_rows * context_size
    span_rows = tok_rows // 2
    span_count = 2 * context_size
    order_row = span_order[0]
    score_scale = head_size ** (-0.5)
    shard_rows = w_query.shape[0]
    query_width = group * head_size
    part_width = query_width + 2 * head_size
    bf16 = jnp.bfloat16
    f32 = jnp.float32

    storage = jnp.arange(seq_len, dtype=jnp.int32)
    select = (storage // span_rows)[:, None] == jnp.arange(span_count, dtype=jnp.int32)[None, :]
    places = (
        jnp.sum(jnp.where(select, order_row[None, :], 0), axis=1) * span_rows + storage % span_rows
    )

    seq_tokens = lax.all_gather(tokens[0], "context", axis=0, tiled=True)
    packed = jnp.concatenate(
        [
            w_query.reshape(shard_rows, context_size, query_width),
            key_projection_weight.reshape(shard_rows, context_size, head_size),
            value_projection_weight.reshape(shard_rows, context_size, head_size),
        ],
        axis=2,
    ).transpose(1, 0, 2)
    columns = lax.all_to_all(packed, "context", split_axis=0, concat_axis=0, tiled=True)
    w_qkv = (
        lax.all_gather(columns, "expert", axis=0, tiled=False)
        .transpose(1, 0, 2, 3)
        .reshape(model_width, part_width)
    )
    out_rows = lax.all_gather(w_out, "expert", axis=0, tiled=True)
    router_full = lax.all_gather(w_router, both, axis=0, tiled=True)
    all_ids = lax.all_gather(expert_ids[0], both, axis=0, tiled=False)

    mine = jnp.any(all_ids == me, axis=-1)
    slot_of = dense_ranks(mine)
    picks = (
        (slot_of[:, None, :] == jnp.arange(capacity, dtype=jnp.int32)[None, :, None])
        & mine[:, None, :]
    ).astype(bf16)

    inputs = seq_tokens.astype(f32)
    normed_in, input_inverse = norm_forward(inputs, norm_gain)
    activation = normed_in.astype(bf16)
    projected = jnp.dot(activation, w_qkv, preferred_element_type=f32)
    query_raw = projected[:, :query_width].reshape(seq_len, group, head_size).transpose(1, 0, 2)
    key_raw = projected[:, query_width : query_width + head_size]
    values = projected[:, query_width + head_size :].astype(bf16)
    cosine_table, sine_table = rotary_tables(places, head_size)
    cosine_table, sine_table = (cosine_table[:, 0], sine_table[:, 0])
    query_normed, query_inverse = norm_forward(query_raw, query_gain)
    key_normed, key_inverse = norm_forward(key_raw, key_gain)
    queries = rotate(query_normed, cosine_table, sine_table, 1.0).astype(bf16)
    keys = rotate(key_normed, cosine_table, sine_table, 1.0).astype(bf16)
    visible = (places[:, None] >= places[None, :])[None]
    scores = jnp.einsum("htd,kd->htk", queries, keys, preferred_element_type=f32) * score_scale
    scores = jnp.where(visible, scores, very_negative)
    peak = jnp.max(scores, axis=-1, keepdims=True)
    weights = jnp.exp(scores - peak)
    probs = weights / jnp.sum(weights, axis=-1, keepdims=True)
    probs_low = probs.astype(bf16)
    attended = jnp.einsum("htk,kd->htd", probs_low, values, preferred_element_type=f32)
    attn_low = attended.astype(bf16).transpose(1, 0, 2).reshape(seq_len, query_width)
    out_part = jnp.dot(attn_low, out_rows, preferred_element_type=f32)
    own_inputs = tokens[0].astype(f32)
    residual = own_inputs + lax.psum_scatter(
        out_part.astype(bf16), "context", scatter_dimension=0, tiled=True
    ).astype(f32)
    normed_post, post_inverse = norm_forward(residual, post_gain)
    mixed = normed_post.astype(bf16)
    logits = jnp.dot(mixed, router_full, preferred_element_type=f32)
    chooser = (
        expert_ids[0][:, :, None] == jnp.arange(device_count, dtype=jnp.int32)[None, None, :]
    ).astype(f32)
    chosen = jnp.sum(chooser * logits[:, None, :], axis=-1)
    gates = jax.nn.softmax(chosen, axis=-1)
    gates_dense = jnp.sum(chooser * gates[..., None], axis=1)
    gates_mine = lax.all_to_all(gates_dense.T, both, split_axis=0, concat_axis=0, tiled=True)
    gate_rows = jnp.sum(picks.astype(f32) * gates_mine[:, None, :], axis=-1)[..., None]

    all_mixed = lax.all_gather(mixed, both, axis=0, tiled=False)
    all_grads = lax.all_gather(cotangent[0], both, axis=0, tiled=False)
    row_count = device_count * capacity

    def take(table):
        return jnp.einsum("bst,btd->bsd", picks, table, preferred_element_type=f32).astype(bf16)

    def give(rows):
        spread = jnp.einsum(
            "bst,bsd->btd", picks, rows, preferred_element_type=f32
        ).astype(bf16)
        return lax.psum_scatter(
            spread.reshape(device_count * tok_rows, model_width),
            both,
            scatter_dimension=0,
            tiled=True,
        ).astype(f32)

    expert_rows = take(all_mixed).reshape(row_count, model_width)
    grad_rows = take(all_grads)
    gate_pre = jnp.dot(expert_rows, w_gate[0], preferred_element_type=f32)
    up_pre = jnp.dot(expert_rows, w_up[0], preferred_element_type=f32)
    activated = jax.nn.silu(gate_pre)
    hidden = (activated * up_pre).astype(bf16)
    expert_out = jnp.dot(hidden, w_down[0], preferred_element_type=f32).astype(bf16)
    expert_out = expert_out.reshape(device_count, capacity, model_width)
    pair_out = (gate_rows * expert_out.astype(f32)).astype(bf16)
    grad_gate_rows = jnp.sum(grad_rows.astype(f32) * expert_out.astype(f32), axis=-1)
    grad_gates_back = jnp.sum(picks.astype(f32) * grad_gate_rows[..., None], axis=1)
    grad_gates_dense = lax.all_to_all(
        grad_gates_back, both, split_axis=0, concat_axis=0, tiled=True
    ).T
    grad_arrived = (gate_rows * grad_rows.astype(f32)).astype(bf16).reshape(row_count, model_width)
    final = residual + give(pair_out)

    upstream = cotangent[0].astype(f32)
    grad_w_down = jnp.einsum("rf,rd->fd", hidden, grad_arrived, preferred_element_type=f32)
    grad_hidden = jnp.einsum("rd,fd->rf", grad_arrived, w_down[0], preferred_element_type=f32)
    sigmoid = jax.nn.sigmoid(gate_pre)
    grad_gate = (grad_hidden * up_pre * sigmoid * (1.0 + gate_pre * (1.0 - sigmoid))).astype(bf16)
    grad_up = (grad_hidden * activated).astype(bf16)
    grad_w_gate = jnp.einsum("rd,rf->df", expert_rows, grad_gate, preferred_element_type=f32)
    grad_w_up = jnp.einsum("rd,rf->df", expert_rows, grad_up, preferred_element_type=f32)
    grad_pair = (
        jnp.einsum("rf,df->rd", grad_gate, w_gate[0], preferred_element_type=f32)
        + jnp.einsum("rf,df->rd", grad_up, w_up[0], preferred_element_type=f32)
    ).astype(bf16)
    grad_mixed = give(grad_pair.reshape(device_count, capacity, model_width))

    grad_gates = jnp.sum(chooser * grad_gates_dense[:, None, :], axis=-1)
    grad_chosen = gates * (grad_gates - jnp.sum(gates * grad_gates, axis=-1, keepdims=True))
    grad_logits = jnp.sum(chooser * grad_chosen[..., None], axis=1).astype(bf16)
    grad_mixed = grad_mixed + jnp.einsum(
        "te,de->td", grad_logits, router_full, preferred_element_type=f32
    )
    grad_w_router = jnp.einsum("td,te->de", mixed, grad_logits, preferred_element_type=f32)
    grad_resid_norm, post_terms = norm_backward(residual, post_inverse, post_gain, grad_mixed)
    grad_residual = upstream + grad_resid_norm
    resid_low = lax.all_gather(grad_residual.astype(bf16), "context", axis=0, tiled=True)
    grad_w_out = jnp.einsum("tc,td->cd", attn_low, resid_low, preferred_element_type=f32)
    grad_attn = (
        jnp.einsum("td,cd->tc", resid_low, out_rows, preferred_element_type=f32)
        .astype(bf16)
        .reshape(seq_len, group, head_size)
        .transpose(1, 0, 2)
    )
    grad_probs = jnp.einsum("htd,kd->htk", grad_attn, values, preferred_element_type=f32)
    delta = jnp.sum(probs * grad_probs, axis=-1, keepdims=True)
    grad_scores = (probs * (grad_probs - delta)).astype(bf16)
    grad_query = (
        jnp.einsum("htk,kd->htd", grad_scores, keys, preferred_element_type=f32) * score_scale
    ).astype(bf16)
    grad_key = (
        jnp.einsum("htk,htd->kd", grad_scores, queries, preferred_element_type=f32) * score_scale
    ).astype(bf16)
    grad_value = jnp.einsum(
        "htk,htd->kd", probs_low, grad_attn, preferred_element_type=f32
    ).astype(bf16)
    grad_query_raw, query_terms = norm_backward(
        query_raw,
        query_inverse,
        query_gain,
        rotate(grad_query.astype(f32), cosine_table, sine_table, -1.0),
    )
    grad_key_raw, key_terms = norm_backward(
        key_raw, key_inverse, key_gain, rotate(grad_key.astype(f32), cosine_table, sine_table, -1.0)
    )
    grad_parts = jnp.concatenate(
        [
            grad_query_raw.astype(bf16).transpose(1, 0, 2).reshape(seq_len, query_width),
            grad_key_raw.astype(bf16),
            grad_value,
        ],
        axis=1,
    )
    activation_part = jnp.einsum("tc,dc->td", grad_parts, w_qkv, preferred_element_type=f32)
    grad_activation = lax.psum_scatter(
        activation_part.astype(bf16), "context", scatter_dimension=0, tiled=True
    ).astype(f32)
    own_inverse = lax.rsqrt(
        jnp.mean(own_inputs * own_inputs, axis=-1, keepdims=True) + epsilon
    )
    grad_input_norm, input_terms = norm_backward(own_inputs, own_inverse, norm_gain, grad_activation)
    grad_tokens = grad_residual + grad_input_norm

    grad_w_qkv = jnp.einsum("td,tc->dc", activation, grad_parts, preferred_element_type=f32)
    column_sums = lax.psum_scatter(
        grad_w_qkv.astype(bf16)
        .reshape(context_size, expert_size, shard_rows, part_width)
        .transpose(1, 0, 2, 3)
        .reshape(model_width, part_width),
        "expert",
        scatter_dimension=0,
        tiled=True,
    ).reshape(context_size, shard_rows, part_width)
    shard_qkv = lax.all_to_all(column_sums, "context", split_axis=0, concat_axis=0, tiled=True)
    shard_qkv = shard_qkv.transpose(1, 0, 2).astype(f32)
    shard_query = shard_qkv[:, :, :query_width].reshape(shard_rows, -1)
    shard_key = shard_qkv[:, :, query_width : query_width + head_size].reshape(shard_rows, -1)
    shard_value = shard_qkv[:, :, query_width + head_size :].reshape(shard_rows, -1)
    shard_out = lax.psum_scatter(
        grad_w_out.astype(bf16), "expert", scatter_dimension=0, tiled=True
    ).astype(f32)
    shard_router = lax.psum_scatter(grad_w_router, both, scatter_dimension=0, tiled=True)
    gain_norm, gain_post, gain_query, gain_key = lax.psum(
        (
            jnp.sum(input_terms, axis=0),
            jnp.sum(post_terms, axis=0),
            jnp.sum(query_terms, axis=(0, 1)),
            jnp.sum(key_terms, axis=0),
        ),
        both,
    )
    return (
        final.astype(bf16)[None],
        grad_tokens[None],
        gain_norm,
        shard_query,
        shard_key,
        shard_value,
        gain_query,
        gain_key,
        shard_out,
        gain_post,
        shard_router,
        grad_w_gate[None],
        grad_w_up[None],
        grad_w_down[None],
    )


def shards(
    tokens,
    span_order,
    expert_ids,
    norm_gain,
    w_query,
    key_projection_weight,
    value_projection_weight,
    query_gain,
    key_gain,
    w_out,
    post_gain,
    w_router,
    w_gate,
    w_up,
    w_down,
    cotangent,
):
    tok_rows = tokens.shape[1]
    model_width = tokens.shape[2]
    head_size = query_gain.shape[0]
    top_count = expert_ids.shape[2]
    query_heads = w_query.shape[1] // head_size
    kv_heads = key_projection_weight.shape[1] // head_size
    query_group_count = query_heads // kv_heads
    context_size = lax.axis_size("context")
    device_count = lax.axis_size(("context", "expert"))
    capacity = max(2, 2 * tok_rows * top_count // device_count)
    seq_len = tok_rows * context_size
    span_rows = tok_rows // 2
    span_count = 2 * context_size
    order_row = span_order[0]
    score_scale = head_size ** (-0.5)
    bf16 = jnp.bfloat16
    f32 = jnp.float32

    def positions(first_row, row_count):
        storage = first_row + jnp.arange(row_count, dtype=jnp.int32)
        select = (storage // span_rows)[:, None] == jnp.arange(span_count, dtype=jnp.int32)[None, :]
        return (
            jnp.sum(jnp.where(select, order_row[None, :], 0), axis=1) * span_rows
            + storage % span_rows
        )

    query_places = positions(lax.axis_index("context") * tok_rows, tok_rows)
    row_places = jnp.tile(query_places, query_group_count)
    gathered = (
        lax.all_gather(w_query, ("context", "expert"), axis=0, tiled=True),
        lax.all_gather(key_projection_weight, ("context", "expert"), axis=0, tiled=True),
        lax.all_gather(value_projection_weight, ("context", "expert"), axis=0, tiled=True),
        lax.all_gather(w_out, ("context", "expert"), axis=0, tiled=True),
        lax.all_gather(w_router, ("context", "expert"), axis=0, tiled=True),
    )
    query_full, key_full, value_full, out_full, router_full = gathered
    inputs = tokens[0].astype(f32)
    normed_in, input_inverse = norm_forward(inputs, norm_gain)
    activation_output = normed_in.astype(bf16)
    query_raw = jnp.dot(activation_output, query_full, preferred_element_type=f32).reshape(
        tok_rows, query_heads, head_size
    )
    key_unrotated = jnp.dot(activation_output, key_full, preferred_element_type=f32).reshape(
        tok_rows, kv_heads, head_size
    )
    value_flat = jnp.dot(activation_output, value_full, preferred_element_type=f32).astype(bf16)
    cosine_table, sine_table = rotary_tables(query_places, head_size)
    query_normed, query_inverse = norm_forward(query_raw, query_gain)
    key_normed, key_inverse = norm_forward(key_unrotated, key_gain)
    query_prepared = rotate(query_normed, cosine_table, sine_table, 1.0).astype(bf16)
    key_flat = (
        rotate(key_normed, cosine_table, sine_table, 1.0)
        .astype(bf16)
        .reshape(tok_rows, kv_heads * head_size)
    )
    query_arr = head_rows(query_prepared, kv_heads, query_group_count)
    row_count_all = query_group_count * tok_rows
    whole_keys, whole_values = (
        lax.all_gather(key_flat, "context", axis=0, tiled=True),
        lax.all_gather(value_flat, "context", axis=0, tiled=True),
    )
    key_block = min(512, seq_len)
    block_count = seq_len // key_block
    key_blocks = whole_keys.reshape(block_count, key_block, kv_heads, head_size)
    value_blocks = whole_values.reshape(block_count, key_block, kv_heads, head_size)
    block_firsts = key_block * jnp.arange(block_count, dtype=jnp.int32)

    def block_scores(keys_now, start_now):
        scores = (
            jnp.einsum("hrd,khd->hrk", query_arr, keys_now, preferred_element_type=f32)
            * score_scale
        )
        visible = (row_places[:, None] >= positions(start_now, key_block)[None, :])[None]
        return (scores, visible)

    def stat_block(state, packed):
        keys_now, start_now = packed
        running_max, running_total = state
        scores, visible = block_scores(keys_now, start_now)
        scores = jnp.where(visible, scores, very_negative)
        new_max = jnp.maximum(running_max, jnp.max(scores, axis=-1))
        weights = jnp.where(visible, jnp.exp(scores - new_max[..., None]), 0.0)
        running_total = running_total * jnp.exp(running_max - new_max) + jnp.sum(weights, axis=-1)
        return ((new_max, running_total), None)

    (att_max, att_total), unused = lax.scan(
        stat_block,
        (
            jnp.full((kv_heads, row_count_all), very_negative, f32),
            jnp.zeros((kv_heads, row_count_all), f32),
        ),
        (key_blocks, block_firsts),
    )
    log_total = att_max + jnp.log(att_total)

    def block_probs(keys_now, start_now):
        scores, visible = block_scores(keys_now, start_now)
        return jnp.where(visible, jnp.exp(scores - log_total[..., None]), 0.0)

    def attend_block(accum, packed):
        keys_now, values_now, start_now = packed
        probs_now = block_probs(keys_now, start_now)
        accum = accum + jnp.einsum(
            "hrk,khd->hrd", probs_now.astype(bf16), values_now, preferred_element_type=f32
        )
        return (accum, None)

    attended_output, unused = lax.scan(
        attend_block,
        jnp.zeros((kv_heads, row_count_all, head_size), f32),
        (key_blocks, value_blocks, block_firsts),
    )
    attn_low = token_rows_of(attended_output, kv_heads, query_group_count, tok_rows).astype(bf16)
    residual = inputs + jnp.dot(attn_low, out_full, preferred_element_type=f32)
    normed_post, post_inverse = norm_forward(residual, post_gain)
    mixed = normed_post.astype(bf16)
    logits = jnp.dot(mixed, router_full, preferred_element_type=f32)
    local_ids = expert_ids[0]
    chooser = (
        local_ids[:, :, None] == jnp.arange(device_count, dtype=jnp.int32)[None, None, :]
    ).astype(f32)
    chosen = jnp.sum(chooser * logits[:, None, :], axis=-1)
    gates = jax.nn.softmax(chosen, axis=-1)
    flat_ids = local_ids.reshape(-1)
    pair_hot = (flat_ids[:, None] == jnp.arange(device_count, dtype=jnp.int32)[None, :]).astype(
        jnp.int32
    )
    ranks = jnp.sum(jnp.cumsum(pair_hot, axis=0) * pair_hot, axis=1) - 1
    slots = flat_ids * capacity + ranks
    pair_rows = jnp.repeat(mixed, top_count, axis=0)
    outgoing = jnp.zeros((device_count * capacity, model_width), bf16).at[slots].set(pair_rows)
    arrived = lax.all_to_all(
        outgoing.reshape(device_count, capacity, model_width),
        ("context", "expert"),
        split_axis=0,
        concat_axis=0,
        tiled=True,
    )
    expert_rows = arrived.reshape(device_count * capacity, model_width)
    gate_pre = jnp.dot(expert_rows, w_gate[0], preferred_element_type=f32)
    up_pre = jnp.dot(expert_rows, w_up[0], preferred_element_type=f32)
    activated = jax.nn.silu(gate_pre)
    hidden = (activated * up_pre).astype(bf16)
    expert_out = jnp.dot(hidden, w_down[0], preferred_element_type=f32).astype(bf16)
    returned = lax.all_to_all(
        expert_out.reshape(device_count, capacity, model_width),
        ("context", "expert"),
        split_axis=0,
        concat_axis=0,
        tiled=True,
    )
    pair_out = (
        returned.reshape(device_count * capacity, model_width)[slots]
        .reshape(tok_rows, top_count, model_width)
        .astype(f32)
    )
    final = residual + jnp.sum(gates[..., None] * pair_out, axis=1)
    again = (
        lax.all_gather(w_query, ("context", "expert"), axis=0, tiled=True),
        lax.all_gather(key_projection_weight, ("context", "expert"), axis=0, tiled=True),
        lax.all_gather(value_projection_weight, ("context", "expert"), axis=0, tiled=True),
        lax.all_gather(w_out, ("context", "expert"), axis=0, tiled=True),
        lax.all_gather(w_router, ("context", "expert"), axis=0, tiled=True),
    )
    query_back, key_back, value_back, out_back, router_back = again
    upstream = cotangent[0].astype(f32)
    grad_gates = jnp.sum(upstream[:, None, :] * pair_out, axis=-1)
    pair_grads = (
        (upstream[:, None, :] * gates[..., None])
        .astype(bf16)
        .reshape(tok_rows * top_count, model_width)
    )
    grad_outgoing = (
        jnp.zeros((device_count * capacity, model_width), bf16).at[slots].set(pair_grads)
    )
    grad_arrived = lax.all_to_all(
        grad_outgoing.reshape(device_count, capacity, model_width),
        ("context", "expert"),
        split_axis=0,
        concat_axis=0,
        tiled=True,
    ).reshape(device_count * capacity, model_width)
    grad_w_down = jnp.einsum("rf,rd->fd", hidden, grad_arrived, preferred_element_type=f32)
    grad_hidden = jnp.einsum("rd,fd->rf", grad_arrived, w_down[0], preferred_element_type=f32)
    sigmoid = jax.nn.sigmoid(gate_pre)
    grad_gate = (grad_hidden * up_pre * sigmoid * (1.0 + gate_pre * (1.0 - sigmoid))).astype(bf16)
    grad_up = (grad_hidden * activated).astype(bf16)
    grad_w_gate = jnp.einsum("rd,rf->df", expert_rows, grad_gate, preferred_element_type=f32)
    grad_w_up = jnp.einsum("rd,rf->df", expert_rows, grad_up, preferred_element_type=f32)
    grad_rows = (
        jnp.einsum("rf,df->rd", grad_gate, w_gate[0], preferred_element_type=f32)
        + jnp.einsum("rf,df->rd", grad_up, w_up[0], preferred_element_type=f32)
    ).astype(bf16)
    grad_back = lax.all_to_all(
        grad_rows.reshape(device_count, capacity, model_width),
        ("context", "expert"),
        split_axis=0,
        concat_axis=0,
        tiled=True,
    )
    grad_mixed = jnp.sum(
        grad_back.reshape(device_count * capacity, model_width)[slots]
        .reshape(tok_rows, top_count, model_width)
        .astype(f32),
        axis=1,
    )
    grad_chosen = gates * (grad_gates - jnp.sum(gates * grad_gates, axis=-1, keepdims=True))
    grad_logits = jnp.sum(chooser * grad_chosen[..., None], axis=1).astype(bf16)
    grad_mixed = grad_mixed + jnp.einsum(
        "te,de->td", grad_logits, router_back, preferred_element_type=f32
    )
    grad_w_router = jnp.einsum("td,te->de", mixed, grad_logits, preferred_element_type=f32)
    grad_resid_norm, post_terms = norm_backward(residual, post_inverse, post_gain, grad_mixed)
    grad_residual = upstream + grad_resid_norm
    resid_low = grad_residual.astype(bf16)
    grad_w_out = jnp.einsum("tc,td->cd", attn_low, resid_low, preferred_element_type=f32)
    grad_attn = jnp.einsum("td,cd->tc", resid_low, out_back, preferred_element_type=f32).astype(
        bf16
    )
    grad_arr = head_rows(
        grad_attn.reshape(tok_rows, query_heads, head_size), kv_heads, query_group_count
    )

    def delta_block(total, packed):
        keys_now, values_now, start_now = packed
        probs_now = block_probs(keys_now, start_now)
        grad_probs = jnp.einsum("hrd,khd->hrk", grad_arr, values_now, preferred_element_type=f32)
        return (total + jnp.sum(probs_now * grad_probs, axis=-1), None)

    delta, unused = lax.scan(
        delta_block,
        jnp.zeros((kv_heads, row_count_all), f32),
        (key_blocks, value_blocks, block_firsts),
    )

    def back_block(grad_query, packed):
        keys_now, values_now, start_now = packed
        probs_now = block_probs(keys_now, start_now)
        grad_probs = jnp.einsum("hrd,khd->hrk", grad_arr, values_now, preferred_element_type=f32)
        grad_scores = (probs_now * (grad_probs - delta[..., None])).astype(bf16)
        grad_query = (
            grad_query
            + jnp.einsum("hrk,khd->hrd", grad_scores, keys_now, preferred_element_type=f32)
            * score_scale
        )
        grad_keys = (
            jnp.einsum("hrk,hrd->khd", grad_scores, query_arr, preferred_element_type=f32)
            * score_scale
        )
        grad_values = jnp.einsum(
            "hrk,hrd->khd", probs_now.astype(bf16), grad_arr, preferred_element_type=f32
        )
        return (
            grad_query,
            jnp.concatenate(
                [grad_keys.reshape(key_block, -1), grad_values.reshape(key_block, -1)], axis=-1
            ),
        )

    grad_query, key_terms = lax.scan(
        back_block,
        jnp.zeros((kv_heads, row_count_all, head_size), f32),
        (key_blocks, value_blocks, block_firsts),
    )
    own_terms = lax.psum_scatter(
        key_terms.reshape(seq_len, 2 * kv_heads * head_size),
        "context",
        scatter_dimension=0,
        tiled=True,
    )
    kv_width = kv_heads * head_size
    grad_key_rot = (
        own_terms[:, :kv_width].astype(bf16).astype(f32).reshape(tok_rows, kv_heads, head_size)
    )
    grad_value_low = own_terms[:, kv_width:].astype(bf16)
    grad_query_rot = token_rows_of(
        grad_query.astype(bf16).astype(f32), kv_heads, query_group_count, tok_rows
    ).reshape(tok_rows, query_heads, head_size)
    grad_query_raw, query_terms = norm_backward(
        query_raw, query_inverse, query_gain, rotate(grad_query_rot, cosine_table, sine_table, -1.0)
    )
    grad_key_raw, key_terms_gain = norm_backward(
        key_unrotated, key_inverse, key_gain, rotate(grad_key_rot, cosine_table, sine_table, -1.0)
    )
    grad_query_low = grad_query_raw.reshape(tok_rows, query_heads * head_size).astype(bf16)
    grad_key_low = grad_key_raw.reshape(tok_rows, kv_width).astype(bf16)
    grad_activation = (
        jnp.einsum("tc,dc->td", grad_query_low, query_back, preferred_element_type=f32)
        + jnp.einsum("tc,dc->td", grad_key_low, key_back, preferred_element_type=f32)
        + jnp.einsum("tc,dc->td", grad_value_low, value_back, preferred_element_type=f32)
    )
    grad_w_query = jnp.einsum(
        "td,tc->dc", activation_output, grad_query_low, preferred_element_type=f32
    )
    grad_w_key = jnp.einsum(
        "td,tc->dc", activation_output, grad_key_low, preferred_element_type=f32
    )
    grad_w_value = jnp.einsum(
        "td,tc->dc", activation_output, grad_value_low, preferred_element_type=f32
    )
    grad_input_norm, input_terms = norm_backward(inputs, input_inverse, norm_gain, grad_activation)
    grad_tokens = grad_residual + grad_input_norm
    shard_query, shard_key, shard_value, shard_out, shard_router = (
        lax.psum_scatter(grad_w_query, ("context", "expert"), scatter_dimension=0, tiled=True),
        lax.psum_scatter(grad_w_key, ("context", "expert"), scatter_dimension=0, tiled=True),
        lax.psum_scatter(grad_w_value, ("context", "expert"), scatter_dimension=0, tiled=True),
        lax.psum_scatter(grad_w_out, ("context", "expert"), scatter_dimension=0, tiled=True),
        lax.psum_scatter(grad_w_router, ("context", "expert"), scatter_dimension=0, tiled=True),
    )
    gain_norm, gain_post, gain_query, gain_key = lax.psum(
        (
            jnp.sum(input_terms, axis=0),
            jnp.sum(post_terms, axis=0),
            jnp.sum(query_terms, axis=(0, 1)),
            jnp.sum(key_terms_gain, axis=(0, 1)),
        ),
        ("context", "expert"),
    )
    return (
        final.astype(bf16)[None],
        grad_tokens[None],
        gain_norm,
        shard_query,
        shard_key,
        shard_value,
        gain_query,
        gain_key,
        shard_out,
        gain_post,
        shard_router,
        grad_w_gate[None],
        grad_w_up[None],
        grad_w_down[None],
    )


def solution(mesh):
    placed = (
        P("expert", "context", None),
        P("expert", None),
        P("expert", "context", None),
        P(),
        P(("context", "expert"), None),
        P(("context", "expert"), None),
        P(("context", "expert"), None),
        P(),
        P(),
        P(("context", "expert"), None),
        P(),
        P(("context", "expert"), None),
        P(("context", "expert"), None, None),
        P(("context", "expert"), None, None),
        P(("context", "expert"), None, None),
        P("expert", "context", None),
    )
    placed_out = (
        P("expert", "context", None),
        P("expert", "context", None),
        P(),
        P(("context", "expert"), None),
        P(("context", "expert"), None),
        P(("context", "expert"), None),
        P(),
        P(),
        P(("context", "expert"), None),
        P(),
        P(("context", "expert"), None),
        P(("context", "expert"), None, None),
        P(("context", "expert"), None, None),
        P(("context", "expert"), None, None),
    )

    def step(*arrays):
        key_width, head_size = (arrays[5].shape[1], arrays[7].shape[0])
        own_head = key_width == mesh.shape["context"] * head_size
        return jax.shard_map(
            grouped if own_head else shards,
            mesh=mesh,
            in_specs=placed,
            out_specs=placed_out,
            check_vma=False,
        )(*arrays)

    return step
```

```python
import jax
import jax.numpy as jnp
from jax import lax
from jax.experimental import pallas as pl
from jax.experimental.pallas import tpu as pltpu
from jax.sharding import Mesh
from jax.sharding import PartitionSpec as P

epsilon = 1e-06
rotary_base = 1000000.0
very_negative = -1e30


def norm_forward(values, scale_gain):
    inverse = lax.rsqrt(jnp.mean(values * values, axis=-1, keepdims=True) + epsilon)
    return (values * inverse * scale_gain, inverse)


def norm_backward(values, inverse, scale_gain, upstream):
    normed = values * inverse
    weighted = upstream * scale_gain
    inner = jnp.mean(weighted * normed, axis=-1, keepdims=True)
    return (inverse * (weighted - normed * inner), upstream * normed)


def rotary_tables(token_positions, head_width):
    half_width = head_width // 2
    frequency = rotary_base ** (-jnp.arange(half_width, dtype=jnp.float32) * 2.0 / head_width)
    angles = token_positions.astype(jnp.float32)[:, None] * frequency[None, :]
    return (jnp.cos(angles)[:, None, :], jnp.sin(angles)[:, None, :])


def rotate(values, cosine_table, sine_table, direction):
    half_width = values.shape[-1] // 2
    first_half = values[..., :half_width]
    second_half = values[..., half_width:]
    return jnp.concatenate(
        [
            first_half * cosine_table - direction * second_half * sine_table,
            second_half * cosine_table + direction * first_half * sine_table,
        ],
        axis=-1,
    )


def head_rows(array_in, kv_heads, query_group_count):
    row_total = array_in.shape[0]
    return (
        array_in.reshape(row_total, kv_heads, query_group_count, -1)
        .transpose(1, 2, 0, 3)
        .reshape(kv_heads, query_group_count * row_total, -1)
    )


def token_rows_of(array_in, kv_heads, query_group_count, tok_rows):
    return (
        array_in.reshape(kv_heads, query_group_count, tok_rows, -1)
        .transpose(2, 0, 1, 3)
        .reshape(tok_rows, -1)
    )


def dense_ranks(mask):
    width = mask.shape[-1]
    before = (
        jnp.arange(width, dtype=jnp.int32)[:, None] < jnp.arange(width, dtype=jnp.int32)[None, :]
    )
    return jnp.dot(
        mask.astype(jnp.bfloat16), before.astype(jnp.bfloat16), preferred_element_type=jnp.float32
    ).astype(jnp.int32)


context_axes = ("y", "x")
expert_axes = ("z", "core")
plane_axes = ("y", "x", "core")
both = context_axes + expert_axes
bf16 = jnp.bfloat16
f32 = jnp.float32


class Wires:
    def __init__(self, expert_size):
        self.layers = expert_size // 2
        self.context = lax.axis_index(context_axes)
        self.expert = lax.axis_index(expert_axes)
        self.core = self.expert % 2
        self.layer = self.expert // 2

    def pairs(self, move):
        found = []
        for y in range(2):
            for x in range(2):
                for z in range(self.layers):
                    for core in range(2):
                        there = move(y, x, z, core)
                        found.append((self.number(y, x, z, core), self.number(*there)))
        return found

    def number(self, y, x, z, core):
        return ((y * 2 + x) * self.layers + z) * 2 + core

    def send(self, value, move):
        return lax.ppermute(value, both, self.pairs(move))

    def swap(self, value):
        return self.send(value, lambda y, x, z, core: (y, x, z, 1 - core))

    def first(self, value):
        return self.send(
            value, lambda y, x, z, core: (y, 1 - x, z, core) if core else (1 - y, x, z, core)
        )

    def second(self, value):
        return self.send(
            value, lambda y, x, z, core: (1 - y, x, z, core) if core else (y, 1 - x, z, core)
        )

    def along(self, value, flip_y, flip_x):
        return self.send(value, lambda y, x, z, core: (y ^ flip_y, x ^ flip_x, z, core))

    def layer_flip(self, value, bit):
        return self.send(value, lambda y, x, z, core: (y, x, z ^ bit, core))

    def from_layer(self, value, step):
        return self.send(value, lambda y, x, z, core: (y, x, (z - step) % self.layers, core))

    def to_layer(self, value, step):
        return self.send(value, lambda y, x, z, core: (y, x, (z + step) % self.layers, core))

    def contexts(self, core):
        index = jnp.arange(4, dtype=jnp.int32)
        one, two = (index // 2, index % 2)
        swapped = two * 2 + one
        return self.context ^ jnp.where(core == 0, index, swapped)

    def blocks(self):
        found = []
        for step in range(self.layers):
            for flip in range(2):
                core = self.core ^ flip
                layer = (self.layer + step) % self.layers
                found.append(self.contexts(core) * (2 * self.layers) + layer * 2 + core)
        return jnp.concatenate(found)

    def gather_plane(self, value):
        crossed = self.second(value)
        return jnp.concatenate(
            [value, crossed, self.first(value), self.first(crossed)], axis=0
        )

    def scatter_plane(self, value):
        half = value.shape[0] // 2
        quarter = half // 2
        there = self.first(value[half:])
        mine = add_low(value[quarter:half], there[quarter:])
        kept = add_low(value[:quarter], there[:quarter])
        return kept.astype(f32) + self.second(mine).astype(f32)

    def turns(self):
        others = sorted(range(1, self.layers), key=lambda step: -min(step, self.layers - step))
        return [0] + others

    def layers_of(self, value, *after):
        found = [value]
        for turn, step in enumerate(self.turns()[1:]):
            start = tie(value, *found[-1:], *(after if turn > 0 else ()))
            found.append(self.from_layer(start, step))
        return found

    def total(self, value):
        value = value + self.swap(value)
        value = value + self.along(value, 1, 0)
        value = value + self.along(value, 0, 1)
        bit = 1
        while bit < self.layers:
            value = value + self.layer_flip(value, bit)
            bit *= 2
        return value


def add_low(one, two):
    return (one.astype(f32) + two.astype(f32)).astype(bf16)


def tie(value, *after):
    return lax.optimization_barrier((value, *after))[0]


def sum_of_products(lefts, rights, tile):
    rows, height = lefts[0].shape
    width = rights[0].shape[1]
    parts = len(lefts)

    def body(*refs):
        total = None
        for left, right in zip(refs[:parts], refs[parts : 2 * parts]):
            term = lax.dot_general(
                left[...], right[...], (((0,), (0,)), ((), ())), preferred_element_type=f32
            )
            total = term if total is None else total + term
        refs[2 * parts][...] = total

    return pl.pallas_call(
        body,
        grid=(height // tile,),
        in_specs=[pl.BlockSpec((rows, tile), lambda i: (0, i))] * parts
        + [pl.BlockSpec((rows, width), lambda i: (0, 0))] * parts,
        out_specs=pl.BlockSpec((tile, width), lambda i: (i, 0)),
        out_shape=jax.ShapeDtypeStruct((height, width), f32),
        cost_estimate=pl.CostEstimate(
            flops=2 * parts * rows * height * width,
            bytes_accessed=2 * parts * rows * (height + width) + 4 * height * width,
            transcendentals=0,
        ),
        name="sum_of_products",
    )(*lefts, *rights)


def estimate(flops, moved):
    return pl.CostEstimate(flops=flops, bytes_accessed=moved, transcendentals=0)


def fixed(shape):
    return pl.BlockSpec(shape, lambda *i: (0,) * len(shape))


def pull_step(picks, pieces, w_down):
    blocks, capacity, halves = picks.shape
    width, tile = (w_down.shape[2], 256)
    rows, hidden_width = (blocks * capacity, w_down.shape[1])

    def body(picks_ref, *refs):
        down_ref, rows_ref, pulled_ref = refs[blocks:]

        @pl.when(pl.program_id(0) == 0)
        def _():
            for block in range(blocks):
                rows_ref[pl.ds(block * capacity, capacity), :] = jnp.dot(
                    picks_ref[block], refs[block][...], preferred_element_type=f32
                ).astype(bf16)

        pulled_ref[...] = lax.dot_general(
            rows_ref[...], down_ref[0], (((1,), (1,)), ((), ())), preferred_element_type=f32
        )

    return pl.pallas_call(
        body,
        grid=(hidden_width // tile,),
        in_specs=[fixed(picks.shape)]
        + [fixed((halves, width))] * blocks
        + [pl.BlockSpec((1, tile, width), lambda i: (0, i, 0))],
        out_specs=[fixed((rows, width)), pl.BlockSpec((rows, tile), lambda i: (0, i))],
        out_shape=[
            jax.ShapeDtypeStruct((rows, width), bf16),
            jax.ShapeDtypeStruct((rows, hidden_width), f32),
        ],
        cost_estimate=estimate(2 * rows * width * (hidden_width + 2 * halves), 4 * rows * width),
        name="pull_step",
    )(picks, *pieces, w_down)


def expert_step(picks, pieces, gate, pulled, w_gate, w_up, w_down, joined):
    blocks, capacity, halves = picks.shape
    width, tile, slab = (w_gate.shape[1], 256, 32)
    rows, hidden_width = (blocks * capacity, w_gate.shape[2])
    count = hidden_width // tile

    def body(picks_ref, *refs):
        gate_ref, pulled_ref, w_gate_ref, w_up_ref, w_down_ref = refs[blocks : blocks + 5]
        rows_ref, weighted_ref, grad_gate_ref, grad_up_ref, dots_ref = refs[
            blocks + 5 : blocks + 10
        ]
        back_refs = refs[blocks + 10 : -4]
        pre_ref, up_ref, total_ref, out_ref = refs[-4:]
        turn = pl.program_id(0)

        @pl.when(turn == 0)
        def _():
            dots_ref[...] = jnp.zeros_like(dots_ref)
            for block in range(blocks):
                rows_ref[pl.ds(block * capacity, capacity), :] = jnp.dot(
                    picks_ref[block], refs[block][...], preferred_element_type=f32
                ).astype(bf16)

        pre_ref[...] = jnp.dot(rows_ref[...], w_gate_ref[0], preferred_element_type=f32)
        up_ref[...] = jnp.dot(rows_ref[...], w_up_ref[0], preferred_element_type=f32)

        @pl.loop(0, rows // slab)
        def _(place):
            at = pl.ds(pl.multiple_of(place * slab, slab), slab)
            pre, up, gates, pull = (pre_ref[at, :], up_ref[at, :], gate_ref[at, :], pulled_ref[at, :])
            sigmoid = jax.nn.sigmoid(pre)
            activated = pre * sigmoid
            hidden = activated * up
            dots_ref[at, :] += jnp.sum(hidden * pull, axis=1, keepdims=True)
            weighted_ref[at, :] = (gates * hidden).astype(bf16)
            grad_hidden = gates * pull
            grad_gate_ref[at, :] = (
                grad_hidden * up * sigmoid * (1.0 + pre * (1.0 - sigmoid))
            ).astype(bf16)
            grad_up_ref[at, :] = (grad_hidden * activated).astype(bf16)

        across = (((1,), (1,)), ((), ()))
        term = lax.dot_general(
            grad_gate_ref[...], w_gate_ref[0], across, preferred_element_type=f32
        ) + lax.dot_general(grad_up_ref[...], w_up_ref[0], across, preferred_element_type=f32)

        pair = jnp.dot(weighted_ref[...], w_down_ref[0], preferred_element_type=f32)

        @pl.when(turn == 0)
        def _():
            total_ref[...] = term
            out_ref[...] = pair

        @pl.when(turn > 0)
        def _():
            total_ref[...] += term
            out_ref[...] += pair

        @pl.when(turn == count - 1)
        def _():
            for block in range(blocks):
                for side, table in enumerate((total_ref, out_ref)):
                    found = lax.dot_general(
                        picks_ref[block],
                        table[pl.ds(block * capacity, capacity), :].astype(bf16),
                        (((0,), (0,)), ((), ())),
                        preferred_element_type=f32,
                    ).astype(bf16)
                    if joined:
                        back_refs[block][pl.ds(side * halves, halves), :] = found
                    else:
                        back_refs[side * blocks + block][...] = found

    tiled = pl.BlockSpec((rows, tile), lambda i: (0, i))
    weights = pl.BlockSpec((1, width, tile), lambda i: (0, 0, i))
    back = [((2 if joined else 1) * halves, width)] * (blocks if joined else 2 * blocks)
    narrow = jax.ShapeDtypeStruct((rows, hidden_width), bf16)
    found = pl.pallas_call(
        body,
        grid=(count,),
        in_specs=[fixed(picks.shape)]
        + [fixed((halves, width))] * blocks
        + [fixed((rows, 1)), tiled, weights, weights]
        + [pl.BlockSpec((1, tile, width), lambda i: (0, i, 0))],
        out_specs=[fixed((rows, width)), tiled, tiled, tiled, fixed((rows, 1))]
        + [fixed(shape) for shape in back],
        out_shape=[
            jax.ShapeDtypeStruct((rows, width), bf16),
            narrow,
            narrow,
            narrow,
            jax.ShapeDtypeStruct((rows, 1), f32),
        ]
        + [jax.ShapeDtypeStruct(shape, bf16) for shape in back],
        scratch_shapes=[
            pltpu.VMEM((rows, tile), f32),
            pltpu.VMEM((rows, tile), f32),
            pltpu.VMEM((rows, width), f32),
            pltpu.VMEM((rows, width), f32),
        ],
        cost_estimate=estimate(10 * rows * width * hidden_width, 24 * rows * width),
        name="expert_step",
    )(picks, *pieces, gate, pulled, w_gate, w_up, w_down)
    return (*found[:5], found[5:])


def grouped(
    tokens,
    span_order,
    expert_ids,
    norm_gain,
    w_query,
    key_projection_weight,
    value_projection_weight,
    query_gain,
    key_gain,
    w_out,
    post_gain,
    w_router,
    w_gate,
    w_up,
    w_down,
    cotangent,
):
    tok_rows = tokens.shape[1]
    model_width = tokens.shape[2]
    head_size = query_gain.shape[0]
    top_count = expert_ids.shape[2]
    query_heads = w_query.shape[1] // head_size
    kv_heads = key_projection_weight.shape[1] // head_size
    group = query_heads // kv_heads
    context_size = lax.axis_size(context_axes)
    expert_size = lax.axis_size(expert_axes)
    device_count = context_size * expert_size
    wires = Wires(expert_size)
    layers = wires.layers
    chain = wires.turns()
    capacity = 2 * tok_rows * top_count // device_count
    seq_len = tok_rows * context_size
    span_rows = tok_rows // 2
    span_count = 2 * context_size
    order_row = span_order[0]
    score_scale = head_size ** (-0.5)
    shard_rows = w_query.shape[0]
    query_width = group * head_size
    part_width = query_width + 2 * head_size
    hidden_width = w_gate.shape[2]

    seq_tokens = wires.gather_plane(tokens[0])
    storage = (
        wires.contexts(wires.core)[:, None] * tok_rows
        + jnp.arange(tok_rows, dtype=jnp.int32)[None, :]
    ).reshape(-1)
    select = (storage // span_rows)[:, None] == jnp.arange(span_count, dtype=jnp.int32)[None, :]
    places = (
        jnp.sum(jnp.where(select, order_row[None, :], 0), axis=1) * span_rows + storage % span_rows
    )

    packed = jnp.concatenate(
        [
            w_query.reshape(shard_rows, context_size, query_width),
            key_projection_weight.reshape(shard_rows, context_size, head_size),
            value_projection_weight.reshape(shard_rows, context_size, head_size),
        ],
        axis=2,
    ).transpose(1, 0, 2)
    flips = wires.context ^ jnp.arange(context_size, dtype=jnp.int32)

    def exchange(parts):
        facing = jnp.take(parts, flips, axis=0)
        got = [facing[0]] + [
            wires.along(facing[flip], flip // 2, flip % 2) for flip in range(1, context_size)
        ]
        return jnp.take(jnp.stack(got), flips, axis=0)

    columns = exchange(packed)
    grad_columns = [
        wires.from_layer(cotangent[0], step) if step else cotangent[0] for step in range(layers)
    ]
    columns = tie(columns, *grad_columns[1:2])
    every_column = lax.all_gather(columns, expert_axes, axis=0, tiled=False)
    router_full = lax.all_to_all(
        jnp.broadcast_to(w_router.reshape(1, -1), (device_count, w_router.size)),
        both,
        split_axis=0,
        concat_axis=0,
        tiled=True,
    ).reshape(model_width, device_count)

    order = wires.blocks()
    chooser = (
        expert_ids[0][:, :, None] == jnp.arange(device_count, dtype=jnp.int32)[None, None, :]
    ).astype(f32)
    chosen_by = lax.all_to_all(
        jnp.sum(chooser, axis=1).T, both, split_axis=0, concat_axis=0, tiled=True
    )
    mine = jnp.take(chosen_by, order, axis=0) > 0.5
    slot_of = dense_ranks(mine)
    picks_true = (
        slot_of[:, None, :] == jnp.arange(capacity, dtype=jnp.int32)[None, :, None]
    ) & mine[:, None, :]
    picks = picks_true.astype(bf16)
    picks_by = picks.reshape(layers, 8, capacity, tok_rows)
    count = layers

    class Plane:
        def __init__(self, column):
            self.near = [column]
            self.far = []

        def cross(self, *after):
            self.near.append(wires.second(tie(self.near[0], *after)))

        def finish(self, *after):
            self.near += [wires.first(tie(part, *after)) for part in self.near[:2]]

        def swap(self):
            self.far = [wires.swap(part) for part in self.near]

    def pull(turn, *after):
        plane = grad_planes[turn]
        found = pull_step(
            tie(picks_by[chain[turn]], *after), plane.near + plane.far, w_down
        )
        grad_rows[turn], pulled[turn] = found

    picks_by = tie(picks_by, router_full)
    grad_planes = [Plane(grad_columns[step]) for step in chain]
    pulled, grad_rows = ([None] * count, [None] * count)
    early, late = (
        [turn for turn in range(count) if chain[turn] < 2],
        [turn for turn in range(count) if chain[turn] > 1],
    )
    for turn in early:
        grad_planes[turn].cross(*([grad_planes[0].near[0]] if turn else []))
    for turn in early:
        grad_planes[turn].finish()
        grad_planes[turn].swap()
        pull(turn)
    out_rows = lax.all_gather(tie(w_out, pulled[0]), expert_axes, axis=0, tiled=True)

    inputs = seq_tokens.astype(f32)
    normed_in, input_inverse = norm_forward(inputs, norm_gain)
    activation = normed_in.astype(bf16)
    every_column = tie(
        every_column, activation, *[pulled[turn] for turn in early], *grad_columns[2:]
    )
    w_qkv = every_column.transpose(1, 0, 2, 3).reshape(model_width, part_width)
    projected = jnp.dot(activation, w_qkv, preferred_element_type=f32)
    query_raw = projected[:, :query_width].reshape(seq_len, group, head_size).transpose(1, 0, 2)
    key_raw = projected[:, query_width : query_width + head_size]
    values = projected[:, query_width + head_size :].astype(bf16)
    cosine_table, sine_table = rotary_tables(places, head_size)
    cosine_table, sine_table = (cosine_table[:, 0], sine_table[:, 0])
    query_normed, query_inverse = norm_forward(query_raw, query_gain)
    key_normed, key_inverse = norm_forward(key_raw, key_gain)
    queries = rotate(query_normed, cosine_table, sine_table, 1.0).astype(bf16)
    keys = rotate(key_normed, cosine_table, sine_table, 1.0).astype(bf16)
    visible = (places[:, None] >= places[None, :])[None]
    scores = jnp.einsum("htd,kd->htk", queries, keys, preferred_element_type=f32) * score_scale
    scores = jnp.where(visible, scores, very_negative)
    peak = jnp.max(scores, axis=-1, keepdims=True)
    weights = jnp.exp(scores - peak)
    probs = weights / jnp.sum(weights, axis=-1, keepdims=True)
    probs_low = probs.astype(bf16)
    attended = jnp.einsum("htk,kd->htd", probs_low, values, preferred_element_type=f32)
    for turn in late:
        grad_planes[turn].cross()
    attended = tie(attended, *[grad_planes[turn].near[1] for turn in late])
    for turn in late:
        grad_planes[turn].finish()
    attn_low = attended.astype(bf16).transpose(1, 0, 2).reshape(seq_len, query_width)
    attn_low = tie(attn_low, *[grad_planes[turn].near[3] for turn in late])
    for turn in late:
        grad_planes[turn].swap()
    out_part = jnp.dot(attn_low, out_rows, preferred_element_type=f32).astype(bf16)
    own_inputs = tokens[0].astype(f32)
    residual = own_inputs + wires.scatter_plane(out_part)
    residual = tie(residual, *[part for turn in late for part in grad_planes[turn].far])
    normed_post, post_inverse = norm_forward(residual, post_gain)
    mixed = normed_post.astype(bf16)
    logits = jnp.dot(mixed, router_full, preferred_element_type=f32)
    chosen = jnp.sum(chooser * logits[:, None, :], axis=-1)
    gates = jax.nn.softmax(chosen, axis=-1)
    gates_dense = jnp.sum(chooser * gates[..., None], axis=1)
    gates_mine = lax.all_to_all(gates_dense.T, both, split_axis=0, concat_axis=0, tiled=True)
    mixed_columns = wires.layers_of(mixed)
    planes = [Plane(column) for column in mixed_columns]
    planes[0].cross()
    planes[0].finish()
    planes[0].swap()
    gates_mine = tie(gates_mine, *planes[0].near)
    gates_mine = jnp.take(gates_mine, order, axis=0)
    gate_rows = jnp.sum(jnp.where(picks_true, gates_mine[:, None, :], 0.0), axis=-1)
    gate_by = gate_rows.reshape(layers, 8 * capacity, 1)

    class Back:
        def __init__(self, step, parts):
            self.step, self.near = (step, parts[:4])
            self.swapped = [wires.swap(part) for part in parts[4:]]

        def first(self, *after):
            leaving = [add_low(self.near[part], self.swapped[part]) for part in (2, 3)]
            self.halved = [wires.first(tie(part, *after)) for part in leaving]

        def second(self, *after):
            self.kept = [
                (
                    self.near[part].astype(f32)
                    + self.swapped[part].astype(f32)
                    + self.halved[part].astype(f32)
                ).astype(bf16)
                for part in (0, 1)
            ]
            self.crossed = wires.second(tie(self.kept[1], *after))

        def send(self, own):
            return own if self.step == 0 else wires.to_layer(own, self.step)

        def layer(self, *after):
            own = add_low(self.kept[0], self.crossed)
            self.sum = self.send(tie(own[:tok_rows], *after))
            self.rest = own[tok_rows:]

    expert_rows, weighted, grad_pre, grad_gate_rows, backs = ([], [], [], [], [])
    if count > 1:
        planes[1].cross()
    for turn in late:
        pull(turn, *planes[0].near[:2])
    for turn, step in enumerate(chain):
        last = turn == count - 1
        waits = []
        if turn == 0:
            waits += pulled
        if 0 < turn and not last:
            waits += planes[turn + 1].near[1:2]
        if turn > 0:
            waits += backs[turn - 1].swapped
        if turn > 1:
            waits.append(backs[turn - 2].crossed)
            backs[turn - 2].layer()
        pieces = planes[turn].near + planes[turn].far
        found = expert_step(
            picks_by[step],
            [tie(pieces[0], *waits)] + pieces[1:],
            gate_by[step],
            pulled[turn],
            w_gate,
            w_up,
            w_down,
            not last,
        )
        expert_rows.append(found[0])
        weighted.append(found[1])
        grad_pre.append(found[2:4])
        grad_gate_rows.append(found[4])
        backs.append(Back(step, found[5][:8]))
        if last:
            out_back = Back(step, found[5][8:])
        else:
            planes[turn + 1].finish()
            planes[turn + 1].swap()
            if turn + 2 < count:
                planes[turn + 2].cross(found[0])
            waits = list(planes[turn + 1].near[2:])
        if turn > 0:
            backs[turn - 1].first()
            if not last:
                waits += backs[turn - 1].halved
                backs[turn - 1].second()
        if not last:
            planes[turn + 1].near[0] = tie(planes[turn + 1].near[0], *waits)

    by_step = dict(zip(chain, grad_gate_rows))
    grad_gate_all = jnp.concatenate([by_step[step] for step in range(layers)]).reshape(
        device_count, capacity
    )
    grad_gates_back = jnp.sum(jnp.where(picks_true, grad_gate_all[..., None], 0.0), axis=1)
    numbers = jnp.arange(device_count, dtype=jnp.int32)
    inverse = jnp.sum(jnp.where(order[:, None] == numbers[None, :], numbers[:, None], 0), axis=0)
    grad_gates_back = jnp.take(grad_gates_back, inverse, axis=0)
    grad_gates_dense = lax.all_to_all(
        grad_gates_back, both, split_axis=0, concat_axis=0, tiled=True
    ).T

    grad_w_down = sum_of_products(weighted, grad_rows, 256)
    grad_w_gate = sum_of_products(expert_rows, [gate for gate, up in grad_pre], 256)
    grad_w_up = sum_of_products(expert_rows, [up for gate, up in grad_pre], 256)
    if count > 1:
        backs[-2].second()
    backs[-1].first()
    backs[-1].second(grad_w_down, grad_gates_dense)
    for turn, back in enumerate(backs):
        if not hasattr(back, "sum"):
            if turn < count - 1:
                back.layer()
            else:
                own = add_low(back.kept[0], back.crossed)
                back.sum = back.send(own)
    grad_mixed = sum(back.sum.astype(f32) for back in backs)
    rest = [back.rest for back in backs[:-1]]

    def send_late(turn):
        if turn < count - 1:
            rest[turn] = backs[turn].send(rest[turn])
        return rest[turn : turn + 1]

    upstream = cotangent[0].astype(f32)
    grad_gates = jnp.sum(chooser * grad_gates_dense[:, None, :], axis=-1)
    grad_chosen = gates * (grad_gates - jnp.sum(gates * grad_gates, axis=-1, keepdims=True))
    grad_logits = jnp.sum(chooser * grad_chosen[..., None], axis=1).astype(bf16)
    grad_mixed = grad_mixed + jnp.einsum(
        "te,de->td", grad_logits, router_full, preferred_element_type=f32
    )
    grad_w_router = jnp.einsum("td,te->ed", mixed, grad_logits, preferred_element_type=f32)
    router_sums = wires.total(grad_w_router)
    shard_router = lax.dynamic_slice_in_dim(
        router_sums,
        (wires.context * expert_size + wires.expert) * shard_rows,
        shard_rows,
        axis=1,
    ).T
    grad_resid_norm, post_terms = norm_backward(residual, post_inverse, post_gain, grad_mixed)
    grad_residual = upstream + grad_resid_norm
    resid_low = tie(
        wires.gather_plane(grad_residual.astype(bf16)), *out_back.swapped
    )
    out_back.first()

    grad_w_out = jnp.einsum(
        "tc,td->cd", attn_low, resid_low, preferred_element_type=f32
    ).astype(bf16)
    shard_out = lax.psum_scatter(
        grad_w_out, expert_axes, scatter_dimension=0, tiled=True
    ).astype(f32)
    grad_attn = (
        jnp.einsum("td,cd->tc", resid_low, out_rows, preferred_element_type=f32)
        .astype(bf16)
        .reshape(seq_len, group, head_size)
        .transpose(1, 0, 2)
    )
    grad_probs = jnp.einsum("htd,kd->htk", grad_attn, values, preferred_element_type=f32)
    delta = jnp.sum(probs * grad_probs, axis=-1, keepdims=True)
    delta = tie(delta, grad_w_out, *out_back.halved, *send_late(0), *send_late(1))
    out_back.second()
    grad_scores = (probs * (grad_probs - delta)).astype(bf16)
    grad_query = (
        jnp.einsum("htk,kd->htd", grad_scores, keys, preferred_element_type=f32) * score_scale
    ).astype(bf16)
    grad_key = (
        jnp.einsum("htk,htd->kd", grad_scores, queries, preferred_element_type=f32) * score_scale
    ).astype(bf16)
    grad_value = jnp.einsum(
        "htk,htd->kd", probs_low, grad_attn, preferred_element_type=f32
    ).astype(bf16)
    grad_query = tie(grad_query, out_back.crossed, *send_late(2))
    out_sum = out_back.send(add_low(out_back.kept[0], out_back.crossed))
    grad_query_raw, query_terms = norm_backward(
        query_raw,
        query_inverse,
        query_gain,
        rotate(grad_query.astype(f32), cosine_table, sine_table, -1.0),
    )
    grad_key_raw, key_terms = norm_backward(
        key_raw, key_inverse, key_gain, rotate(grad_key.astype(f32), cosine_table, sine_table, -1.0)
    )
    grad_parts = jnp.concatenate(
        [
            grad_query_raw.astype(bf16).transpose(1, 0, 2).reshape(seq_len, query_width),
            grad_key_raw.astype(bf16),
            grad_value,
        ],
        axis=1,
    )
    grad_parts = tie(grad_parts, out_sum, router_sums, shard_out)
    final = residual + out_sum.astype(f32) + sum(part.astype(f32) for part in rest)
    activation_part = jnp.einsum("tc,dc->td", grad_parts, w_qkv, preferred_element_type=f32)
    grad_activation = wires.scatter_plane(activation_part.astype(bf16))
    own_inverse = input_inverse[:tok_rows]
    grad_input_norm, unused = norm_backward(own_inputs, own_inverse, norm_gain, grad_activation)
    grad_tokens = grad_residual + grad_input_norm

    grad_w_qkv = jnp.einsum("td,tc->dc", activation, grad_parts, preferred_element_type=f32)
    column_sums = lax.psum_scatter(
        grad_w_qkv.astype(bf16)
        .reshape(context_size, expert_size, shard_rows, part_width)
        .transpose(1, 0, 2, 3)
        .reshape(model_width, part_width),
        expert_axes,
        scatter_dimension=0,
        tiled=True,
    ).reshape(context_size, shard_rows, part_width)
    shard_qkv = exchange(column_sums).transpose(1, 0, 2).astype(f32)
    shard_query = shard_qkv[:, :, :query_width].reshape(shard_rows, -1)
    shard_key = shard_qkv[:, :, query_width : query_width + head_size].reshape(shard_rows, -1)
    shard_value = shard_qkv[:, :, query_width + head_size :].reshape(shard_rows, -1)
    gains = wires.total(
        jnp.concatenate(
            [
                jnp.sum(activation_part * (inputs * input_inverse), axis=0),
                jnp.sum(post_terms, axis=0),
                jnp.sum(query_terms, axis=(0, 1)),
                jnp.sum(key_terms, axis=0),
            ]
        )
    )
    gain_norm, gain_post, gain_query, gain_key = jnp.split(
        gains, [model_width, 2 * model_width, 2 * model_width + head_size]
    )
    return (
        final.astype(bf16)[None],
        grad_tokens[None],
        gain_norm,
        shard_query,
        shard_key,
        shard_value,
        gain_query,
        gain_key,
        shard_out,
        gain_post,
        shard_router,
        grad_w_gate[None],
        grad_w_up[None],
        grad_w_down[None],
    )


def shards(
    tokens,
    span_order,
    expert_ids,
    norm_gain,
    w_query,
    key_projection_weight,
    value_projection_weight,
    query_gain,
    key_gain,
    w_out,
    post_gain,
    w_router,
    w_gate,
    w_up,
    w_down,
    cotangent,
):
    tok_rows = tokens.shape[1]
    model_width = tokens.shape[2]
    head_size = query_gain.shape[0]
    top_count = expert_ids.shape[2]
    query_heads = w_query.shape[1] // head_size
    kv_heads = key_projection_weight.shape[1] // head_size
    query_group_count = query_heads // kv_heads
    context_size = lax.axis_size("context")
    device_count = lax.axis_size(("context", "expert"))
    capacity = max(2, 2 * tok_rows * top_count // device_count)
    seq_len = tok_rows * context_size
    span_rows = tok_rows // 2
    span_count = 2 * context_size
    order_row = span_order[0]
    score_scale = head_size ** (-0.5)
    bf16 = jnp.bfloat16
    f32 = jnp.float32

    def positions(first_row, row_count):
        storage = first_row + jnp.arange(row_count, dtype=jnp.int32)
        select = (storage // span_rows)[:, None] == jnp.arange(span_count, dtype=jnp.int32)[None, :]
        return (
            jnp.sum(jnp.where(select, order_row[None, :], 0), axis=1) * span_rows
            + storage % span_rows
        )

    query_places = positions(lax.axis_index("context") * tok_rows, tok_rows)
    row_places = jnp.tile(query_places, query_group_count)
    gathered = (
        lax.all_gather(w_query, ("context", "expert"), axis=0, tiled=True),
        lax.all_gather(key_projection_weight, ("context", "expert"), axis=0, tiled=True),
        lax.all_gather(value_projection_weight, ("context", "expert"), axis=0, tiled=True),
        lax.all_gather(w_out, ("context", "expert"), axis=0, tiled=True),
        lax.all_gather(w_router, ("context", "expert"), axis=0, tiled=True),
    )
    query_full, key_full, value_full, out_full, router_full = gathered
    inputs = tokens[0].astype(f32)
    normed_in, input_inverse = norm_forward(inputs, norm_gain)
    activation_output = normed_in.astype(bf16)
    query_raw = jnp.dot(activation_output, query_full, preferred_element_type=f32).reshape(
        tok_rows, query_heads, head_size
    )
    key_unrotated = jnp.dot(activation_output, key_full, preferred_element_type=f32).reshape(
        tok_rows, kv_heads, head_size
    )
    value_flat = jnp.dot(activation_output, value_full, preferred_element_type=f32).astype(bf16)
    cosine_table, sine_table = rotary_tables(query_places, head_size)
    query_normed, query_inverse = norm_forward(query_raw, query_gain)
    key_normed, key_inverse = norm_forward(key_unrotated, key_gain)
    query_prepared = rotate(query_normed, cosine_table, sine_table, 1.0).astype(bf16)
    key_flat = (
        rotate(key_normed, cosine_table, sine_table, 1.0)
        .astype(bf16)
        .reshape(tok_rows, kv_heads * head_size)
    )
    query_arr = head_rows(query_prepared, kv_heads, query_group_count)
    row_count_all = query_group_count * tok_rows
    whole_keys, whole_values = (
        lax.all_gather(key_flat, "context", axis=0, tiled=True),
        lax.all_gather(value_flat, "context", axis=0, tiled=True),
    )
    key_block = min(512, seq_len)
    block_count = seq_len // key_block
    key_blocks = whole_keys.reshape(block_count, key_block, kv_heads, head_size)
    value_blocks = whole_values.reshape(block_count, key_block, kv_heads, head_size)
    block_firsts = key_block * jnp.arange(block_count, dtype=jnp.int32)

    def block_scores(keys_now, start_now):
        scores = (
            jnp.einsum("hrd,khd->hrk", query_arr, keys_now, preferred_element_type=f32)
            * score_scale
        )
        visible = (row_places[:, None] >= positions(start_now, key_block)[None, :])[None]
        return (scores, visible)

    def stat_block(state, packed):
        keys_now, start_now = packed
        running_max, running_total = state
        scores, visible = block_scores(keys_now, start_now)
        scores = jnp.where(visible, scores, very_negative)
        new_max = jnp.maximum(running_max, jnp.max(scores, axis=-1))
        weights = jnp.where(visible, jnp.exp(scores - new_max[..., None]), 0.0)
        running_total = running_total * jnp.exp(running_max - new_max) + jnp.sum(weights, axis=-1)
        return ((new_max, running_total), None)

    (att_max, att_total), unused = lax.scan(
        stat_block,
        (
            jnp.full((kv_heads, row_count_all), very_negative, f32),
            jnp.zeros((kv_heads, row_count_all), f32),
        ),
        (key_blocks, block_firsts),
    )
    log_total = att_max + jnp.log(att_total)

    def block_probs(keys_now, start_now):
        scores, visible = block_scores(keys_now, start_now)
        return jnp.where(visible, jnp.exp(scores - log_total[..., None]), 0.0)

    def attend_block(accum, packed):
        keys_now, values_now, start_now = packed
        probs_now = block_probs(keys_now, start_now)
        accum = accum + jnp.einsum(
            "hrk,khd->hrd", probs_now.astype(bf16), values_now, preferred_element_type=f32
        )
        return (accum, None)

    attended_output, unused = lax.scan(
        attend_block,
        jnp.zeros((kv_heads, row_count_all, head_size), f32),
        (key_blocks, value_blocks, block_firsts),
    )
    attn_low = token_rows_of(attended_output, kv_heads, query_group_count, tok_rows).astype(bf16)
    residual = inputs + jnp.dot(attn_low, out_full, preferred_element_type=f32)
    normed_post, post_inverse = norm_forward(residual, post_gain)
    mixed = normed_post.astype(bf16)
    logits = jnp.dot(mixed, router_full, preferred_element_type=f32)
    local_ids = expert_ids[0]
    chooser = (
        local_ids[:, :, None] == jnp.arange(device_count, dtype=jnp.int32)[None, None, :]
    ).astype(f32)
    chosen = jnp.sum(chooser * logits[:, None, :], axis=-1)
    gates = jax.nn.softmax(chosen, axis=-1)
    flat_ids = local_ids.reshape(-1)
    pair_hot = (flat_ids[:, None] == jnp.arange(device_count, dtype=jnp.int32)[None, :]).astype(
        jnp.int32
    )
    ranks = jnp.sum(jnp.cumsum(pair_hot, axis=0) * pair_hot, axis=1) - 1
    slots = flat_ids * capacity + ranks
    pair_rows = jnp.repeat(mixed, top_count, axis=0)
    outgoing = jnp.zeros((device_count * capacity, model_width), bf16).at[slots].set(pair_rows)
    arrived = lax.all_to_all(
        outgoing.reshape(device_count, capacity, model_width),
        ("context", "expert"),
        split_axis=0,
        concat_axis=0,
        tiled=True,
    )
    expert_rows = arrived.reshape(device_count * capacity, model_width)
    gate_pre = jnp.dot(expert_rows, w_gate[0], preferred_element_type=f32)
    up_pre = jnp.dot(expert_rows, w_up[0], preferred_element_type=f32)
    activated = jax.nn.silu(gate_pre)
    hidden = (activated * up_pre).astype(bf16)
    expert_out = jnp.dot(hidden, w_down[0], preferred_element_type=f32).astype(bf16)
    returned = lax.all_to_all(
        expert_out.reshape(device_count, capacity, model_width),
        ("context", "expert"),
        split_axis=0,
        concat_axis=0,
        tiled=True,
    )
    pair_out = (
        returned.reshape(device_count * capacity, model_width)[slots]
        .reshape(tok_rows, top_count, model_width)
        .astype(f32)
    )
    final = residual + jnp.sum(gates[..., None] * pair_out, axis=1)
    again = (
        lax.all_gather(w_query, ("context", "expert"), axis=0, tiled=True),
        lax.all_gather(key_projection_weight, ("context", "expert"), axis=0, tiled=True),
        lax.all_gather(value_projection_weight, ("context", "expert"), axis=0, tiled=True),
        lax.all_gather(w_out, ("context", "expert"), axis=0, tiled=True),
        lax.all_gather(w_router, ("context", "expert"), axis=0, tiled=True),
    )
    query_back, key_back, value_back, out_back, router_back = again
    upstream = cotangent[0].astype(f32)
    grad_gates = jnp.sum(upstream[:, None, :] * pair_out, axis=-1)
    pair_grads = (
        (upstream[:, None, :] * gates[..., None])
        .astype(bf16)
        .reshape(tok_rows * top_count, model_width)
    )
    grad_outgoing = (
        jnp.zeros((device_count * capacity, model_width), bf16).at[slots].set(pair_grads)
    )
    grad_arrived = lax.all_to_all(
        grad_outgoing.reshape(device_count, capacity, model_width),
        ("context", "expert"),
        split_axis=0,
        concat_axis=0,
        tiled=True,
    ).reshape(device_count * capacity, model_width)
    grad_w_down = jnp.einsum("rf,rd->fd", hidden, grad_arrived, preferred_element_type=f32)
    grad_hidden = jnp.einsum("rd,fd->rf", grad_arrived, w_down[0], preferred_element_type=f32)
    sigmoid = jax.nn.sigmoid(gate_pre)
    grad_gate = (grad_hidden * up_pre * sigmoid * (1.0 + gate_pre * (1.0 - sigmoid))).astype(bf16)
    grad_up = (grad_hidden * activated).astype(bf16)
    grad_w_gate = jnp.einsum("rd,rf->df", expert_rows, grad_gate, preferred_element_type=f32)
    grad_w_up = jnp.einsum("rd,rf->df", expert_rows, grad_up, preferred_element_type=f32)
    grad_rows = (
        jnp.einsum("rf,df->rd", grad_gate, w_gate[0], preferred_element_type=f32)
        + jnp.einsum("rf,df->rd", grad_up, w_up[0], preferred_element_type=f32)
    ).astype(bf16)
    grad_back = lax.all_to_all(
        grad_rows.reshape(device_count, capacity, model_width),
        ("context", "expert"),
        split_axis=0,
        concat_axis=0,
        tiled=True,
    )
    grad_mixed = jnp.sum(
        grad_back.reshape(device_count * capacity, model_width)[slots]
        .reshape(tok_rows, top_count, model_width)
        .astype(f32),
        axis=1,
    )
    grad_chosen = gates * (grad_gates - jnp.sum(gates * grad_gates, axis=-1, keepdims=True))
    grad_logits = jnp.sum(chooser * grad_chosen[..., None], axis=1).astype(bf16)
    grad_mixed = grad_mixed + jnp.einsum(
        "te,de->td", grad_logits, router_back, preferred_element_type=f32
    )
    grad_w_router = jnp.einsum("td,te->de", mixed, grad_logits, preferred_element_type=f32)
    grad_resid_norm, post_terms = norm_backward(residual, post_inverse, post_gain, grad_mixed)
    grad_residual = upstream + grad_resid_norm
    resid_low = grad_residual.astype(bf16)
    grad_w_out = jnp.einsum("tc,td->cd", attn_low, resid_low, preferred_element_type=f32)
    grad_attn = jnp.einsum("td,cd->tc", resid_low, out_back, preferred_element_type=f32).astype(
        bf16
    )
    grad_arr = head_rows(
        grad_attn.reshape(tok_rows, query_heads, head_size), kv_heads, query_group_count
    )

    def delta_block(total, packed):
        keys_now, values_now, start_now = packed
        probs_now = block_probs(keys_now, start_now)
        grad_probs = jnp.einsum("hrd,khd->hrk", grad_arr, values_now, preferred_element_type=f32)
        return (total + jnp.sum(probs_now * grad_probs, axis=-1), None)

    delta, unused = lax.scan(
        delta_block,
        jnp.zeros((kv_heads, row_count_all), f32),
        (key_blocks, value_blocks, block_firsts),
    )

    def back_block(grad_query, packed):
        keys_now, values_now, start_now = packed
        probs_now = block_probs(keys_now, start_now)
        grad_probs = jnp.einsum("hrd,khd->hrk", grad_arr, values_now, preferred_element_type=f32)
        grad_scores = (probs_now * (grad_probs - delta[..., None])).astype(bf16)
        grad_query = (
            grad_query
            + jnp.einsum("hrk,khd->hrd", grad_scores, keys_now, preferred_element_type=f32)
            * score_scale
        )
        grad_keys = (
            jnp.einsum("hrk,hrd->khd", grad_scores, query_arr, preferred_element_type=f32)
            * score_scale
        )
        grad_values = jnp.einsum(
            "hrk,hrd->khd", probs_now.astype(bf16), grad_arr, preferred_element_type=f32
        )
        return (
            grad_query,
            jnp.concatenate(
                [grad_keys.reshape(key_block, -1), grad_values.reshape(key_block, -1)], axis=-1
            ),
        )

    grad_query, key_terms = lax.scan(
        back_block,
        jnp.zeros((kv_heads, row_count_all, head_size), f32),
        (key_blocks, value_blocks, block_firsts),
    )
    own_terms = lax.psum_scatter(
        key_terms.reshape(seq_len, 2 * kv_heads * head_size),
        "context",
        scatter_dimension=0,
        tiled=True,
    )
    kv_width = kv_heads * head_size
    grad_key_rot = (
        own_terms[:, :kv_width].astype(bf16).astype(f32).reshape(tok_rows, kv_heads, head_size)
    )
    grad_value_low = own_terms[:, kv_width:].astype(bf16)
    grad_query_rot = token_rows_of(
        grad_query.astype(bf16).astype(f32), kv_heads, query_group_count, tok_rows
    ).reshape(tok_rows, query_heads, head_size)
    grad_query_raw, query_terms = norm_backward(
        query_raw, query_inverse, query_gain, rotate(grad_query_rot, cosine_table, sine_table, -1.0)
    )
    grad_key_raw, key_terms_gain = norm_backward(
        key_unrotated, key_inverse, key_gain, rotate(grad_key_rot, cosine_table, sine_table, -1.0)
    )
    grad_query_low = grad_query_raw.reshape(tok_rows, query_heads * head_size).astype(bf16)
    grad_key_low = grad_key_raw.reshape(tok_rows, kv_width).astype(bf16)
    grad_activation = (
        jnp.einsum("tc,dc->td", grad_query_low, query_back, preferred_element_type=f32)
        + jnp.einsum("tc,dc->td", grad_key_low, key_back, preferred_element_type=f32)
        + jnp.einsum("tc,dc->td", grad_value_low, value_back, preferred_element_type=f32)
    )
    grad_w_query = jnp.einsum(
        "td,tc->dc", activation_output, grad_query_low, preferred_element_type=f32
    )
    grad_w_key = jnp.einsum(
        "td,tc->dc", activation_output, grad_key_low, preferred_element_type=f32
    )
    grad_w_value = jnp.einsum(
        "td,tc->dc", activation_output, grad_value_low, preferred_element_type=f32
    )
    grad_input_norm, input_terms = norm_backward(inputs, input_inverse, norm_gain, grad_activation)
    grad_tokens = grad_residual + grad_input_norm
    shard_query, shard_key, shard_value, shard_out, shard_router = (
        lax.psum_scatter(grad_w_query, ("context", "expert"), scatter_dimension=0, tiled=True),
        lax.psum_scatter(grad_w_key, ("context", "expert"), scatter_dimension=0, tiled=True),
        lax.psum_scatter(grad_w_value, ("context", "expert"), scatter_dimension=0, tiled=True),
        lax.psum_scatter(grad_w_out, ("context", "expert"), scatter_dimension=0, tiled=True),
        lax.psum_scatter(grad_w_router, ("context", "expert"), scatter_dimension=0, tiled=True),
    )
    gain_norm, gain_post, gain_query, gain_key = lax.psum(
        (
            jnp.sum(input_terms, axis=0),
            jnp.sum(post_terms, axis=0),
            jnp.sum(query_terms, axis=(0, 1)),
            jnp.sum(key_terms_gain, axis=(0, 1)),
        ),
        ("context", "expert"),
    )
    return (
        final.astype(bf16)[None],
        grad_tokens[None],
        gain_norm,
        shard_query,
        shard_key,
        shard_value,
        gain_query,
        gain_key,
        shard_out,
        gain_post,
        shard_router,
        grad_w_gate[None],
        grad_w_up[None],
        grad_w_down[None],
    )


def placements(context, expert):
    whole = (*context, *expert)
    rows = P(expert, context, None)
    shard = P(whole, None)
    experts = P(whole, None, None)
    taken = (
        rows,
        P(expert, None),
        rows,
        P(),
        shard,
        shard,
        shard,
        P(),
        P(),
        shard,
        P(),
        shard,
        experts,
        experts,
        experts,
        rows,
    )
    given = (
        rows,
        rows,
        P(),
        shard,
        shard,
        shard,
        P(),
        P(),
        shard,
        P(),
        shard,
        experts,
        experts,
        experts,
    )
    return taken, given


def solution(mesh):
    context_size, expert_size = (mesh.shape["context"], mesh.shape["expert"])

    def step(*arrays):
        key_width, head_size = (arrays[5].shape[1], arrays[7].shape[0])
        own_head = key_width == context_size * head_size
        if own_head and context_size == 4 and expert_size % 2 == 0:
            devices = mesh.devices.reshape(2, 2, expert_size // 2, 2)
            used = Mesh(devices, both)
            taken, given = placements(context_axes, expert_axes)
            body = grouped
        else:
            used, body = (mesh, shards)
            taken, given = placements(("context",), ("expert",))
        return jax.shard_map(
            body, mesh=used, in_specs=taken, out_specs=given, check_vma=False
        )(*arrays)

    return step
```

```python
import jax
import jax.numpy as jnp
from jax import lax
from jax.experimental import pallas as pl
from jax.experimental.pallas import tpu as pltpu
from jax.sharding import Mesh
from jax.sharding import PartitionSpec as P

epsilon = 1e-06
rotary_base = 1000000.0
very_negative = -1e30


def norm_forward(values, scale_gain):
    inverse = lax.rsqrt(jnp.mean(values * values, axis=-1, keepdims=True) + epsilon)
    return (values * inverse * scale_gain, inverse)


def norm_backward(values, inverse, scale_gain, upstream):
    normed = values * inverse
    weighted = upstream * scale_gain
    inner = jnp.mean(weighted * normed, axis=-1, keepdims=True)
    return (inverse * (weighted - normed * inner), upstream * normed)


def rotary_tables(token_positions, head_width):
    half_width = head_width // 2
    frequency = rotary_base ** (-jnp.arange(half_width, dtype=jnp.float32) * 2.0 / head_width)
    angles = token_positions.astype(jnp.float32)[:, None] * frequency[None, :]
    return (jnp.cos(angles)[:, None, :], jnp.sin(angles)[:, None, :])


def rotate(values, cosine_table, sine_table, direction):
    half_width = values.shape[-1] // 2
    first_half = values[..., :half_width]
    second_half = values[..., half_width:]
    return jnp.concatenate(
        [
            first_half * cosine_table - direction * second_half * sine_table,
            second_half * cosine_table + direction * first_half * sine_table,
        ],
        axis=-1,
    )


def head_rows(array_in, kv_heads, query_group_count):
    row_total = array_in.shape[0]
    return (
        array_in.reshape(row_total, kv_heads, query_group_count, -1)
        .transpose(1, 2, 0, 3)
        .reshape(kv_heads, query_group_count * row_total, -1)
    )


def token_rows_of(array_in, kv_heads, query_group_count, tok_rows):
    return (
        array_in.reshape(kv_heads, query_group_count, tok_rows, -1)
        .transpose(2, 0, 1, 3)
        .reshape(tok_rows, -1)
    )


def dense_ranks(mask):
    width = mask.shape[-1]
    before = (
        jnp.arange(width, dtype=jnp.int32)[:, None] < jnp.arange(width, dtype=jnp.int32)[None, :]
    )
    return jnp.dot(
        mask.astype(jnp.bfloat16), before.astype(jnp.bfloat16), preferred_element_type=jnp.float32
    ).astype(jnp.int32)


context_axes = ("y", "x")
expert_axes = ("z", "core")
plane_axes = ("y", "x", "core")
both = context_axes + expert_axes
bf16 = jnp.bfloat16
f32 = jnp.float32


class Wires:
    def __init__(self, expert_size):
        self.layers = expert_size // 2
        self.context = lax.axis_index(context_axes)
        self.expert = lax.axis_index(expert_axes)
        self.core = self.expert % 2
        self.layer = self.expert // 2

    def pairs(self, move):
        found = []
        for y in range(2):
            for x in range(2):
                for z in range(self.layers):
                    for core in range(2):
                        there = move(y, x, z, core)
                        found.append((self.number(y, x, z, core), self.number(*there)))
        return found

    def number(self, y, x, z, core):
        return ((y * 2 + x) * self.layers + z) * 2 + core

    def send(self, value, move):
        return lax.ppermute(value, both, self.pairs(move))

    def swap(self, value):
        return self.send(value, lambda y, x, z, core: (y, x, z, 1 - core))

    def first(self, value):
        return self.send(
            value, lambda y, x, z, core: (y, 1 - x, z, core) if core else (1 - y, x, z, core)
        )

    def second(self, value):
        return self.send(
            value, lambda y, x, z, core: (1 - y, x, z, core) if core else (y, 1 - x, z, core)
        )

    def along(self, value, flip_y, flip_x):
        return self.send(value, lambda y, x, z, core: (y ^ flip_y, x ^ flip_x, z, core))

    def layer_flip(self, value, bit):
        return self.send(value, lambda y, x, z, core: (y, x, z ^ bit, core))

    def from_layer(self, value, step):
        return self.send(value, lambda y, x, z, core: (y, x, (z - step) % self.layers, core))

    def to_layer(self, value, step):
        return self.send(value, lambda y, x, z, core: (y, x, (z + step) % self.layers, core))

    def contexts(self, core):
        index = jnp.arange(4, dtype=jnp.int32)
        one, two = (index // 2, index % 2)
        swapped = two * 2 + one
        return self.context ^ jnp.where(core == 0, index, swapped)

    def blocks(self):
        found = []
        for step in range(self.layers):
            for flip in range(2):
                core = self.core ^ flip
                layer = (self.layer + step) % self.layers
                found.append(self.contexts(core) * (2 * self.layers) + layer * 2 + core)
        return jnp.concatenate(found)

    def gather_plane(self, value):
        crossed = self.second(value)
        return jnp.concatenate(
            [value, crossed, self.first(value), self.first(crossed)], axis=0
        )

    def scatter_plane(self, value, *after):
        half = value.shape[0] // 2
        quarter = half // 2
        there = self.first(value[half:])
        mine = tie(add_low(value[quarter:half], there[quarter:]), *after)
        kept = add_low(value[:quarter], there[:quarter])
        return kept.astype(f32) + self.second(mine).astype(f32)

    def turns(self):
        others = sorted(range(1, self.layers), key=lambda step: -min(step, self.layers - step))
        return [0] + others

    def layers_of(self, value, *after):
        found = [value]
        for turn, step in enumerate(self.turns()[1:]):
            start = tie(value, *found[-1:], *(after if turn > 0 else ()))
            found.append(self.from_layer(start, step))
        return found

    def total(self, value):
        value = value + self.swap(value)
        value = value + self.along(value, 1, 0)
        value = value + self.along(value, 0, 1)
        bit = 1
        while bit < self.layers:
            value = value + self.layer_flip(value, bit)
            bit *= 2
        return value


def add_low(one, two):
    return (one.astype(f32) + two.astype(f32)).astype(bf16)


def tie(value, *after):
    return lax.optimization_barrier((value, *after))[0]


def sum_of_products(lefts, rights, tile):
    rows, height = lefts[0].shape
    width = rights[0].shape[1]
    parts = len(lefts)

    def body(*refs):
        total = None
        for left, right in zip(refs[:parts], refs[parts : 2 * parts]):
            term = lax.dot_general(
                left[...], right[...], (((0,), (0,)), ((), ())), preferred_element_type=f32
            )
            total = term if total is None else total + term
        refs[2 * parts][...] = total

    return pl.pallas_call(
        body,
        grid=(height // tile,),
        in_specs=[pl.BlockSpec((rows, tile), lambda i: (0, i))] * parts
        + [pl.BlockSpec((rows, width), lambda i: (0, 0))] * parts,
        out_specs=pl.BlockSpec((tile, width), lambda i: (i, 0)),
        out_shape=jax.ShapeDtypeStruct((height, width), f32),
        cost_estimate=pl.CostEstimate(
            flops=2 * parts * rows * height * width,
            bytes_accessed=2 * parts * rows * (height + width) + 4 * height * width,
            transcendentals=0,
        ),
        name="sum_of_products",
    )(*lefts, *rights)


def estimate(flops, moved):
    return pl.CostEstimate(flops=flops, bytes_accessed=moved, transcendentals=0)


def fixed(shape):
    return pl.BlockSpec(shape, lambda *i: (0,) * len(shape))


def pull_step(places, picks, tables, w_down):
    blocks, capacity, halves = picks.shape
    width, tile = (w_down.shape[2], 256)
    rows, hidden_width = (blocks * capacity, w_down.shape[1])

    def body(places_ref, picks_ref, *refs):
        down_ref, rows_ref, pulled_ref = refs[blocks:]

        @pl.when(pl.program_id(0) == 0)
        def _():
            for block in range(blocks):
                rows_ref[pl.ds(block * capacity, capacity), :] = jnp.dot(
                    picks_ref[block], refs[block][0], preferred_element_type=f32
                ).astype(bf16)

        pulled_ref[...] = lax.dot_general(
            rows_ref[...], down_ref[0], (((1,), (1,)), ((), ())), preferred_element_type=f32
        )

    def piece(block):
        return pl.BlockSpec((1, halves, width), lambda i, places_ref: (places_ref[block], 0, 0))

    return pl.pallas_call(
        body,
        grid_spec=pltpu.PrefetchScalarGridSpec(
            num_scalar_prefetch=1,
            grid=(hidden_width // tile,),
            in_specs=[fixed(picks.shape)]
            + [piece(block) for block in range(blocks)]
            + [pl.BlockSpec((1, tile, width), lambda i, places_ref: (0, i, 0))],
            out_specs=[
                fixed((rows, width)),
                pl.BlockSpec((rows, tile), lambda i, places_ref: (0, i)),
            ],
        ),
        out_shape=[
            jax.ShapeDtypeStruct((rows, width), bf16),
            jax.ShapeDtypeStruct((rows, hidden_width), f32),
        ],
        cost_estimate=estimate(2 * rows * width * (hidden_width + 2 * halves), 4 * rows * width),
        name="pull_step",
    )(places, picks, *tables, w_down)


def expert_step(picks, pieces, gate, pulled, w_gate, w_up, w_down, joined):
    blocks, capacity, halves = picks.shape
    width, tile, slab = (w_gate.shape[1], 256, 32)
    rows, hidden_width = (blocks * capacity, w_gate.shape[2])
    count = hidden_width // tile

    def body(picks_ref, *refs):
        gate_ref, pulled_ref, w_gate_ref, w_up_ref, w_down_ref = refs[blocks : blocks + 5]
        rows_ref, weighted_ref, grad_gate_ref, grad_up_ref, dots_ref = refs[
            blocks + 5 : blocks + 10
        ]
        back_refs = refs[blocks + 10 : -4]
        pre_ref, up_ref, total_ref, out_ref = refs[-4:]
        turn = pl.program_id(0)

        @pl.when(turn == 0)
        def _():
            dots_ref[...] = jnp.zeros_like(dots_ref)
            for block in range(blocks):
                rows_ref[pl.ds(block * capacity, capacity), :] = jnp.dot(
                    picks_ref[block], refs[block][...], preferred_element_type=f32
                ).astype(bf16)

        pre_ref[...] = jnp.dot(rows_ref[...], w_gate_ref[0], preferred_element_type=f32)
        up_ref[...] = jnp.dot(rows_ref[...], w_up_ref[0], preferred_element_type=f32)

        @pl.loop(0, rows // slab)
        def _(place):
            at = pl.ds(pl.multiple_of(place * slab, slab), slab)
            pre, up, gates, pull = (pre_ref[at, :], up_ref[at, :], gate_ref[at, :], pulled_ref[at, :])
            sigmoid = jax.nn.sigmoid(pre)
            activated = pre * sigmoid
            hidden = activated * up
            dots_ref[at, :] += jnp.sum(hidden * pull, axis=1, keepdims=True)
            weighted_ref[at, :] = (gates * hidden).astype(bf16)
            grad_hidden = gates * pull
            grad_gate_ref[at, :] = (
                grad_hidden * up * sigmoid * (1.0 + pre * (1.0 - sigmoid))
            ).astype(bf16)
            grad_up_ref[at, :] = (grad_hidden * activated).astype(bf16)

        across = (((1,), (1,)), ((), ()))
        term = lax.dot_general(
            grad_gate_ref[...], w_gate_ref[0], across, preferred_element_type=f32
        ) + lax.dot_general(grad_up_ref[...], w_up_ref[0], across, preferred_element_type=f32)

        pair = jnp.dot(weighted_ref[...], w_down_ref[0], preferred_element_type=f32)

        @pl.when(turn == 0)
        def _():
            total_ref[...] = term
            out_ref[...] = pair

        @pl.when(turn > 0)
        def _():
            total_ref[...] += term
            out_ref[...] += pair

        @pl.when(turn == count - 1)
        def _():
            for block in range(blocks):
                for side, table in enumerate((total_ref, out_ref)):
                    found = lax.dot_general(
                        picks_ref[block],
                        table[pl.ds(block * capacity, capacity), :].astype(bf16),
                        (((0,), (0,)), ((), ())),
                        preferred_element_type=f32,
                    ).astype(bf16)
                    if joined:
                        back_refs[block][pl.ds(side * halves, halves), :] = found
                    else:
                        back_refs[side * blocks + block][...] = found

    tiled = pl.BlockSpec((rows, tile), lambda i: (0, i))
    weights = pl.BlockSpec((1, width, tile), lambda i: (0, 0, i))
    back = [((2 if joined else 1) * halves, width)] * (blocks if joined else 2 * blocks)
    narrow = jax.ShapeDtypeStruct((rows, hidden_width), bf16)
    found = pl.pallas_call(
        body,
        grid=(count,),
        in_specs=[fixed(picks.shape)]
        + [fixed((halves, width))] * blocks
        + [fixed((rows, 1)), tiled, weights, weights]
        + [pl.BlockSpec((1, tile, width), lambda i: (0, i, 0))],
        out_specs=[fixed((rows, width)), tiled, tiled, tiled, fixed((rows, 1))]
        + [fixed(shape) for shape in back],
        out_shape=[
            jax.ShapeDtypeStruct((rows, width), bf16),
            narrow,
            narrow,
            narrow,
            jax.ShapeDtypeStruct((rows, 1), f32),
        ]
        + [jax.ShapeDtypeStruct(shape, bf16) for shape in back],
        scratch_shapes=[
            pltpu.VMEM((rows, tile), f32),
            pltpu.VMEM((rows, tile), f32),
            pltpu.VMEM((rows, width), f32),
            pltpu.VMEM((rows, width), f32),
        ],
        cost_estimate=estimate(10 * rows * width * hidden_width, 24 * rows * width),
        name="expert_step",
    )(picks, *pieces, gate, pulled, w_gate, w_up, w_down)
    return (*found[:5], list(found[5:]))


def grouped(
    tokens,
    span_order,
    expert_ids,
    norm_gain,
    w_query,
    key_projection_weight,
    value_projection_weight,
    query_gain,
    key_gain,
    w_out,
    post_gain,
    w_router,
    w_gate,
    w_up,
    w_down,
    cotangent,
):
    tok_rows = tokens.shape[1]
    model_width = tokens.shape[2]
    head_size = query_gain.shape[0]
    top_count = expert_ids.shape[2]
    query_heads = w_query.shape[1] // head_size
    kv_heads = key_projection_weight.shape[1] // head_size
    group = query_heads // kv_heads
    context_size = lax.axis_size(context_axes)
    expert_size = lax.axis_size(expert_axes)
    device_count = context_size * expert_size
    wires = Wires(expert_size)
    layers = wires.layers
    chain = wires.turns()
    capacity = 2 * tok_rows * top_count // device_count
    seq_len = tok_rows * context_size
    span_rows = tok_rows // 2
    span_count = 2 * context_size
    order_row = span_order[0]
    score_scale = head_size ** (-0.5)
    shard_rows = w_query.shape[0]
    query_width = group * head_size
    part_width = query_width + 2 * head_size
    hidden_width = w_gate.shape[2]

    seq_tokens = wires.gather_plane(tokens[0])
    storage = (
        wires.contexts(wires.core)[:, None] * tok_rows
        + jnp.arange(tok_rows, dtype=jnp.int32)[None, :]
    ).reshape(-1)
    select = (storage // span_rows)[:, None] == jnp.arange(span_count, dtype=jnp.int32)[None, :]
    places = (
        jnp.sum(jnp.where(select, order_row[None, :], 0), axis=1) * span_rows + storage % span_rows
    )

    packed = jnp.concatenate(
        [
            w_query.reshape(shard_rows, context_size, query_width),
            key_projection_weight.reshape(shard_rows, context_size, head_size),
            value_projection_weight.reshape(shard_rows, context_size, head_size),
        ],
        axis=2,
    ).transpose(1, 0, 2)
    flips = wires.context ^ jnp.arange(context_size, dtype=jnp.int32)

    def exchange(parts):
        facing = jnp.take(parts, flips, axis=0)
        got = [facing[0]] + [
            wires.along(facing[flip], flip // 2, flip % 2) for flip in range(1, context_size)
        ]
        return jnp.take(jnp.stack(got), flips, axis=0)

    columns = exchange(packed)
    every_column = lax.all_gather(columns, expert_axes, axis=0, tiled=False)
    order = wires.blocks()
    chooser = (
        expert_ids[0][:, :, None] == jnp.arange(device_count, dtype=jnp.int32)[None, None, :]
    ).astype(f32)
    small = lax.all_to_all(
        jnp.concatenate(
            [
                jnp.sum(chooser, axis=1).T.astype(bf16),
                jnp.broadcast_to(w_router.reshape(1, -1), (device_count, w_router.size)),
            ],
            axis=1,
        ),
        both,
        split_axis=0,
        concat_axis=0,
        tiled=True,
    )
    router_full = small[:, tok_rows:].reshape(model_width, device_count)
    mine = jnp.take(small[:, :tok_rows], order, axis=0) > 0.5
    slot_of = dense_ranks(mine)
    picks_true = (
        slot_of[:, None, :] == jnp.arange(capacity, dtype=jnp.int32)[None, :, None]
    ) & mine[:, None, :]
    picks = picks_true.astype(bf16)
    picks_by = picks.reshape(layers, 8, capacity, tok_rows)
    count = layers

    class Plane:
        def __init__(self, column):
            self.near = [column]
            self.far = []

        def cross(self, *after):
            self.near.append(wires.second(tie(self.near[0], *after)))

        def finish(self, *after):
            self.near += [wires.first(tie(part, *after)) for part in self.near[:2]]

        def swap(self):
            self.far = [wires.swap(part) for part in self.near]

    def pull(turn, *after):
        step = chain[turn]
        if step == 0:
            plane = grad_planes[0]
            tables = [part[None] for part in plane.near + plane.far]
            places = 0 * order[:8]
        else:
            tables = [all_grads] * 8
            places = order[step * 8 : step * 8 + 8]
        found = pull_step(places, tie(picks_by[step], *after), tables, w_down)
        grad_rows[turn], pulled[turn] = found

    picks_by = tie(picks_by, router_full)
    pulled, grad_rows = ([None] * count, [None] * count)
    grad_planes = {0: Plane(cotangent[0])}
    grad_planes[0].cross()
    grad_planes[0].finish()
    grad_planes[0].swap()
    pull(0)
    out_rows = lax.all_gather(tie(w_out, pulled[0]), expert_axes, axis=0, tiled=True)
    inputs = seq_tokens.astype(f32)
    normed_in, input_inverse = norm_forward(inputs, norm_gain)
    activation = normed_in.astype(bf16)
    every_column = tie(every_column, activation, pulled[0])
    w_qkv = every_column.transpose(1, 0, 2, 3).reshape(model_width, part_width)
    projected = jnp.dot(activation, w_qkv, preferred_element_type=f32)
    query_raw = projected[:, :query_width].reshape(seq_len, group, head_size).transpose(1, 0, 2)
    key_raw = projected[:, query_width : query_width + head_size]
    values = projected[:, query_width + head_size :].astype(bf16)
    cosine_table, sine_table = rotary_tables(places, head_size)
    cosine_table, sine_table = (cosine_table[:, 0], sine_table[:, 0])
    query_normed, query_inverse = norm_forward(query_raw, query_gain)
    key_normed, key_inverse = norm_forward(key_raw, key_gain)
    queries = rotate(query_normed, cosine_table, sine_table, 1.0).astype(bf16)
    keys = rotate(key_normed, cosine_table, sine_table, 1.0).astype(bf16)
    all_grads = lax.all_gather(tie(cotangent[0], queries), both, axis=0, tiled=False)
    visible = (places[:, None] >= places[None, :])[None]
    scores = jnp.einsum("htd,kd->htk", queries, keys, preferred_element_type=f32) * score_scale
    scores = jnp.where(visible, scores, very_negative)
    peak = jnp.max(scores, axis=-1, keepdims=True)
    weights = jnp.exp(scores - peak)
    probs = weights / jnp.sum(weights, axis=-1, keepdims=True)
    probs_low = probs.astype(bf16)
    attended = jnp.einsum("htk,kd->htd", probs_low, values, preferred_element_type=f32)
    attn_low = attended.astype(bf16).transpose(1, 0, 2).reshape(seq_len, query_width)
    out_part = jnp.dot(attn_low, out_rows, preferred_element_type=f32).astype(bf16)
    own_inputs = tokens[0].astype(f32)
    residual = own_inputs + wires.scatter_plane(out_part)
    normed_post, post_inverse = norm_forward(residual, post_gain)
    mixed = normed_post.astype(bf16)
    logits = jnp.dot(mixed, router_full, preferred_element_type=f32)
    chosen = jnp.sum(chooser * logits[:, None, :], axis=-1)
    gates = jax.nn.softmax(chosen, axis=-1)
    gates_dense = jnp.sum(chooser * gates[..., None], axis=1)
    gates_mine = lax.all_to_all(gates_dense.T, both, split_axis=0, concat_axis=0, tiled=True)
    mixed_columns = wires.layers_of(mixed)
    planes = [Plane(column) for column in mixed_columns]
    planes[0].cross()
    planes[0].finish()
    planes[0].swap()
    gates_mine = tie(gates_mine, *planes[0].near)
    gates_mine = jnp.take(gates_mine, order, axis=0)
    gate_rows = jnp.sum(jnp.where(picks_true, gates_mine[:, None, :], 0.0), axis=-1)
    gate_by = gate_rows.reshape(layers, 8 * capacity, 1)

    class Back:
        def __init__(self, step, parts):
            self.step, self.near = (step, parts[:4])
            self.swapped = [wires.swap(part) for part in parts[4:]]

        def first(self, *after):
            self.leaving = [add_low(self.near[part], self.swapped[part]) for part in (2, 3)]
            self.halved = [wires.first(tie(part, *after)) for part in self.leaving]

        def second(self, *after):
            self.kept = [
                (
                    self.near[part].astype(f32)
                    + self.swapped[part].astype(f32)
                    + self.halved[part].astype(f32)
                ).astype(bf16)
                for part in (0, 1)
            ]
            self.crossed = wires.second(tie(self.kept[1], *after))

        def send(self, own):
            return own if self.step == 0 else wires.to_layer(own, self.step)

        def layer(self, *after):
            own = add_low(self.kept[0], self.crossed)
            self.sum = self.send(tie(own[:tok_rows], *after))
            self.rest = own[tok_rows:]

    expert_rows, weighted, grad_pre, grad_gate_rows, backs = ([], [], [], [], [])
    if count > 1:
        planes[1].cross()
    for turn, step in enumerate(chain):
        last = turn == count - 1
        waits = []
        if 0 < turn and not last:
            waits += planes[turn + 1].near[1:2]
        if 0 < turn and last:
            waits += backs[turn - 1].swapped
        if turn > 1:
            waits += backs[turn - 2].halved
            backs[turn - 2].second()
        if turn > 2:
            waits.append(backs[turn - 3].crossed)
            backs[turn - 3].layer()
        if turn > 1 and last:
            waits.append(backs[turn - 2].crossed)
            backs[turn - 2].layer()
        pieces = planes[turn].near + planes[turn].far
        found = expert_step(
            picks_by[step],
            [tie(pieces[0], *waits)] + pieces[1:],
            gate_by[step],
            pulled[turn],
            w_gate,
            w_up,
            w_down,
            not last,
        )
        if not last:
            pull(turn + 1, found[0])
        expert_rows.append(found[0])
        weighted.append(found[1])
        grad_pre.append(found[2:4])
        grad_gate_rows.append(found[4])
        backs.append(Back(step, found[5][:8]))
        if last:
            out_parts = found[5][8:]
            out_parts[4] = tie(out_parts[4], *backs[-1].swapped)
            out_back = Back(step, out_parts)
        else:
            planes[turn + 1].finish()
            planes[turn + 1].swap()
            if turn + 2 < count:
                planes[turn + 2].cross(found[0])
            waits = list(planes[turn + 1].near[2:])
        if turn > 0:
            backs[turn - 1].first()
        if not last:
            planes[turn + 1].near[0] = tie(planes[turn + 1].near[0], *waits)

    backs[-1].first()
    if count > 1:
        backs[-2].swapped[0] = tie(backs[-2].swapped[0], *backs[-1].leaving)
        backs[-2].second()
    backs[-1].second()
    grad_gate_rows[-1] = tie(grad_gate_rows[-1], *backs[-1].halved)
    by_step = dict(zip(chain, grad_gate_rows))
    grad_gate_all = jnp.concatenate([by_step[step] for step in range(layers)]).reshape(
        device_count, capacity
    )
    grad_gates_back = jnp.sum(jnp.where(picks_true, grad_gate_all[..., None], 0.0), axis=1)
    numbers = jnp.arange(device_count, dtype=jnp.int32)
    inverse = jnp.sum(jnp.where(order[:, None] == numbers[None, :], numbers[:, None], 0), axis=0)
    grad_gates_back = jnp.take(grad_gates_back, inverse, axis=0)
    grad_gates_dense = lax.all_to_all(
        grad_gates_back, both, split_axis=0, concat_axis=0, tiled=True
    ).T

    weighted[-1] = tie(weighted[-1], *backs[-1].halved)
    grad_w_down = sum_of_products(weighted, grad_rows, 256)
    for turn, back in enumerate(backs):
        if not hasattr(back, "sum"):
            if turn < count - 1:
                back.layer()
            else:
                own = tie(add_low(back.kept[0], back.crossed), grad_w_down)
                back.sum = back.send(own)
    grad_mixed = sum(back.sum.astype(f32) for back in backs)
    rest = [back.rest for back in backs[:-1]]

    def send_late(turn):
        if turn < count - 1:
            rest[turn] = backs[turn].send(tie(rest[turn], grad_residual))
        return rest[turn : turn + 1]

    upstream = cotangent[0].astype(f32)
    grad_gates = jnp.sum(chooser * grad_gates_dense[:, None, :], axis=-1)
    grad_chosen = gates * (grad_gates - jnp.sum(gates * grad_gates, axis=-1, keepdims=True))
    grad_logits = jnp.sum(chooser * grad_chosen[..., None], axis=1).astype(bf16)
    grad_mixed = grad_mixed + jnp.einsum(
        "te,de->td", grad_logits, router_full, preferred_element_type=f32
    )
    grad_w_router = jnp.einsum("td,te->ed", mixed, grad_logits, preferred_element_type=f32)
    grad_resid_norm, post_terms = norm_backward(residual, post_inverse, post_gain, grad_mixed)
    grad_residual = upstream + grad_resid_norm
    expert_rows[-1] = tie(expert_rows[-1], grad_residual)
    grad_w_gate = sum_of_products(expert_rows, [gate for gate, up in grad_pre], 256)
    resid_low = tie(
        wires.gather_plane(grad_residual.astype(bf16)), grad_w_gate, *out_back.swapped, *send_late(1)
    )
    out_back.swapped[0] = tie(out_back.swapped[0], grad_residual)
    out_back.first()

    grad_w_out = jnp.einsum(
        "tc,td->cd", attn_low, resid_low, preferred_element_type=f32
    ).astype(bf16)
    shard_out = lax.psum_scatter(
        grad_w_out, expert_axes, scatter_dimension=0, tiled=True
    ).astype(f32)
    grad_attn = (
        jnp.einsum("td,cd->tc", resid_low, out_rows, preferred_element_type=f32)
        .astype(bf16)
        .reshape(seq_len, group, head_size)
        .transpose(1, 0, 2)
    )
    grad_probs = jnp.einsum("htd,kd->htk", grad_attn, values, preferred_element_type=f32)
    delta = jnp.sum(probs * grad_probs, axis=-1, keepdims=True)
    delta = tie(delta, grad_w_out, *out_back.halved)
    out_back.second()
    grad_scores = (probs * (grad_probs - delta)).astype(bf16)
    grad_query = (
        jnp.einsum("htk,kd->htd", grad_scores, keys, preferred_element_type=f32) * score_scale
    ).astype(bf16)
    grad_key = (
        jnp.einsum("htk,htd->kd", grad_scores, queries, preferred_element_type=f32) * score_scale
    ).astype(bf16)
    grad_value = jnp.einsum(
        "htk,htd->kd", probs_low, grad_attn, preferred_element_type=f32
    ).astype(bf16)
    grad_query = tie(grad_query, out_back.crossed)
    for turn in [0, *range(2, count - 1)]:
        grad_query = tie(grad_query, *send_late(turn))
    out_sum = out_back.send(add_low(out_back.kept[0], out_back.crossed))
    grad_query_raw, query_terms = norm_backward(
        query_raw,
        query_inverse,
        query_gain,
        rotate(grad_query.astype(f32), cosine_table, sine_table, -1.0),
    )
    grad_key_raw, key_terms = norm_backward(
        key_raw, key_inverse, key_gain, rotate(grad_key.astype(f32), cosine_table, sine_table, -1.0)
    )
    grad_parts = jnp.concatenate(
        [
            grad_query_raw.astype(bf16).transpose(1, 0, 2).reshape(seq_len, query_width),
            grad_key_raw.astype(bf16),
            grad_value,
        ],
        axis=1,
    )
    grad_parts = tie(grad_parts, out_sum, shard_out)
    final = residual + out_sum.astype(f32) + sum(part.astype(f32) for part in rest)
    activation_part = jnp.einsum("tc,dc->td", grad_parts, w_qkv, preferred_element_type=f32)
    expert_rows[-1] = tie(expert_rows[-1], activation_part)
    grad_w_up = sum_of_products(expert_rows, [up for gate, up in grad_pre], 256)
    grad_activation = wires.scatter_plane(activation_part.astype(bf16), grad_w_up)
    own_inverse = input_inverse[:tok_rows]
    grad_input_norm, unused = norm_backward(own_inputs, own_inverse, norm_gain, grad_activation)
    grad_tokens = grad_residual + grad_input_norm

    grad_w_qkv = jnp.einsum("td,tc->dc", activation, grad_parts, preferred_element_type=f32)
    column_sums = lax.psum_scatter(
        grad_w_qkv.astype(bf16)
        .reshape(context_size, expert_size, shard_rows, part_width)
        .transpose(1, 0, 2, 3)
        .reshape(model_width, part_width),
        expert_axes,
        scatter_dimension=0,
        tiled=True,
    ).reshape(context_size, shard_rows, part_width)
    shard_qkv = exchange(column_sums).transpose(1, 0, 2).astype(f32)
    shard_query = shard_qkv[:, :, :query_width].reshape(shard_rows, -1)
    shard_key = shard_qkv[:, :, query_width : query_width + head_size].reshape(shard_rows, -1)
    shard_value = shard_qkv[:, :, query_width + head_size :].reshape(shard_rows, -1)
    router_sums = wires.total(tie(grad_w_router, activation_part))
    shard_router = lax.dynamic_slice_in_dim(
        router_sums,
        (wires.context * expert_size + wires.expert) * shard_rows,
        shard_rows,
        axis=1,
    ).T
    gains = wires.total(
        jnp.concatenate(
            [
                jnp.sum(activation_part * (inputs * input_inverse), axis=0),
                jnp.sum(post_terms, axis=0),
                jnp.sum(query_terms, axis=(0, 1)),
                jnp.sum(key_terms, axis=0),
            ]
        )
    )
    gain_norm, gain_post, gain_query, gain_key = jnp.split(
        gains, [model_width, 2 * model_width, 2 * model_width + head_size]
    )
    return (
        final.astype(bf16)[None],
        grad_tokens[None],
        gain_norm,
        shard_query,
        shard_key,
        shard_value,
        gain_query,
        gain_key,
        shard_out,
        gain_post,
        shard_router,
        grad_w_gate[None],
        grad_w_up[None],
        grad_w_down[None],
    )


def shards(
    tokens,
    span_order,
    expert_ids,
    norm_gain,
    w_query,
    key_projection_weight,
    value_projection_weight,
    query_gain,
    key_gain,
    w_out,
    post_gain,
    w_router,
    w_gate,
    w_up,
    w_down,
    cotangent,
):
    tok_rows = tokens.shape[1]
    model_width = tokens.shape[2]
    head_size = query_gain.shape[0]
    top_count = expert_ids.shape[2]
    query_heads = w_query.shape[1] // head_size
    kv_heads = key_projection_weight.shape[1] // head_size
    query_group_count = query_heads // kv_heads
    context_size = lax.axis_size("context")
    device_count = lax.axis_size(("context", "expert"))
    capacity = max(2, 2 * tok_rows * top_count // device_count)
    seq_len = tok_rows * context_size
    span_rows = tok_rows // 2
    span_count = 2 * context_size
    order_row = span_order[0]
    score_scale = head_size ** (-0.5)
    bf16 = jnp.bfloat16
    f32 = jnp.float32

    def positions(first_row, row_count):
        storage = first_row + jnp.arange(row_count, dtype=jnp.int32)
        select = (storage // span_rows)[:, None] == jnp.arange(span_count, dtype=jnp.int32)[None, :]
        return (
            jnp.sum(jnp.where(select, order_row[None, :], 0), axis=1) * span_rows
            + storage % span_rows
        )

    query_places = positions(lax.axis_index("context") * tok_rows, tok_rows)
    row_places = jnp.tile(query_places, query_group_count)
    gathered = (
        lax.all_gather(w_query, ("context", "expert"), axis=0, tiled=True),
        lax.all_gather(key_projection_weight, ("context", "expert"), axis=0, tiled=True),
        lax.all_gather(value_projection_weight, ("context", "expert"), axis=0, tiled=True),
        lax.all_gather(w_out, ("context", "expert"), axis=0, tiled=True),
        lax.all_gather(w_router, ("context", "expert"), axis=0, tiled=True),
    )
    query_full, key_full, value_full, out_full, router_full = gathered
    inputs = tokens[0].astype(f32)
    normed_in, input_inverse = norm_forward(inputs, norm_gain)
    activation_output = normed_in.astype(bf16)
    query_raw = jnp.dot(activation_output, query_full, preferred_element_type=f32).reshape(
        tok_rows, query_heads, head_size
    )
    key_unrotated = jnp.dot(activation_output, key_full, preferred_element_type=f32).reshape(
        tok_rows, kv_heads, head_size
    )
    value_flat = jnp.dot(activation_output, value_full, preferred_element_type=f32).astype(bf16)
    cosine_table, sine_table = rotary_tables(query_places, head_size)
    query_normed, query_inverse = norm_forward(query_raw, query_gain)
    key_normed, key_inverse = norm_forward(key_unrotated, key_gain)
    query_prepared = rotate(query_normed, cosine_table, sine_table, 1.0).astype(bf16)
    key_flat = (
        rotate(key_normed, cosine_table, sine_table, 1.0)
        .astype(bf16)
        .reshape(tok_rows, kv_heads * head_size)
    )
    query_arr = head_rows(query_prepared, kv_heads, query_group_count)
    row_count_all = query_group_count * tok_rows
    whole_keys, whole_values = (
        lax.all_gather(key_flat, "context", axis=0, tiled=True),
        lax.all_gather(value_flat, "context", axis=0, tiled=True),
    )
    key_block = min(512, seq_len)
    block_count = seq_len // key_block
    key_blocks = whole_keys.reshape(block_count, key_block, kv_heads, head_size)
    value_blocks = whole_values.reshape(block_count, key_block, kv_heads, head_size)
    block_firsts = key_block * jnp.arange(block_count, dtype=jnp.int32)

    def block_scores(keys_now, start_now):
        scores = (
            jnp.einsum("hrd,khd->hrk", query_arr, keys_now, preferred_element_type=f32)
            * score_scale
        )
        visible = (row_places[:, None] >= positions(start_now, key_block)[None, :])[None]
        return (scores, visible)

    def stat_block(state, packed):
        keys_now, start_now = packed
        running_max, running_total = state
        scores, visible = block_scores(keys_now, start_now)
        scores = jnp.where(visible, scores, very_negative)
        new_max = jnp.maximum(running_max, jnp.max(scores, axis=-1))
        weights = jnp.where(visible, jnp.exp(scores - new_max[..., None]), 0.0)
        running_total = running_total * jnp.exp(running_max - new_max) + jnp.sum(weights, axis=-1)
        return ((new_max, running_total), None)

    (att_max, att_total), unused = lax.scan(
        stat_block,
        (
            jnp.full((kv_heads, row_count_all), very_negative, f32),
            jnp.zeros((kv_heads, row_count_all), f32),
        ),
        (key_blocks, block_firsts),
    )
    log_total = att_max + jnp.log(att_total)

    def block_probs(keys_now, start_now):
        scores, visible = block_scores(keys_now, start_now)
        return jnp.where(visible, jnp.exp(scores - log_total[..., None]), 0.0)

    def attend_block(accum, packed):
        keys_now, values_now, start_now = packed
        probs_now = block_probs(keys_now, start_now)
        accum = accum + jnp.einsum(
            "hrk,khd->hrd", probs_now.astype(bf16), values_now, preferred_element_type=f32
        )
        return (accum, None)

    attended_output, unused = lax.scan(
        attend_block,
        jnp.zeros((kv_heads, row_count_all, head_size), f32),
        (key_blocks, value_blocks, block_firsts),
    )
    attn_low = token_rows_of(attended_output, kv_heads, query_group_count, tok_rows).astype(bf16)
    residual = inputs + jnp.dot(attn_low, out_full, preferred_element_type=f32)
    normed_post, post_inverse = norm_forward(residual, post_gain)
    mixed = normed_post.astype(bf16)
    logits = jnp.dot(mixed, router_full, preferred_element_type=f32)
    local_ids = expert_ids[0]
    chooser = (
        local_ids[:, :, None] == jnp.arange(device_count, dtype=jnp.int32)[None, None, :]
    ).astype(f32)
    chosen = jnp.sum(chooser * logits[:, None, :], axis=-1)
    gates = jax.nn.softmax(chosen, axis=-1)
    flat_ids = local_ids.reshape(-1)
    pair_hot = (flat_ids[:, None] == jnp.arange(device_count, dtype=jnp.int32)[None, :]).astype(
        jnp.int32
    )
    ranks = jnp.sum(jnp.cumsum(pair_hot, axis=0) * pair_hot, axis=1) - 1
    slots = flat_ids * capacity + ranks
    pair_rows = jnp.repeat(mixed, top_count, axis=0)
    outgoing = jnp.zeros((device_count * capacity, model_width), bf16).at[slots].set(pair_rows)
    arrived = lax.all_to_all(
        outgoing.reshape(device_count, capacity, model_width),
        ("context", "expert"),
        split_axis=0,
        concat_axis=0,
        tiled=True,
    )
    expert_rows = arrived.reshape(device_count * capacity, model_width)
    gate_pre = jnp.dot(expert_rows, w_gate[0], preferred_element_type=f32)
    up_pre = jnp.dot(expert_rows, w_up[0], preferred_element_type=f32)
    activated = jax.nn.silu(gate_pre)
    hidden = (activated * up_pre).astype(bf16)
    expert_out = jnp.dot(hidden, w_down[0], preferred_element_type=f32).astype(bf16)
    returned = lax.all_to_all(
        expert_out.reshape(device_count, capacity, model_width),
        ("context", "expert"),
        split_axis=0,
        concat_axis=0,
        tiled=True,
    )
    pair_out = (
        returned.reshape(device_count * capacity, model_width)[slots]
        .reshape(tok_rows, top_count, model_width)
        .astype(f32)
    )
    final = residual + jnp.sum(gates[..., None] * pair_out, axis=1)
    again = (
        lax.all_gather(w_query, ("context", "expert"), axis=0, tiled=True),
        lax.all_gather(key_projection_weight, ("context", "expert"), axis=0, tiled=True),
        lax.all_gather(value_projection_weight, ("context", "expert"), axis=0, tiled=True),
        lax.all_gather(w_out, ("context", "expert"), axis=0, tiled=True),
        lax.all_gather(w_router, ("context", "expert"), axis=0, tiled=True),
    )
    query_back, key_back, value_back, out_back, router_back = again
    upstream = cotangent[0].astype(f32)
    grad_gates = jnp.sum(upstream[:, None, :] * pair_out, axis=-1)
    pair_grads = (
        (upstream[:, None, :] * gates[..., None])
        .astype(bf16)
        .reshape(tok_rows * top_count, model_width)
    )
    grad_outgoing = (
        jnp.zeros((device_count * capacity, model_width), bf16).at[slots].set(pair_grads)
    )
    grad_arrived = lax.all_to_all(
        grad_outgoing.reshape(device_count, capacity, model_width),
        ("context", "expert"),
        split_axis=0,
        concat_axis=0,
        tiled=True,
    ).reshape(device_count * capacity, model_width)
    grad_w_down = jnp.einsum("rf,rd->fd", hidden, grad_arrived, preferred_element_type=f32)
    grad_hidden = jnp.einsum("rd,fd->rf", grad_arrived, w_down[0], preferred_element_type=f32)
    sigmoid = jax.nn.sigmoid(gate_pre)
    grad_gate = (grad_hidden * up_pre * sigmoid * (1.0 + gate_pre * (1.0 - sigmoid))).astype(bf16)
    grad_up = (grad_hidden * activated).astype(bf16)
    grad_w_gate = jnp.einsum("rd,rf->df", expert_rows, grad_gate, preferred_element_type=f32)
    grad_w_up = jnp.einsum("rd,rf->df", expert_rows, grad_up, preferred_element_type=f32)
    grad_rows = (
        jnp.einsum("rf,df->rd", grad_gate, w_gate[0], preferred_element_type=f32)
        + jnp.einsum("rf,df->rd", grad_up, w_up[0], preferred_element_type=f32)
    ).astype(bf16)
    grad_back = lax.all_to_all(
        grad_rows.reshape(device_count, capacity, model_width),
        ("context", "expert"),
        split_axis=0,
        concat_axis=0,
        tiled=True,
    )
    grad_mixed = jnp.sum(
        grad_back.reshape(device_count * capacity, model_width)[slots]
        .reshape(tok_rows, top_count, model_width)
        .astype(f32),
        axis=1,
    )
    grad_chosen = gates * (grad_gates - jnp.sum(gates * grad_gates, axis=-1, keepdims=True))
    grad_logits = jnp.sum(chooser * grad_chosen[..., None], axis=1).astype(bf16)
    grad_mixed = grad_mixed + jnp.einsum(
        "te,de->td", grad_logits, router_back, preferred_element_type=f32
    )
    grad_w_router = jnp.einsum("td,te->de", mixed, grad_logits, preferred_element_type=f32)
    grad_resid_norm, post_terms = norm_backward(residual, post_inverse, post_gain, grad_mixed)
    grad_residual = upstream + grad_resid_norm
    resid_low = grad_residual.astype(bf16)
    grad_w_out = jnp.einsum("tc,td->cd", attn_low, resid_low, preferred_element_type=f32)
    grad_attn = jnp.einsum("td,cd->tc", resid_low, out_back, preferred_element_type=f32).astype(
        bf16
    )
    grad_arr = head_rows(
        grad_attn.reshape(tok_rows, query_heads, head_size), kv_heads, query_group_count
    )

    def delta_block(total, packed):
        keys_now, values_now, start_now = packed
        probs_now = block_probs(keys_now, start_now)
        grad_probs = jnp.einsum("hrd,khd->hrk", grad_arr, values_now, preferred_element_type=f32)
        return (total + jnp.sum(probs_now * grad_probs, axis=-1), None)

    delta, unused = lax.scan(
        delta_block,
        jnp.zeros((kv_heads, row_count_all), f32),
        (key_blocks, value_blocks, block_firsts),
    )

    def back_block(grad_query, packed):
        keys_now, values_now, start_now = packed
        probs_now = block_probs(keys_now, start_now)
        grad_probs = jnp.einsum("hrd,khd->hrk", grad_arr, values_now, preferred_element_type=f32)
        grad_scores = (probs_now * (grad_probs - delta[..., None])).astype(bf16)
        grad_query = (
            grad_query
            + jnp.einsum("hrk,khd->hrd", grad_scores, keys_now, preferred_element_type=f32)
            * score_scale
        )
        grad_keys = (
            jnp.einsum("hrk,hrd->khd", grad_scores, query_arr, preferred_element_type=f32)
            * score_scale
        )
        grad_values = jnp.einsum(
            "hrk,hrd->khd", probs_now.astype(bf16), grad_arr, preferred_element_type=f32
        )
        return (
            grad_query,
            jnp.concatenate(
                [grad_keys.reshape(key_block, -1), grad_values.reshape(key_block, -1)], axis=-1
            ),
        )

    grad_query, key_terms = lax.scan(
        back_block,
        jnp.zeros((kv_heads, row_count_all, head_size), f32),
        (key_blocks, value_blocks, block_firsts),
    )
    own_terms = lax.psum_scatter(
        key_terms.reshape(seq_len, 2 * kv_heads * head_size),
        "context",
        scatter_dimension=0,
        tiled=True,
    )
    kv_width = kv_heads * head_size
    grad_key_rot = (
        own_terms[:, :kv_width].astype(bf16).astype(f32).reshape(tok_rows, kv_heads, head_size)
    )
    grad_value_low = own_terms[:, kv_width:].astype(bf16)
    grad_query_rot = token_rows_of(
        grad_query.astype(bf16).astype(f32), kv_heads, query_group_count, tok_rows
    ).reshape(tok_rows, query_heads, head_size)
    grad_query_raw, query_terms = norm_backward(
        query_raw, query_inverse, query_gain, rotate(grad_query_rot, cosine_table, sine_table, -1.0)
    )
    grad_key_raw, key_terms_gain = norm_backward(
        key_unrotated, key_inverse, key_gain, rotate(grad_key_rot, cosine_table, sine_table, -1.0)
    )
    grad_query_low = grad_query_raw.reshape(tok_rows, query_heads * head_size).astype(bf16)
    grad_key_low = grad_key_raw.reshape(tok_rows, kv_width).astype(bf16)
    grad_activation = (
        jnp.einsum("tc,dc->td", grad_query_low, query_back, preferred_element_type=f32)
        + jnp.einsum("tc,dc->td", grad_key_low, key_back, preferred_element_type=f32)
        + jnp.einsum("tc,dc->td", grad_value_low, value_back, preferred_element_type=f32)
    )
    grad_w_query = jnp.einsum(
        "td,tc->dc", activation_output, grad_query_low, preferred_element_type=f32
    )
    grad_w_key = jnp.einsum(
        "td,tc->dc", activation_output, grad_key_low, preferred_element_type=f32
    )
    grad_w_value = jnp.einsum(
        "td,tc->dc", activation_output, grad_value_low, preferred_element_type=f32
    )
    grad_input_norm, input_terms = norm_backward(inputs, input_inverse, norm_gain, grad_activation)
    grad_tokens = grad_residual + grad_input_norm
    shard_query, shard_key, shard_value, shard_out, shard_router = (
        lax.psum_scatter(grad_w_query, ("context", "expert"), scatter_dimension=0, tiled=True),
        lax.psum_scatter(grad_w_key, ("context", "expert"), scatter_dimension=0, tiled=True),
        lax.psum_scatter(grad_w_value, ("context", "expert"), scatter_dimension=0, tiled=True),
        lax.psum_scatter(grad_w_out, ("context", "expert"), scatter_dimension=0, tiled=True),
        lax.psum_scatter(grad_w_router, ("context", "expert"), scatter_dimension=0, tiled=True),
    )
    gain_norm, gain_post, gain_query, gain_key = lax.psum(
        (
            jnp.sum(input_terms, axis=0),
            jnp.sum(post_terms, axis=0),
            jnp.sum(query_terms, axis=(0, 1)),
            jnp.sum(key_terms_gain, axis=(0, 1)),
        ),
        ("context", "expert"),
    )
    return (
        final.astype(bf16)[None],
        grad_tokens[None],
        gain_norm,
        shard_query,
        shard_key,
        shard_value,
        gain_query,
        gain_key,
        shard_out,
        gain_post,
        shard_router,
        grad_w_gate[None],
        grad_w_up[None],
        grad_w_down[None],
    )


def placements(context, expert):
    whole = (*context, *expert)
    rows = P(expert, context, None)
    shard = P(whole, None)
    experts = P(whole, None, None)
    taken = (
        rows,
        P(expert, None),
        rows,
        P(),
        shard,
        shard,
        shard,
        P(),
        P(),
        shard,
        P(),
        shard,
        experts,
        experts,
        experts,
        rows,
    )
    given = (
        rows,
        rows,
        P(),
        shard,
        shard,
        shard,
        P(),
        P(),
        shard,
        P(),
        shard,
        experts,
        experts,
        experts,
    )
    return taken, given


def solution(mesh):
    context_size, expert_size = (mesh.shape["context"], mesh.shape["expert"])

    def step(*arrays):
        key_width, head_size = (arrays[5].shape[1], arrays[7].shape[0])
        own_head = key_width == context_size * head_size
        if own_head and context_size == 4 and expert_size % 2 == 0:
            devices = mesh.devices.reshape(2, 2, expert_size // 2, 2)
            used = Mesh(devices, both)
            taken, given = placements(context_axes, expert_axes)
            body = grouped
        else:
            used, body = (mesh, shards)
            taken, given = placements(("context",), ("expert",))
        return jax.shard_map(
            body, mesh=used, in_specs=taken, out_specs=given, check_vma=False
        )(*arrays)

    return step
```

```python
import jax
import jax.numpy as jnp
from jax import lax
from jax.experimental import pallas as pl
from jax.experimental.pallas import tpu as pltpu
from jax.sharding import Mesh
from jax.sharding import PartitionSpec as P

epsilon = 1e-06
rotary_base = 1000000.0
very_negative = -1e30


def norm_forward(values, scale_gain):
    inverse = lax.rsqrt(jnp.mean(values * values, axis=-1, keepdims=True) + epsilon)
    return (values * inverse * scale_gain, inverse)


def norm_backward(values, inverse, scale_gain, upstream):
    normed = values * inverse
    weighted = upstream * scale_gain
    inner = jnp.mean(weighted * normed, axis=-1, keepdims=True)
    return (inverse * (weighted - normed * inner), upstream * normed)


def rotary_tables(token_positions, head_width):
    half_width = head_width // 2
    frequency = rotary_base ** (-jnp.arange(half_width, dtype=jnp.float32) * 2.0 / head_width)
    angles = token_positions.astype(jnp.float32)[:, None] * frequency[None, :]
    return (jnp.cos(angles)[:, None, :], jnp.sin(angles)[:, None, :])


def rotate(values, cosine_table, sine_table, direction):
    half_width = values.shape[-1] // 2
    first_half = values[..., :half_width]
    second_half = values[..., half_width:]
    return jnp.concatenate(
        [
            first_half * cosine_table - direction * second_half * sine_table,
            second_half * cosine_table + direction * first_half * sine_table,
        ],
        axis=-1,
    )


def head_rows(array_in, kv_heads, query_group_count):
    row_total = array_in.shape[0]
    return (
        array_in.reshape(row_total, kv_heads, query_group_count, -1)
        .transpose(1, 2, 0, 3)
        .reshape(kv_heads, query_group_count * row_total, -1)
    )


def token_rows_of(array_in, kv_heads, query_group_count, tok_rows):
    return (
        array_in.reshape(kv_heads, query_group_count, tok_rows, -1)
        .transpose(2, 0, 1, 3)
        .reshape(tok_rows, -1)
    )


def dense_ranks(mask):
    width = mask.shape[-1]
    before = (
        jnp.arange(width, dtype=jnp.int32)[:, None] < jnp.arange(width, dtype=jnp.int32)[None, :]
    )
    return jnp.dot(
        mask.astype(jnp.bfloat16), before.astype(jnp.bfloat16), preferred_element_type=jnp.float32
    ).astype(jnp.int32)


context_axes = ("y", "x")
expert_axes = ("z", "core")
plane_axes = ("y", "x", "core")
both = context_axes + expert_axes
bf16 = jnp.bfloat16
f32 = jnp.float32


class Wires:
    def __init__(self, expert_size):
        self.layers = expert_size // 2
        self.context = lax.axis_index(context_axes)
        self.expert = lax.axis_index(expert_axes)
        self.core = self.expert % 2
        self.layer = self.expert // 2

    def pairs(self, move):
        found = []
        for y in range(2):
            for x in range(2):
                for z in range(self.layers):
                    for core in range(2):
                        there = move(y, x, z, core)
                        found.append((self.number(y, x, z, core), self.number(*there)))
        return found

    def number(self, y, x, z, core):
        return ((y * 2 + x) * self.layers + z) * 2 + core

    def send(self, value, move):
        return lax.ppermute(value, both, self.pairs(move))

    def swap(self, value):
        return self.send(value, lambda y, x, z, core: (y, x, z, 1 - core))

    def first(self, value):
        return self.send(
            value, lambda y, x, z, core: (y, 1 - x, z, core) if core else (1 - y, x, z, core)
        )

    def second(self, value):
        return self.send(
            value, lambda y, x, z, core: (1 - y, x, z, core) if core else (y, 1 - x, z, core)
        )

    def along(self, value, flip_y, flip_x):
        return self.send(value, lambda y, x, z, core: (y ^ flip_y, x ^ flip_x, z, core))

    def layer_flip(self, value, bit):
        return self.send(value, lambda y, x, z, core: (y, x, z ^ bit, core))

    def from_layer(self, value, step):
        return self.send(value, lambda y, x, z, core: (y, x, (z - step) % self.layers, core))

    def to_layer(self, value, step):
        return self.send(value, lambda y, x, z, core: (y, x, (z + step) % self.layers, core))

    def contexts(self, core):
        index = jnp.arange(4, dtype=jnp.int32)
        one, two = (index // 2, index % 2)
        swapped = two * 2 + one
        return self.context ^ jnp.where(core == 0, index, swapped)

    def blocks(self):
        found = []
        for step in range(self.layers):
            for flip in range(2):
                core = self.core ^ flip
                layer = (self.layer + step) % self.layers
                found.append(self.contexts(core) * (2 * self.layers) + layer * 2 + core)
        return jnp.concatenate(found)

    def gather_plane(self, value):
        crossed = self.second(value)
        return jnp.concatenate(
            [value, crossed, self.first(value), self.first(crossed)], axis=0
        )

    def scatter_plane(self, value, *after):
        half = value.shape[0] // 2
        quarter = half // 2
        there = self.first(value[half:])
        mine = tie(add_low(value[quarter:half], there[quarter:]), *after)
        kept = add_low(value[:quarter], there[:quarter])
        return kept.astype(f32) + self.second(mine).astype(f32)

    def turns(self):
        others = sorted(range(1, self.layers), key=lambda step: -min(step, self.layers - step))
        return [0] + others

    def layers_of(self, value, *after):
        found = [value]
        for turn, step in enumerate(self.turns()[1:]):
            start = tie(value, *found[-1:], *(after if turn > 0 else ()))
            found.append(self.from_layer(start, step))
        return found

    def total(self, value):
        value = value + self.swap(value)
        value = value + self.along(value, 1, 0)
        value = value + self.along(value, 0, 1)
        bit = 1
        while bit < self.layers:
            value = value + self.layer_flip(value, bit)
            bit *= 2
        return value


def add_low(one, two):
    return (one.astype(f32) + two.astype(f32)).astype(bf16)


def tie(value, *after):
    return lax.optimization_barrier((value, *after))[0]


def sum_of_products(lefts, rights, tile):
    rows, height = lefts[0].shape
    width = rights[0].shape[1]
    parts = len(lefts)

    def body(*refs):
        total = None
        for left, right in zip(refs[:parts], refs[parts : 2 * parts]):
            term = lax.dot_general(
                left[...], right[...], (((0,), (0,)), ((), ())), preferred_element_type=f32
            )
            total = term if total is None else total + term
        refs[2 * parts][...] = total

    return pl.pallas_call(
        body,
        grid=(height // tile,),
        in_specs=[pl.BlockSpec((rows, tile), lambda i: (0, i))] * parts
        + [pl.BlockSpec((rows, width), lambda i: (0, 0))] * parts,
        out_specs=pl.BlockSpec((tile, width), lambda i: (i, 0)),
        out_shape=jax.ShapeDtypeStruct((height, width), f32),
        cost_estimate=pl.CostEstimate(
            flops=2 * parts * rows * height * width,
            bytes_accessed=2 * parts * rows * (height + width) + 4 * height * width,
            transcendentals=0,
        ),
        name="sum_of_products",
    )(*lefts, *rights)


def estimate(flops, moved):
    return pl.CostEstimate(flops=flops, bytes_accessed=moved, transcendentals=0)


def fixed(shape):
    return pl.BlockSpec(shape, lambda *i: (0,) * len(shape))


def add_pairs(nears, fars):
    count, (rows, width) = (len(nears), nears[0].shape)
    slab = rows // 2

    def body(*refs):
        for place in range(count):
            refs[-1][place] = add_low(refs[place][...], refs[count + place][...])

    return pl.pallas_call(
        body,
        grid=(rows // slab,),
        in_specs=[pl.BlockSpec((slab, width), lambda i: (i, 0))] * (2 * count),
        out_specs=pl.BlockSpec((count, slab, width), lambda i: (0, i, 0)),
        out_shape=jax.ShapeDtypeStruct((count, rows, width), bf16),
        cost_estimate=estimate(count * rows * width, 6 * count * rows * width),
        name="add_pairs",
    )(*nears, *fars).reshape(count * rows, width)


def pull_step(places, picks, tables, w_down):
    blocks, capacity, halves = picks.shape
    width, tile = (w_down.shape[2], 256)
    rows, hidden_width = (blocks * capacity, w_down.shape[1])

    def body(places_ref, picks_ref, *refs):
        down_ref, rows_ref, pulled_ref = refs[blocks:]

        @pl.when(pl.program_id(0) == 0)
        def _():
            for block in range(blocks):
                rows_ref[pl.ds(block * capacity, capacity), :] = jnp.dot(
                    picks_ref[block], refs[block][0], preferred_element_type=f32
                ).astype(bf16)

        pulled_ref[...] = lax.dot_general(
            rows_ref[...], down_ref[0], (((1,), (1,)), ((), ())), preferred_element_type=f32
        )

    def piece(block):
        return pl.BlockSpec((1, halves, width), lambda i, places_ref: (places_ref[block], 0, 0))

    return pl.pallas_call(
        body,
        grid_spec=pltpu.PrefetchScalarGridSpec(
            num_scalar_prefetch=1,
            grid=(hidden_width // tile,),
            in_specs=[fixed(picks.shape)]
            + [piece(block) for block in range(blocks)]
            + [pl.BlockSpec((1, tile, width), lambda i, places_ref: (0, i, 0))],
            out_specs=[
                fixed((rows, width)),
                pl.BlockSpec((rows, tile), lambda i, places_ref: (0, i)),
            ],
        ),
        out_shape=[
            jax.ShapeDtypeStruct((rows, width), bf16),
            jax.ShapeDtypeStruct((rows, hidden_width), f32),
        ],
        cost_estimate=estimate(2 * rows * width * (hidden_width + 2 * halves), 4 * rows * width),
        name="pull_step",
    )(places, picks, *tables, w_down)


def expert_step(picks, pieces, gate, pulled, w_gate, w_up, w_down, joined):
    blocks, capacity, halves = picks.shape
    width, tile, slab = (w_gate.shape[1], 256, 32)
    rows, hidden_width = (blocks * capacity, w_gate.shape[2])
    count = hidden_width // tile

    wide = 512
    tail = width // wide

    def body(picks_ref, *refs):
        gate_ref, pulled_ref, w_gate_ref, w_up_ref = refs[blocks : blocks + 4]
        gate_back_ref, up_back_ref, down_ref = refs[blocks + 4 : blocks + 7]
        rows_ref, weighted_ref, grad_gate_ref, grad_up_ref, dots_ref = refs[
            blocks + 7 : blocks + 12
        ]
        back_refs, (pre_ref, up_ref) = (refs[blocks + 12 : -2], refs[-2:])
        turn = pl.program_id(0)

        @pl.when(turn == 0)
        def _():
            dots_ref[...] = jnp.zeros_like(dots_ref)
            for block in range(blocks):
                rows_ref[pl.ds(block * capacity, capacity), :] = jnp.dot(
                    picks_ref[block], refs[block][...], preferred_element_type=f32
                ).astype(bf16)

        @pl.when(turn < count)
        def _():
            pre_ref[...] = jnp.dot(rows_ref[...], w_gate_ref[0], preferred_element_type=f32)
            up_ref[...] = jnp.dot(rows_ref[...], w_up_ref[0], preferred_element_type=f32)
            columns = pl.ds(pl.multiple_of(turn * tile, tile), tile)

            @pl.loop(0, rows // slab)
            def _(place):
                at = pl.ds(pl.multiple_of(place * slab, slab), slab)
                pre, up, gates, pull = (
                    pre_ref[at, :],
                    up_ref[at, :],
                    gate_ref[at, :],
                    pulled_ref[at, :],
                )
                sigmoid = jax.nn.sigmoid(pre)
                activated = pre * sigmoid
                hidden = activated * up
                dots_ref[at, :] += jnp.sum(hidden * pull, axis=1, keepdims=True)
                weighted_ref[at, columns] = (gates * hidden).astype(bf16)
                grad_hidden = gates * pull
                grad_gate_ref[at, columns] = (
                    grad_hidden * up * sigmoid * (1.0 + pre * (1.0 - sigmoid))
                ).astype(bf16)
                grad_up_ref[at, columns] = (grad_hidden * activated).astype(bf16)

        @pl.when(turn >= count)
        def _():
            across = (((1,), (1,)), ((), ()))
            pair = lax.dot_general(
                grad_gate_ref[...], gate_back_ref[0], across, preferred_element_type=f32
            ) + lax.dot_general(
                grad_up_ref[...], up_back_ref[0], across, preferred_element_type=f32
            )
            out = jnp.dot(weighted_ref[...], down_ref[0], preferred_element_type=f32)
            for side, table in enumerate((pair.astype(bf16), out.astype(bf16))):
                for block in range(blocks):
                    found = lax.dot_general(
                        picks_ref[block],
                        table[block * capacity : (block + 1) * capacity],
                        (((0,), (0,)), ((), ())),
                        preferred_element_type=f32,
                    ).astype(bf16)
                    if joined:
                        back_refs[block][pl.ds(side * halves, halves), :] = found
                    else:
                        back_refs[side * blocks + block][...] = found

    def ahead(i):
        return jnp.minimum(i, count - 1)

    def behind(i):
        return jnp.maximum(i - count, 0)

    weights = pl.BlockSpec((1, width, tile), lambda i: (0, 0, ahead(i)))
    weights_back = pl.BlockSpec((1, wide, hidden_width), lambda i: (0, behind(i), 0))
    narrow = jax.ShapeDtypeStruct((rows, hidden_width), bf16)
    back = [((2 if joined else 1) * halves, width)] * (blocks if joined else 2 * blocks)
    found = pl.pallas_call(
        body,
        grid=(count + tail,),
        in_specs=[fixed(picks.shape)]
        + [fixed((halves, width))] * blocks
        + [
            fixed((rows, 1)),
            pl.BlockSpec((rows, tile), lambda i: (0, ahead(i))),
            weights,
            weights,
            weights_back,
            weights_back,
            pl.BlockSpec((1, hidden_width, wide), lambda i: (0, 0, behind(i))),
        ],
        out_specs=[fixed((rows, width))]
        + [fixed((rows, hidden_width))] * 3
        + [fixed((rows, 1))]
        + [pl.BlockSpec((shape[0], wide), lambda i: (0, behind(i))) for shape in back],
        out_shape=[
            jax.ShapeDtypeStruct((rows, width), bf16),
            narrow,
            narrow,
            narrow,
            jax.ShapeDtypeStruct((rows, 1), f32),
        ]
        + [jax.ShapeDtypeStruct(shape, bf16) for shape in back],
        scratch_shapes=[pltpu.VMEM((rows, tile), f32), pltpu.VMEM((rows, tile), f32)],
        cost_estimate=estimate(10 * rows * width * hidden_width, 24 * rows * width),
        name="expert_step",
    )(picks, *pieces, gate, pulled, w_gate, w_up, w_gate, w_up, w_down)
    return (*found[:5], list(found[5:]))


def grouped(
    tokens,
    span_order,
    expert_ids,
    norm_gain,
    w_query,
    key_projection_weight,
    value_projection_weight,
    query_gain,
    key_gain,
    w_out,
    post_gain,
    w_router,
    w_gate,
    w_up,
    w_down,
    cotangent,
):
    tok_rows = tokens.shape[1]
    model_width = tokens.shape[2]
    head_size = query_gain.shape[0]
    top_count = expert_ids.shape[2]
    query_heads = w_query.shape[1] // head_size
    kv_heads = key_projection_weight.shape[1] // head_size
    group = query_heads // kv_heads
    context_size = lax.axis_size(context_axes)
    expert_size = lax.axis_size(expert_axes)
    device_count = context_size * expert_size
    wires = Wires(expert_size)
    layers = wires.layers
    chain = wires.turns()
    capacity = 2 * tok_rows * top_count // device_count
    seq_len = tok_rows * context_size
    span_rows = tok_rows // 2
    span_count = 2 * context_size
    order_row = span_order[0]
    score_scale = head_size ** (-0.5)
    shard_rows = w_query.shape[0]
    query_width = group * head_size
    part_width = query_width + 2 * head_size
    hidden_width = w_gate.shape[2]

    seq_tokens = wires.gather_plane(tokens[0])
    storage = (
        wires.contexts(wires.core)[:, None] * tok_rows
        + jnp.arange(tok_rows, dtype=jnp.int32)[None, :]
    ).reshape(-1)
    select = (storage // span_rows)[:, None] == jnp.arange(span_count, dtype=jnp.int32)[None, :]
    places = (
        jnp.sum(jnp.where(select, order_row[None, :], 0), axis=1) * span_rows + storage % span_rows
    )

    packed = jnp.concatenate(
        [
            w_query.reshape(shard_rows, context_size, query_width),
            key_projection_weight.reshape(shard_rows, context_size, head_size),
            value_projection_weight.reshape(shard_rows, context_size, head_size),
        ],
        axis=2,
    ).transpose(1, 0, 2)
    flips = wires.context ^ jnp.arange(context_size, dtype=jnp.int32)

    def exchange(parts):
        facing = jnp.take(parts, flips, axis=0)
        got = [facing[0]] + [
            wires.along(facing[flip], flip // 2, flip % 2) for flip in range(1, context_size)
        ]
        return jnp.take(jnp.stack(got), flips, axis=0)

    columns = exchange(packed)
    every_column = lax.all_gather(columns, expert_axes, axis=0, tiled=False)
    order = wires.blocks()
    chooser = (
        expert_ids[0][:, :, None] == jnp.arange(device_count, dtype=jnp.int32)[None, None, :]
    ).astype(f32)
    small = lax.all_to_all(
        jnp.concatenate(
            [
                jnp.sum(chooser, axis=1).T.astype(bf16),
                jnp.broadcast_to(w_router.reshape(1, -1), (device_count, w_router.size)),
            ],
            axis=1,
        ),
        both,
        split_axis=0,
        concat_axis=0,
        tiled=True,
    )
    router_full = small[:, tok_rows:].reshape(model_width, device_count)
    mine = jnp.take(small[:, :tok_rows], order, axis=0) > 0.5
    slot_of = dense_ranks(mine)
    picks_true = (
        slot_of[:, None, :] == jnp.arange(capacity, dtype=jnp.int32)[None, :, None]
    ) & mine[:, None, :]
    picks = picks_true.astype(bf16)
    picks_by = picks.reshape(layers, 8, capacity, tok_rows)
    count = layers

    class Plane:
        def __init__(self, column):
            self.near = [column]
            self.far = []

        def cross(self, *after):
            self.near.append(wires.second(tie(self.near[0], *after)))

        def finish(self, *after):
            self.near += [wires.first(tie(part, *after)) for part in self.near[:2]]

        def swap(self):
            self.far = [wires.swap(part) for part in self.near]

    def pull(turn, *after):
        step = chain[turn]
        if step == 0:
            plane = grad_planes[0]
            tables = [part[None] for part in plane.near + plane.far]
            places = 0 * order[:8]
        else:
            tables = [all_grads] * 8
            places = order[step * 8 : step * 8 + 8]
        found = pull_step(places, tie(picks_by[step], *after), tables, w_down)
        grad_rows[turn], pulled[turn] = found

    picks_by = tie(picks_by, router_full, seq_tokens)
    pulled, grad_rows = ([None] * count, [None] * count)
    grad_planes = {0: Plane(cotangent[0])}
    grad_planes[0].cross()
    grad_planes[0].finish()
    grad_planes[0].swap()
    pull(0)
    out_rows = lax.all_gather(tie(w_out, pulled[0]), expert_axes, axis=0, tiled=True)
    inputs = seq_tokens.astype(f32)
    normed_in, input_inverse = norm_forward(inputs, norm_gain)
    activation = normed_in.astype(bf16)
    every_column = tie(every_column, activation, pulled[0])
    w_qkv = every_column.transpose(1, 0, 2, 3).reshape(model_width, part_width)
    projected = jnp.dot(activation, w_qkv, preferred_element_type=f32)
    query_raw = projected[:, :query_width].reshape(seq_len, group, head_size).transpose(1, 0, 2)
    key_raw = projected[:, query_width : query_width + head_size]
    values = projected[:, query_width + head_size :].astype(bf16)
    cosine_table, sine_table = rotary_tables(places, head_size)
    cosine_table, sine_table = (cosine_table[:, 0], sine_table[:, 0])
    query_normed, query_inverse = norm_forward(query_raw, query_gain)
    key_normed, key_inverse = norm_forward(key_raw, key_gain)
    queries = rotate(query_normed, cosine_table, sine_table, 1.0).astype(bf16)
    keys = rotate(key_normed, cosine_table, sine_table, 1.0).astype(bf16)
    all_grads = lax.all_gather(tie(cotangent[0], queries), both, axis=0, tiled=False)
    visible = (places[:, None] >= places[None, :])[None]
    scores = jnp.einsum("htd,kd->htk", queries, keys, preferred_element_type=f32) * score_scale
    scores = jnp.where(visible, scores, very_negative)
    peak = jnp.max(scores, axis=-1, keepdims=True)
    weights = jnp.exp(scores - peak)
    probs = weights / jnp.sum(weights, axis=-1, keepdims=True)
    probs_low = probs.astype(bf16)
    attended = jnp.einsum("htk,kd->htd", probs_low, values, preferred_element_type=f32)
    attn_low = attended.astype(bf16).transpose(1, 0, 2).reshape(seq_len, query_width)
    out_part = jnp.dot(attn_low, out_rows, preferred_element_type=f32).astype(bf16)
    own_inputs = tokens[0].astype(f32)
    residual = own_inputs + wires.scatter_plane(out_part)
    normed_post, post_inverse = norm_forward(residual, post_gain)
    mixed = normed_post.astype(bf16)
    logits = jnp.dot(mixed, router_full, preferred_element_type=f32)
    chosen = jnp.sum(chooser * logits[:, None, :], axis=-1)
    gates = jax.nn.softmax(chosen, axis=-1)
    gates_dense = jnp.sum(chooser * gates[..., None], axis=1)
    gates_mine = lax.all_to_all(gates_dense.T, both, split_axis=0, concat_axis=0, tiled=True)
    mixed_columns = wires.layers_of(mixed)
    planes = [Plane(column) for column in mixed_columns]
    planes[0].cross()
    planes[0].finish()
    planes[0].swap()
    gates_mine = tie(gates_mine, *planes[0].near)
    gates_mine = jnp.take(gates_mine, order, axis=0)
    gate_rows = jnp.sum(jnp.where(picks_true, gates_mine[:, None, :], 0.0), axis=-1)
    gate_by = gate_rows.reshape(layers, 8 * capacity, 1)

    class Back:
        def __init__(self, step, parts):
            self.step, self.near = (step, parts[:4])
            self.swapped = [wires.swap(part) for part in parts[4:]]

        def first(self, *after):
            self.leaving = [add_pairs(self.near[2:], self.swapped[2:])]
            self.halved = [wires.first(tie(self.leaving[0], *after))]

        def second(self, *after):
            half = self.halved[0].reshape(2, *self.near[0].shape)
            self.kept = [
                (
                    self.near[part].astype(f32)
                    + self.swapped[part].astype(f32)
                    + half[part].astype(f32)
                ).astype(bf16)
                for part in (0, 1)
            ]
            self.crossed = wires.second(tie(self.kept[1], *after))

        def send(self, own):
            return own if self.step == 0 else wires.to_layer(own, self.step)

        def layer(self, *after):
            own = add_low(self.kept[0], self.crossed)
            self.sum = self.send(tie(own[:tok_rows], *after))
            self.rest = own[tok_rows:]

    expert_rows, weighted, grad_pre, grad_gate_rows, backs = ([], [], [], [], [])
    if count > 1:
        planes[1].cross()
    for turn, step in enumerate(chain):
        last = turn == count - 1
        waits = []
        if 0 < turn and not last:
            waits += planes[turn + 1].near[1:]
        if 0 < turn and last:
            waits += backs[turn - 1].swapped
        if turn > 1:
            waits += backs[turn - 2].halved
            backs[turn - 2].second()
        if turn > 2:
            waits.append(backs[turn - 3].crossed)
            backs[turn - 3].layer()
        if turn > 1 and last:
            waits.append(backs[turn - 2].crossed)
            backs[turn - 2].layer()
        pieces = planes[turn].near + planes[turn].far
        found = expert_step(
            picks_by[step],
            [tie(pieces[0], *waits)] + pieces[1:],
            gate_by[step],
            pulled[turn],
            w_gate,
            w_up,
            w_down,
            not last,
        )
        if not last:
            pull(turn + 1, found[0])
        expert_rows.append(found[0])
        weighted.append(found[1])
        grad_pre.append(found[2:4])
        grad_gate_rows.append(found[4])
        backs.append(Back(step, found[5][:8]))
        if last:
            out_parts = found[5][8:]
            out_parts[4] = tie(out_parts[4], *backs[-1].swapped)
            out_back = Back(step, out_parts)
        else:
            planes[turn + 1].finish()
            planes[turn + 1].swap()
            if turn + 2 < count:
                planes[turn + 2].cross(found[0])
            waits = list(planes[turn + 1].near[2:])
        if turn > 0:
            backs[turn - 1].first()
        if not last:
            planes[turn + 1].near[0] = tie(planes[turn + 1].near[0], *waits)

    backs[-1].first()
    if count > 1:
        backs[-2].swapped[0] = tie(backs[-2].swapped[0], *backs[-1].leaving)
        backs[-2].second()
    backs[-1].second()
    grad_gate_rows[-1] = tie(grad_gate_rows[-1], *backs[-1].halved)
    by_step = dict(zip(chain, grad_gate_rows))
    grad_gate_all = jnp.concatenate([by_step[step] for step in range(layers)]).reshape(
        device_count, capacity
    )
    grad_gates_back = jnp.sum(jnp.where(picks_true, grad_gate_all[..., None], 0.0), axis=1)
    numbers = jnp.arange(device_count, dtype=jnp.int32)
    inverse = jnp.sum(jnp.where(order[:, None] == numbers[None, :], numbers[:, None], 0), axis=0)
    grad_gates_back = jnp.take(grad_gates_back, inverse, axis=0)
    grad_gates_dense = lax.all_to_all(
        grad_gates_back, both, split_axis=0, concat_axis=0, tiled=True
    ).T

    weighted[-1] = tie(weighted[-1], *backs[-1].halved)
    grad_w_down = sum_of_products(weighted, grad_rows, 256)
    for turn, back in enumerate(backs):
        if not hasattr(back, "sum"):
            if turn < count - 1:
                back.layer()
            else:
                own = tie(add_low(back.kept[0], back.crossed), grad_w_down)
                back.sum = back.send(own)
    grad_mixed = sum(back.sum.astype(f32) for back in backs)
    rest = [back.rest for back in backs[:-1]]

    def send_late(turn):
        if turn < count - 1:
            rest[turn] = backs[turn].send(tie(rest[turn], grad_residual))
        return rest[turn : turn + 1]

    upstream = cotangent[0].astype(f32)
    grad_gates = jnp.sum(chooser * grad_gates_dense[:, None, :], axis=-1)
    grad_chosen = gates * (grad_gates - jnp.sum(gates * grad_gates, axis=-1, keepdims=True))
    grad_logits = jnp.sum(chooser * grad_chosen[..., None], axis=1).astype(bf16)
    grad_mixed = grad_mixed + jnp.einsum(
        "te,de->td", grad_logits, router_full, preferred_element_type=f32
    )
    grad_w_router = jnp.einsum("td,te->ed", mixed, grad_logits, preferred_element_type=f32)
    grad_resid_norm, post_terms = norm_backward(residual, post_inverse, post_gain, grad_mixed)
    grad_residual = upstream + grad_resid_norm
    expert_rows[-1] = tie(expert_rows[-1], grad_residual)
    grad_w_gate = sum_of_products(expert_rows, [gate for gate, up in grad_pre], 256)
    resid_low = tie(
        wires.gather_plane(grad_residual.astype(bf16)), grad_w_gate, *out_back.swapped, *send_late(1)
    )
    out_back.swapped[0] = tie(out_back.swapped[0], grad_residual)
    out_back.first()

    grad_w_out = jnp.einsum(
        "tc,td->cd", attn_low, resid_low, preferred_element_type=f32
    ).astype(bf16)
    shard_out = lax.psum_scatter(
        grad_w_out, expert_axes, scatter_dimension=0, tiled=True
    ).astype(f32)
    grad_attn = (
        jnp.einsum("td,cd->tc", resid_low, out_rows, preferred_element_type=f32)
        .astype(bf16)
        .reshape(seq_len, group, head_size)
        .transpose(1, 0, 2)
    )
    grad_probs = jnp.einsum("htd,kd->htk", grad_attn, values, preferred_element_type=f32)
    delta = jnp.sum(probs * grad_probs, axis=-1, keepdims=True)
    delta = tie(delta, grad_w_out, *out_back.halved)
    out_back.second()
    grad_scores = (probs * (grad_probs - delta)).astype(bf16)
    grad_query = (
        jnp.einsum("htk,kd->htd", grad_scores, keys, preferred_element_type=f32) * score_scale
    ).astype(bf16)
    grad_key = (
        jnp.einsum("htk,htd->kd", grad_scores, queries, preferred_element_type=f32) * score_scale
    ).astype(bf16)
    grad_value = jnp.einsum(
        "htk,htd->kd", probs_low, grad_attn, preferred_element_type=f32
    ).astype(bf16)
    grad_query = tie(grad_query, out_back.crossed)
    for turn in [0, *range(2, count - 1)]:
        grad_query = tie(grad_query, *send_late(turn))
    out_sum = out_back.send(add_low(out_back.kept[0], out_back.crossed))
    grad_query_raw, query_terms = norm_backward(
        query_raw,
        query_inverse,
        query_gain,
        rotate(grad_query.astype(f32), cosine_table, sine_table, -1.0),
    )
    grad_key_raw, key_terms = norm_backward(
        key_raw, key_inverse, key_gain, rotate(grad_key.astype(f32), cosine_table, sine_table, -1.0)
    )
    grad_parts = jnp.concatenate(
        [
            grad_query_raw.astype(bf16).transpose(1, 0, 2).reshape(seq_len, query_width),
            grad_key_raw.astype(bf16),
            grad_value,
        ],
        axis=1,
    )
    grad_parts = tie(grad_parts, out_sum, shard_out)
    final = residual + out_sum.astype(f32) + sum(part.astype(f32) for part in rest)
    activation_part = jnp.einsum("tc,dc->td", grad_parts, w_qkv, preferred_element_type=f32)
    expert_rows[-1] = tie(expert_rows[-1], activation_part)
    grad_w_up = sum_of_products(expert_rows, [up for gate, up in grad_pre], 256)
    grad_activation = wires.scatter_plane(activation_part.astype(bf16), grad_w_up)
    own_inverse = input_inverse[:tok_rows]
    grad_input_norm, unused = norm_backward(own_inputs, own_inverse, norm_gain, grad_activation)
    grad_tokens = grad_residual + grad_input_norm

    grad_w_qkv = jnp.einsum("td,tc->dc", activation, grad_parts, preferred_element_type=f32)
    column_sums = lax.psum_scatter(
        grad_w_qkv.astype(bf16)
        .reshape(context_size, expert_size, shard_rows, part_width)
        .transpose(1, 0, 2, 3)
        .reshape(model_width, part_width),
        expert_axes,
        scatter_dimension=0,
        tiled=True,
    ).reshape(context_size, shard_rows, part_width)
    shard_qkv = exchange(column_sums).transpose(1, 0, 2).astype(f32)
    shard_query = shard_qkv[:, :, :query_width].reshape(shard_rows, -1)
    shard_key = shard_qkv[:, :, query_width : query_width + head_size].reshape(shard_rows, -1)
    shard_value = shard_qkv[:, :, query_width + head_size :].reshape(shard_rows, -1)
    router_sums = wires.total(tie(grad_w_router, activation_part))
    shard_router = lax.dynamic_slice_in_dim(
        router_sums,
        (wires.context * expert_size + wires.expert) * shard_rows,
        shard_rows,
        axis=1,
    ).T
    gains = wires.total(
        jnp.concatenate(
            [
                jnp.sum(activation_part * (inputs * input_inverse), axis=0),
                jnp.sum(post_terms, axis=0),
                jnp.sum(query_terms, axis=(0, 1)),
                jnp.sum(key_terms, axis=0),
            ]
        )
    )
    gain_norm, gain_post, gain_query, gain_key = jnp.split(
        gains, [model_width, 2 * model_width, 2 * model_width + head_size]
    )
    return (
        final.astype(bf16)[None],
        grad_tokens[None],
        gain_norm,
        shard_query,
        shard_key,
        shard_value,
        gain_query,
        gain_key,
        shard_out,
        gain_post,
        shard_router,
        grad_w_gate[None],
        grad_w_up[None],
        grad_w_down[None],
    )


def shards(
    tokens,
    span_order,
    expert_ids,
    norm_gain,
    w_query,
    key_projection_weight,
    value_projection_weight,
    query_gain,
    key_gain,
    w_out,
    post_gain,
    w_router,
    w_gate,
    w_up,
    w_down,
    cotangent,
):
    tok_rows = tokens.shape[1]
    model_width = tokens.shape[2]
    head_size = query_gain.shape[0]
    top_count = expert_ids.shape[2]
    query_heads = w_query.shape[1] // head_size
    kv_heads = key_projection_weight.shape[1] // head_size
    query_group_count = query_heads // kv_heads
    context_size = lax.axis_size("context")
    device_count = lax.axis_size(("context", "expert"))
    capacity = max(2, 2 * tok_rows * top_count // device_count)
    seq_len = tok_rows * context_size
    span_rows = tok_rows // 2
    span_count = 2 * context_size
    order_row = span_order[0]
    score_scale = head_size ** (-0.5)
    bf16 = jnp.bfloat16
    f32 = jnp.float32

    def positions(first_row, row_count):
        storage = first_row + jnp.arange(row_count, dtype=jnp.int32)
        select = (storage // span_rows)[:, None] == jnp.arange(span_count, dtype=jnp.int32)[None, :]
        return (
            jnp.sum(jnp.where(select, order_row[None, :], 0), axis=1) * span_rows
            + storage % span_rows
        )

    query_places = positions(lax.axis_index("context") * tok_rows, tok_rows)
    row_places = jnp.tile(query_places, query_group_count)
    gathered = (
        lax.all_gather(w_query, ("context", "expert"), axis=0, tiled=True),
        lax.all_gather(key_projection_weight, ("context", "expert"), axis=0, tiled=True),
        lax.all_gather(value_projection_weight, ("context", "expert"), axis=0, tiled=True),
        lax.all_gather(w_out, ("context", "expert"), axis=0, tiled=True),
        lax.all_gather(w_router, ("context", "expert"), axis=0, tiled=True),
    )
    query_full, key_full, value_full, out_full, router_full = gathered
    inputs = tokens[0].astype(f32)
    normed_in, input_inverse = norm_forward(inputs, norm_gain)
    activation_output = normed_in.astype(bf16)
    query_raw = jnp.dot(activation_output, query_full, preferred_element_type=f32).reshape(
        tok_rows, query_heads, head_size
    )
    key_unrotated = jnp.dot(activation_output, key_full, preferred_element_type=f32).reshape(
        tok_rows, kv_heads, head_size
    )
    value_flat = jnp.dot(activation_output, value_full, preferred_element_type=f32).astype(bf16)
    cosine_table, sine_table = rotary_tables(query_places, head_size)
    query_normed, query_inverse = norm_forward(query_raw, query_gain)
    key_normed, key_inverse = norm_forward(key_unrotated, key_gain)
    query_prepared = rotate(query_normed, cosine_table, sine_table, 1.0).astype(bf16)
    key_flat = (
        rotate(key_normed, cosine_table, sine_table, 1.0)
        .astype(bf16)
        .reshape(tok_rows, kv_heads * head_size)
    )
    query_arr = head_rows(query_prepared, kv_heads, query_group_count)
    row_count_all = query_group_count * tok_rows
    whole_keys, whole_values = (
        lax.all_gather(key_flat, "context", axis=0, tiled=True),
        lax.all_gather(value_flat, "context", axis=0, tiled=True),
    )
    key_block = min(512, seq_len)
    block_count = seq_len // key_block
    key_blocks = whole_keys.reshape(block_count, key_block, kv_heads, head_size)
    value_blocks = whole_values.reshape(block_count, key_block, kv_heads, head_size)
    block_firsts = key_block * jnp.arange(block_count, dtype=jnp.int32)

    def block_scores(keys_now, start_now):
        scores = (
            jnp.einsum("hrd,khd->hrk", query_arr, keys_now, preferred_element_type=f32)
            * score_scale
        )
        visible = (row_places[:, None] >= positions(start_now, key_block)[None, :])[None]
        return (scores, visible)

    def stat_block(state, packed):
        keys_now, start_now = packed
        running_max, running_total = state
        scores, visible = block_scores(keys_now, start_now)
        scores = jnp.where(visible, scores, very_negative)
        new_max = jnp.maximum(running_max, jnp.max(scores, axis=-1))
        weights = jnp.where(visible, jnp.exp(scores - new_max[..., None]), 0.0)
        running_total = running_total * jnp.exp(running_max - new_max) + jnp.sum(weights, axis=-1)
        return ((new_max, running_total), None)

    (att_max, att_total), unused = lax.scan(
        stat_block,
        (
            jnp.full((kv_heads, row_count_all), very_negative, f32),
            jnp.zeros((kv_heads, row_count_all), f32),
        ),
        (key_blocks, block_firsts),
    )
    log_total = att_max + jnp.log(att_total)

    def block_probs(keys_now, start_now):
        scores, visible = block_scores(keys_now, start_now)
        return jnp.where(visible, jnp.exp(scores - log_total[..., None]), 0.0)

    def attend_block(accum, packed):
        keys_now, values_now, start_now = packed
        probs_now = block_probs(keys_now, start_now)
        accum = accum + jnp.einsum(
            "hrk,khd->hrd", probs_now.astype(bf16), values_now, preferred_element_type=f32
        )
        return (accum, None)

    attended_output, unused = lax.scan(
        attend_block,
        jnp.zeros((kv_heads, row_count_all, head_size), f32),
        (key_blocks, value_blocks, block_firsts),
    )
    attn_low = token_rows_of(attended_output, kv_heads, query_group_count, tok_rows).astype(bf16)
    residual = inputs + jnp.dot(attn_low, out_full, preferred_element_type=f32)
    normed_post, post_inverse = norm_forward(residual, post_gain)
    mixed = normed_post.astype(bf16)
    logits = jnp.dot(mixed, router_full, preferred_element_type=f32)
    local_ids = expert_ids[0]
    chooser = (
        local_ids[:, :, None] == jnp.arange(device_count, dtype=jnp.int32)[None, None, :]
    ).astype(f32)
    chosen = jnp.sum(chooser * logits[:, None, :], axis=-1)
    gates = jax.nn.softmax(chosen, axis=-1)
    flat_ids = local_ids.reshape(-1)
    pair_hot = (flat_ids[:, None] == jnp.arange(device_count, dtype=jnp.int32)[None, :]).astype(
        jnp.int32
    )
    ranks = jnp.sum(jnp.cumsum(pair_hot, axis=0) * pair_hot, axis=1) - 1
    slots = flat_ids * capacity + ranks
    pair_rows = jnp.repeat(mixed, top_count, axis=0)
    outgoing = jnp.zeros((device_count * capacity, model_width), bf16).at[slots].set(pair_rows)
    arrived = lax.all_to_all(
        outgoing.reshape(device_count, capacity, model_width),
        ("context", "expert"),
        split_axis=0,
        concat_axis=0,
        tiled=True,
    )
    expert_rows = arrived.reshape(device_count * capacity, model_width)
    gate_pre = jnp.dot(expert_rows, w_gate[0], preferred_element_type=f32)
    up_pre = jnp.dot(expert_rows, w_up[0], preferred_element_type=f32)
    activated = jax.nn.silu(gate_pre)
    hidden = (activated * up_pre).astype(bf16)
    expert_out = jnp.dot(hidden, w_down[0], preferred_element_type=f32).astype(bf16)
    returned = lax.all_to_all(
        expert_out.reshape(device_count, capacity, model_width),
        ("context", "expert"),
        split_axis=0,
        concat_axis=0,
        tiled=True,
    )
    pair_out = (
        returned.reshape(device_count * capacity, model_width)[slots]
        .reshape(tok_rows, top_count, model_width)
        .astype(f32)
    )
    final = residual + jnp.sum(gates[..., None] * pair_out, axis=1)
    again = (
        lax.all_gather(w_query, ("context", "expert"), axis=0, tiled=True),
        lax.all_gather(key_projection_weight, ("context", "expert"), axis=0, tiled=True),
        lax.all_gather(value_projection_weight, ("context", "expert"), axis=0, tiled=True),
        lax.all_gather(w_out, ("context", "expert"), axis=0, tiled=True),
        lax.all_gather(w_router, ("context", "expert"), axis=0, tiled=True),
    )
    query_back, key_back, value_back, out_back, router_back = again
    upstream = cotangent[0].astype(f32)
    grad_gates = jnp.sum(upstream[:, None, :] * pair_out, axis=-1)
    pair_grads = (
        (upstream[:, None, :] * gates[..., None])
        .astype(bf16)
        .reshape(tok_rows * top_count, model_width)
    )
    grad_outgoing = (
        jnp.zeros((device_count * capacity, model_width), bf16).at[slots].set(pair_grads)
    )
    grad_arrived = lax.all_to_all(
        grad_outgoing.reshape(device_count, capacity, model_width),
        ("context", "expert"),
        split_axis=0,
        concat_axis=0,
        tiled=True,
    ).reshape(device_count * capacity, model_width)
    grad_w_down = jnp.einsum("rf,rd->fd", hidden, grad_arrived, preferred_element_type=f32)
    grad_hidden = jnp.einsum("rd,fd->rf", grad_arrived, w_down[0], preferred_element_type=f32)
    sigmoid = jax.nn.sigmoid(gate_pre)
    grad_gate = (grad_hidden * up_pre * sigmoid * (1.0 + gate_pre * (1.0 - sigmoid))).astype(bf16)
    grad_up = (grad_hidden * activated).astype(bf16)
    grad_w_gate = jnp.einsum("rd,rf->df", expert_rows, grad_gate, preferred_element_type=f32)
    grad_w_up = jnp.einsum("rd,rf->df", expert_rows, grad_up, preferred_element_type=f32)
    grad_rows = (
        jnp.einsum("rf,df->rd", grad_gate, w_gate[0], preferred_element_type=f32)
        + jnp.einsum("rf,df->rd", grad_up, w_up[0], preferred_element_type=f32)
    ).astype(bf16)
    grad_back = lax.all_to_all(
        grad_rows.reshape(device_count, capacity, model_width),
        ("context", "expert"),
        split_axis=0,
        concat_axis=0,
        tiled=True,
    )
    grad_mixed = jnp.sum(
        grad_back.reshape(device_count * capacity, model_width)[slots]
        .reshape(tok_rows, top_count, model_width)
        .astype(f32),
        axis=1,
    )
    grad_chosen = gates * (grad_gates - jnp.sum(gates * grad_gates, axis=-1, keepdims=True))
    grad_logits = jnp.sum(chooser * grad_chosen[..., None], axis=1).astype(bf16)
    grad_mixed = grad_mixed + jnp.einsum(
        "te,de->td", grad_logits, router_back, preferred_element_type=f32
    )
    grad_w_router = jnp.einsum("td,te->de", mixed, grad_logits, preferred_element_type=f32)
    grad_resid_norm, post_terms = norm_backward(residual, post_inverse, post_gain, grad_mixed)
    grad_residual = upstream + grad_resid_norm
    resid_low = grad_residual.astype(bf16)
    grad_w_out = jnp.einsum("tc,td->cd", attn_low, resid_low, preferred_element_type=f32)
    grad_attn = jnp.einsum("td,cd->tc", resid_low, out_back, preferred_element_type=f32).astype(
        bf16
    )
    grad_arr = head_rows(
        grad_attn.reshape(tok_rows, query_heads, head_size), kv_heads, query_group_count
    )

    def delta_block(total, packed):
        keys_now, values_now, start_now = packed
        probs_now = block_probs(keys_now, start_now)
        grad_probs = jnp.einsum("hrd,khd->hrk", grad_arr, values_now, preferred_element_type=f32)
        return (total + jnp.sum(probs_now * grad_probs, axis=-1), None)

    delta, unused = lax.scan(
        delta_block,
        jnp.zeros((kv_heads, row_count_all), f32),
        (key_blocks, value_blocks, block_firsts),
    )

    def back_block(grad_query, packed):
        keys_now, values_now, start_now = packed
        probs_now = block_probs(keys_now, start_now)
        grad_probs = jnp.einsum("hrd,khd->hrk", grad_arr, values_now, preferred_element_type=f32)
        grad_scores = (probs_now * (grad_probs - delta[..., None])).astype(bf16)
        grad_query = (
            grad_query
            + jnp.einsum("hrk,khd->hrd", grad_scores, keys_now, preferred_element_type=f32)
            * score_scale
        )
        grad_keys = (
            jnp.einsum("hrk,hrd->khd", grad_scores, query_arr, preferred_element_type=f32)
            * score_scale
        )
        grad_values = jnp.einsum(
            "hrk,hrd->khd", probs_now.astype(bf16), grad_arr, preferred_element_type=f32
        )
        return (
            grad_query,
            jnp.concatenate(
                [grad_keys.reshape(key_block, -1), grad_values.reshape(key_block, -1)], axis=-1
            ),
        )

    grad_query, key_terms = lax.scan(
        back_block,
        jnp.zeros((kv_heads, row_count_all, head_size), f32),
        (key_blocks, value_blocks, block_firsts),
    )
    own_terms = lax.psum_scatter(
        key_terms.reshape(seq_len, 2 * kv_heads * head_size),
        "context",
        scatter_dimension=0,
        tiled=True,
    )
    kv_width = kv_heads * head_size
    grad_key_rot = (
        own_terms[:, :kv_width].astype(bf16).astype(f32).reshape(tok_rows, kv_heads, head_size)
    )
    grad_value_low = own_terms[:, kv_width:].astype(bf16)
    grad_query_rot = token_rows_of(
        grad_query.astype(bf16).astype(f32), kv_heads, query_group_count, tok_rows
    ).reshape(tok_rows, query_heads, head_size)
    grad_query_raw, query_terms = norm_backward(
        query_raw, query_inverse, query_gain, rotate(grad_query_rot, cosine_table, sine_table, -1.0)
    )
    grad_key_raw, key_terms_gain = norm_backward(
        key_unrotated, key_inverse, key_gain, rotate(grad_key_rot, cosine_table, sine_table, -1.0)
    )
    grad_query_low = grad_query_raw.reshape(tok_rows, query_heads * head_size).astype(bf16)
    grad_key_low = grad_key_raw.reshape(tok_rows, kv_width).astype(bf16)
    grad_activation = (
        jnp.einsum("tc,dc->td", grad_query_low, query_back, preferred_element_type=f32)
        + jnp.einsum("tc,dc->td", grad_key_low, key_back, preferred_element_type=f32)
        + jnp.einsum("tc,dc->td", grad_value_low, value_back, preferred_element_type=f32)
    )
    grad_w_query = jnp.einsum(
        "td,tc->dc", activation_output, grad_query_low, preferred_element_type=f32
    )
    grad_w_key = jnp.einsum(
        "td,tc->dc", activation_output, grad_key_low, preferred_element_type=f32
    )
    grad_w_value = jnp.einsum(
        "td,tc->dc", activation_output, grad_value_low, preferred_element_type=f32
    )
    grad_input_norm, input_terms = norm_backward(inputs, input_inverse, norm_gain, grad_activation)
    grad_tokens = grad_residual + grad_input_norm
    shard_query, shard_key, shard_value, shard_out, shard_router = (
        lax.psum_scatter(grad_w_query, ("context", "expert"), scatter_dimension=0, tiled=True),
        lax.psum_scatter(grad_w_key, ("context", "expert"), scatter_dimension=0, tiled=True),
        lax.psum_scatter(grad_w_value, ("context", "expert"), scatter_dimension=0, tiled=True),
        lax.psum_scatter(grad_w_out, ("context", "expert"), scatter_dimension=0, tiled=True),
        lax.psum_scatter(grad_w_router, ("context", "expert"), scatter_dimension=0, tiled=True),
    )
    gain_norm, gain_post, gain_query, gain_key = lax.psum(
        (
            jnp.sum(input_terms, axis=0),
            jnp.sum(post_terms, axis=0),
            jnp.sum(query_terms, axis=(0, 1)),
            jnp.sum(key_terms_gain, axis=(0, 1)),
        ),
        ("context", "expert"),
    )
    return (
        final.astype(bf16)[None],
        grad_tokens[None],
        gain_norm,
        shard_query,
        shard_key,
        shard_value,
        gain_query,
        gain_key,
        shard_out,
        gain_post,
        shard_router,
        grad_w_gate[None],
        grad_w_up[None],
        grad_w_down[None],
    )


def placements(context, expert):
    whole = (*context, *expert)
    rows = P(expert, context, None)
    shard = P(whole, None)
    experts = P(whole, None, None)
    taken = (
        rows,
        P(expert, None),
        rows,
        P(),
        shard,
        shard,
        shard,
        P(),
        P(),
        shard,
        P(),
        shard,
        experts,
        experts,
        experts,
        rows,
    )
    given = (
        rows,
        rows,
        P(),
        shard,
        shard,
        shard,
        P(),
        P(),
        shard,
        P(),
        shard,
        experts,
        experts,
        experts,
    )
    return taken, given


def solution(mesh):
    context_size, expert_size = (mesh.shape["context"], mesh.shape["expert"])

    def step(*arrays):
        key_width, head_size = (arrays[5].shape[1], arrays[7].shape[0])
        own_head = key_width == context_size * head_size
        if own_head and context_size == 4 and expert_size % 2 == 0:
            devices = mesh.devices.reshape(2, 2, expert_size // 2, 2)
            used = Mesh(devices, both)
            taken, given = placements(context_axes, expert_axes)
            body = grouped
        else:
            used, body = (mesh, shards)
            taken, given = placements(("context",), ("expert",))
        return jax.shard_map(
            body, mesh=used, in_specs=taken, out_specs=given, check_vma=False
        )(*arrays)

    return step
```

```python
import jax
import jax.numpy as jnp
from jax import lax
from jax.experimental import pallas as pl
from jax.experimental.pallas import tpu as pltpu
from jax.sharding import Mesh
from jax.sharding import PartitionSpec as P

epsilon = 1e-06
rotary_base = 1000000.0
very_negative = -1e30


def norm_forward(values, scale_gain):
    inverse = lax.rsqrt(jnp.mean(values * values, axis=-1, keepdims=True) + epsilon)
    return (values * inverse * scale_gain, inverse)


def norm_backward(values, inverse, scale_gain, upstream):
    normed = values * inverse
    weighted = upstream * scale_gain
    inner = jnp.mean(weighted * normed, axis=-1, keepdims=True)
    return (inverse * (weighted - normed * inner), upstream * normed)


def rotary_tables(token_positions, head_width):
    half_width = head_width // 2
    frequency = rotary_base ** (-jnp.arange(half_width, dtype=jnp.float32) * 2.0 / head_width)
    angles = token_positions.astype(jnp.float32)[:, None] * frequency[None, :]
    return (jnp.cos(angles)[:, None, :], jnp.sin(angles)[:, None, :])


def rotate(values, cosine_table, sine_table, direction):
    half_width = values.shape[-1] // 2
    first_half = values[..., :half_width]
    second_half = values[..., half_width:]
    return jnp.concatenate(
        [
            first_half * cosine_table - direction * second_half * sine_table,
            second_half * cosine_table + direction * first_half * sine_table,
        ],
        axis=-1,
    )


def head_rows(array_in, kv_heads, query_group_count):
    row_total = array_in.shape[0]
    return (
        array_in.reshape(row_total, kv_heads, query_group_count, -1)
        .transpose(1, 2, 0, 3)
        .reshape(kv_heads, query_group_count * row_total, -1)
    )


def token_rows_of(array_in, kv_heads, query_group_count, tok_rows):
    return (
        array_in.reshape(kv_heads, query_group_count, tok_rows, -1)
        .transpose(2, 0, 1, 3)
        .reshape(tok_rows, -1)
    )


def dense_ranks(mask):
    width = mask.shape[-1]
    before = (
        jnp.arange(width, dtype=jnp.int32)[:, None] < jnp.arange(width, dtype=jnp.int32)[None, :]
    )
    return jnp.dot(
        mask.astype(jnp.bfloat16), before.astype(jnp.bfloat16), preferred_element_type=jnp.float32
    ).astype(jnp.int32)


context_axes = ("y", "x")
expert_axes = ("z", "core")
plane_axes = ("y", "x", "core")
both = context_axes + expert_axes
bf16 = jnp.bfloat16
f32 = jnp.float32


class Wires:
    def __init__(self, expert_size):
        self.layers = expert_size // 2
        self.context = lax.axis_index(context_axes)
        self.expert = lax.axis_index(expert_axes)
        self.core = self.expert % 2
        self.layer = self.expert // 2

    def pairs(self, move):
        found = []
        for y in range(2):
            for x in range(2):
                for z in range(self.layers):
                    for core in range(2):
                        there = move(y, x, z, core)
                        found.append((self.number(y, x, z, core), self.number(*there)))
        return found

    def number(self, y, x, z, core):
        return ((y * 2 + x) * self.layers + z) * 2 + core

    def send(self, value, move):
        return lax.ppermute(value, both, self.pairs(move))

    def swap(self, value):
        return self.send(value, lambda y, x, z, core: (y, x, z, 1 - core))

    def first(self, value):
        return self.send(
            value, lambda y, x, z, core: (y, 1 - x, z, core) if core else (1 - y, x, z, core)
        )

    def second(self, value):
        return self.send(
            value, lambda y, x, z, core: (1 - y, x, z, core) if core else (y, 1 - x, z, core)
        )

    def along(self, value, flip_y, flip_x):
        return self.send(value, lambda y, x, z, core: (y ^ flip_y, x ^ flip_x, z, core))

    def layer_flip(self, value, bit):
        return self.send(value, lambda y, x, z, core: (y, x, z ^ bit, core))

    def from_layer(self, value, step):
        return self.send(value, lambda y, x, z, core: (y, x, (z - step) % self.layers, core))

    def to_layer(self, value, step):
        return self.send(value, lambda y, x, z, core: (y, x, (z + step) % self.layers, core))

    def contexts(self, core):
        index = jnp.arange(4, dtype=jnp.int32)
        one, two = (index // 2, index % 2)
        swapped = two * 2 + one
        return self.context ^ jnp.where(core == 0, index, swapped)

    def blocks(self):
        found = []
        for step in range(self.layers):
            for flip in range(2):
                core = self.core ^ flip
                layer = (self.layer + step) % self.layers
                found.append(self.contexts(core) * (2 * self.layers) + layer * 2 + core)
        return jnp.concatenate(found)

    def gather_plane(self, value):
        crossed = self.second(value)
        return jnp.concatenate(
            [value, crossed, self.first(value), self.first(crossed)], axis=0
        )

    def scatter_plane(self, value, *after):
        half = value.shape[0] // 2
        quarter = half // 2
        there = self.first(value[half:])
        mine = tie(add_low(value[quarter:half], there[quarter:]), *after)
        kept = add_low(value[:quarter], there[:quarter])
        return kept.astype(f32) + self.second(mine).astype(f32)

    def turns(self):
        others = sorted(range(1, self.layers), key=lambda step: -min(step, self.layers - step))
        return [0] + others

    def layers_of(self, value, *after):
        found = [value]
        for turn, step in enumerate(self.turns()[1:]):
            start = tie(value, *found[-1:], *(after if turn > 0 else ()))
            found.append(self.from_layer(start, step))
        return found

    def total(self, value):
        value = value + self.swap(value)
        value = value + self.along(value, 1, 0)
        value = value + self.along(value, 0, 1)
        bit = 1
        while bit < self.layers:
            value = value + self.layer_flip(value, bit)
            bit *= 2
        return value


def add_low(one, two):
    return (one.astype(f32) + two.astype(f32)).astype(bf16)


def tie(value, *after):
    return lax.optimization_barrier((value, *after))[0]


def sum_of_products(lefts, rights, tile):
    rows, height = lefts[0].shape
    width = rights[0].shape[1]
    parts = len(lefts)

    def body(*refs):
        total = None
        for left, right in zip(refs[:parts], refs[parts : 2 * parts]):
            term = lax.dot_general(
                left[...], right[...], (((0,), (0,)), ((), ())), preferred_element_type=f32
            )
            total = term if total is None else total + term
        refs[2 * parts][...] = total

    return pl.pallas_call(
        body,
        grid=(height // tile,),
        in_specs=[pl.BlockSpec((rows, tile), lambda i: (0, i))] * parts
        + [pl.BlockSpec((rows, width), lambda i: (0, 0))] * parts,
        out_specs=pl.BlockSpec((tile, width), lambda i: (i, 0)),
        out_shape=jax.ShapeDtypeStruct((height, width), f32),
        cost_estimate=pl.CostEstimate(
            flops=2 * parts * rows * height * width,
            bytes_accessed=2 * parts * rows * (height + width) + 4 * height * width,
            transcendentals=0,
        ),
        name="sum_of_products",
    )(*lefts, *rights)


def estimate(flops, moved):
    return pl.CostEstimate(flops=flops, bytes_accessed=moved, transcendentals=0)


def fixed(shape):
    return pl.BlockSpec(shape, lambda *i: (0,) * len(shape))


def add_pairs(nears, fars):
    count, (rows, width) = (len(nears), nears[0].shape)
    slab = rows // 2

    def body(*refs):
        for place in range(count):
            refs[-1][place] = add_low(refs[place][...], refs[count + place][...])

    return pl.pallas_call(
        body,
        grid=(rows // slab,),
        in_specs=[pl.BlockSpec((slab, width), lambda i: (i, 0))] * (2 * count),
        out_specs=pl.BlockSpec((count, slab, width), lambda i: (0, i, 0)),
        out_shape=jax.ShapeDtypeStruct((count, rows, width), bf16),
        cost_estimate=estimate(count * rows * width, 6 * count * rows * width),
        name="add_pairs",
    )(*nears, *fars).reshape(count * rows, width)


def pull_step(places, picks, tables, w_down):
    blocks, capacity, halves = picks.shape
    width, tile = (w_down.shape[2], 256)
    rows, hidden_width = (blocks * capacity, w_down.shape[1])

    def body(places_ref, picks_ref, *refs):
        down_ref, rows_ref, pulled_ref = refs[blocks:]

        @pl.when(pl.program_id(0) == 0)
        def _():
            for block in range(blocks):
                rows_ref[pl.ds(block * capacity, capacity), :] = jnp.dot(
                    picks_ref[block], refs[block][0], preferred_element_type=f32
                ).astype(bf16)

        pulled_ref[...] = lax.dot_general(
            rows_ref[...], down_ref[0], (((1,), (1,)), ((), ())), preferred_element_type=f32
        )

    def piece(block):
        return pl.BlockSpec((1, halves, width), lambda i, places_ref: (places_ref[block], 0, 0))

    return pl.pallas_call(
        body,
        grid_spec=pltpu.PrefetchScalarGridSpec(
            num_scalar_prefetch=1,
            grid=(hidden_width // tile,),
            in_specs=[fixed(picks.shape)]
            + [piece(block) for block in range(blocks)]
            + [pl.BlockSpec((1, tile, width), lambda i, places_ref: (0, i, 0))],
            out_specs=[
                fixed((rows, width)),
                pl.BlockSpec((rows, tile), lambda i, places_ref: (0, i)),
            ],
        ),
        out_shape=[
            jax.ShapeDtypeStruct((rows, width), bf16),
            jax.ShapeDtypeStruct((rows, hidden_width), f32),
        ],
        cost_estimate=estimate(2 * rows * width * (hidden_width + 2 * halves), 4 * rows * width),
        name="pull_step",
    )(places, picks, *tables, w_down)


def expert_step(picks, pieces, gate, pulled, w_gate, w_up, w_down, joined):
    blocks, capacity, halves = picks.shape
    width, tile, slab = (w_gate.shape[1], 256, 32)
    rows, hidden_width = (blocks * capacity, w_gate.shape[2])
    count = hidden_width // tile

    wide = 512
    tail = width // wide

    def body(picks_ref, *refs):
        gate_ref, pulled_ref, w_gate_ref, w_up_ref = refs[blocks : blocks + 4]
        gate_back_ref, up_back_ref, down_ref = refs[blocks + 4 : blocks + 7]
        rows_ref, weighted_ref, grad_gate_ref, grad_up_ref, dots_ref = refs[
            blocks + 7 : blocks + 12
        ]
        back_refs, (pre_ref, up_ref) = (refs[blocks + 12 : -2], refs[-2:])
        turn = pl.program_id(0)

        @pl.when(turn == 0)
        def _():
            dots_ref[...] = jnp.zeros_like(dots_ref)
            for block in range(blocks):
                rows_ref[pl.ds(block * capacity, capacity), :] = jnp.dot(
                    picks_ref[block], refs[block][...], preferred_element_type=f32
                ).astype(bf16)

        @pl.when(turn < count)
        def _():
            pre_ref[...] = jnp.dot(rows_ref[...], w_gate_ref[0], preferred_element_type=f32)
            up_ref[...] = jnp.dot(rows_ref[...], w_up_ref[0], preferred_element_type=f32)
            columns = pl.ds(pl.multiple_of(turn * tile, tile), tile)

            @pl.loop(0, rows // slab)
            def _(place):
                at = pl.ds(pl.multiple_of(place * slab, slab), slab)
                pre, up, gates, pull = (
                    pre_ref[at, :],
                    up_ref[at, :],
                    gate_ref[at, :],
                    pulled_ref[at, :],
                )
                sigmoid = jax.nn.sigmoid(pre)
                activated = pre * sigmoid
                hidden = activated * up
                dots_ref[at, :] += jnp.sum(hidden * pull, axis=1, keepdims=True)
                weighted_ref[at, columns] = (gates * hidden).astype(bf16)
                grad_hidden = gates * pull
                grad_gate_ref[at, columns] = (
                    grad_hidden * up * sigmoid * (1.0 + pre * (1.0 - sigmoid))
                ).astype(bf16)
                grad_up_ref[at, columns] = (grad_hidden * activated).astype(bf16)

        @pl.when(turn >= count)
        def _():
            across = (((1,), (1,)), ((), ()))
            pair = lax.dot_general(
                grad_gate_ref[...], gate_back_ref[0], across, preferred_element_type=f32
            ) + lax.dot_general(
                grad_up_ref[...], up_back_ref[0], across, preferred_element_type=f32
            )
            out = jnp.dot(weighted_ref[...], down_ref[0], preferred_element_type=f32)
            for side, table in enumerate((pair.astype(bf16), out.astype(bf16))):
                for block in range(blocks):
                    found = lax.dot_general(
                        picks_ref[block],
                        table[block * capacity : (block + 1) * capacity],
                        (((0,), (0,)), ((), ())),
                        preferred_element_type=f32,
                    ).astype(bf16)
                    if joined:
                        back_refs[block][pl.ds(side * halves, halves), :] = found
                    else:
                        back_refs[side * blocks + block][...] = found

    def ahead(i):
        return jnp.minimum(i, count - 1)

    def behind(i):
        return jnp.maximum(i - count, 0)

    weights = pl.BlockSpec((1, width, tile), lambda i: (0, 0, ahead(i)))
    weights_back = pl.BlockSpec((1, wide, hidden_width), lambda i: (0, behind(i), 0))
    narrow = jax.ShapeDtypeStruct((rows, hidden_width), bf16)
    back = [((2 if joined else 1) * halves, width)] * (blocks if joined else 2 * blocks)
    found = pl.pallas_call(
        body,
        grid=(count + tail,),
        in_specs=[fixed(picks.shape)]
        + [fixed((halves, width))] * blocks
        + [
            fixed((rows, 1)),
            pl.BlockSpec((rows, tile), lambda i: (0, ahead(i))),
            weights,
            weights,
            weights_back,
            weights_back,
            pl.BlockSpec((1, hidden_width, wide), lambda i: (0, 0, behind(i))),
        ],
        out_specs=[fixed((rows, width))]
        + [fixed((rows, hidden_width))] * 3
        + [fixed((rows, 1))]
        + [pl.BlockSpec((shape[0], wide), lambda i: (0, behind(i))) for shape in back],
        out_shape=[
            jax.ShapeDtypeStruct((rows, width), bf16),
            narrow,
            narrow,
            narrow,
            jax.ShapeDtypeStruct((rows, 1), f32),
        ]
        + [jax.ShapeDtypeStruct(shape, bf16) for shape in back],
        scratch_shapes=[pltpu.VMEM((rows, tile), f32), pltpu.VMEM((rows, tile), f32)],
        cost_estimate=estimate(10 * rows * width * hidden_width, 24 * rows * width),
        name="expert_step",
    )(picks, *pieces, gate, pulled, w_gate, w_up, w_gate, w_up, w_down)
    return (*found[:5], list(found[5:]))


def grouped(
    tokens,
    span_order,
    expert_ids,
    norm_gain,
    w_query,
    key_projection_weight,
    value_projection_weight,
    query_gain,
    key_gain,
    w_out,
    post_gain,
    w_router,
    w_gate,
    w_up,
    w_down,
    cotangent,
):
    tok_rows = tokens.shape[1]
    model_width = tokens.shape[2]
    head_size = query_gain.shape[0]
    top_count = expert_ids.shape[2]
    query_heads = w_query.shape[1] // head_size
    kv_heads = key_projection_weight.shape[1] // head_size
    group = query_heads // kv_heads
    context_size = lax.axis_size(context_axes)
    expert_size = lax.axis_size(expert_axes)
    device_count = context_size * expert_size
    wires = Wires(expert_size)
    layers = wires.layers
    chain = wires.turns()
    capacity = 2 * tok_rows * top_count // device_count
    seq_len = tok_rows * context_size
    span_rows = tok_rows // 2
    span_count = 2 * context_size
    order_row = span_order[0]
    score_scale = head_size ** (-0.5)
    shard_rows = w_query.shape[0]
    query_width = group * head_size
    part_width = query_width + 2 * head_size
    hidden_width = w_gate.shape[2]

    seq_tokens = wires.gather_plane(tokens[0])
    storage = (
        wires.contexts(wires.core)[:, None] * tok_rows
        + jnp.arange(tok_rows, dtype=jnp.int32)[None, :]
    ).reshape(-1)
    select = (storage // span_rows)[:, None] == jnp.arange(span_count, dtype=jnp.int32)[None, :]
    places = (
        jnp.sum(jnp.where(select, order_row[None, :], 0), axis=1) * span_rows + storage % span_rows
    )

    packed = jnp.concatenate(
        [
            w_query.reshape(shard_rows, context_size, query_width),
            key_projection_weight.reshape(shard_rows, context_size, head_size),
            value_projection_weight.reshape(shard_rows, context_size, head_size),
        ],
        axis=2,
    ).transpose(1, 0, 2)
    flips = wires.context ^ jnp.arange(context_size, dtype=jnp.int32)

    def exchange(parts):
        facing = jnp.take(parts, flips, axis=0)
        got = [facing[0]] + [
            wires.along(facing[flip], flip // 2, flip % 2) for flip in range(1, context_size)
        ]
        return jnp.take(jnp.stack(got), flips, axis=0)

    columns = exchange(packed)
    every_column = lax.all_gather(columns, expert_axes, axis=0, tiled=False)
    order = wires.blocks()
    chooser = (
        expert_ids[0][:, :, None] == jnp.arange(device_count, dtype=jnp.int32)[None, None, :]
    ).astype(f32)
    small = lax.all_to_all(
        jnp.concatenate(
            [
                jnp.sum(chooser, axis=1).T.astype(bf16),
                jnp.broadcast_to(w_router.reshape(1, -1), (device_count, w_router.size)),
            ],
            axis=1,
        ),
        both,
        split_axis=0,
        concat_axis=0,
        tiled=True,
    )
    router_full = small[:, tok_rows:].reshape(model_width, device_count)
    mine = jnp.take(small[:, :tok_rows], order, axis=0) > 0.5
    slot_of = dense_ranks(mine)
    picks_true = (
        slot_of[:, None, :] == jnp.arange(capacity, dtype=jnp.int32)[None, :, None]
    ) & mine[:, None, :]
    picks = picks_true.astype(bf16)
    picks_by = picks.reshape(layers, 8, capacity, tok_rows)
    count = layers

    class Plane:
        def __init__(self, column):
            self.near = [column]
            self.far = []

        def cross(self, *after):
            self.near.append(wires.second(tie(self.near[0], *after)))

        def finish(self, *after):
            self.near += [wires.first(tie(part, *after)) for part in self.near[:2]]

        def swap(self):
            self.far = [wires.swap(part) for part in self.near]

    def pull(turn, *after):
        step = chain[turn]
        if step == 0:
            plane = grad_planes[0]
            tables = [part[None] for part in plane.near + plane.far]
            places = 0 * order[:8]
        else:
            tables = [all_grads] * 8
            places = order[step * 8 : step * 8 + 8]
        found = pull_step(places, tie(picks_by[step], *after), tables, w_down)
        grad_rows[turn], pulled[turn] = found

    picks_by = tie(picks_by, router_full, seq_tokens)
    pulled, grad_rows = ([None] * count, [None] * count)
    grad_planes = {0: Plane(cotangent[0])}
    grad_planes[0].cross()
    grad_planes[0].finish()
    grad_planes[0].swap()
    pull(0)
    out_rows = lax.all_gather(tie(w_out, pulled[0]), expert_axes, axis=0, tiled=True)
    inputs = seq_tokens.astype(f32)
    normed_in, input_inverse = norm_forward(inputs, norm_gain)
    activation = normed_in.astype(bf16)
    every_column = tie(every_column, activation, pulled[0])
    w_qkv = every_column.transpose(1, 0, 2, 3).reshape(model_width, part_width)
    projected = jnp.dot(activation, w_qkv, preferred_element_type=f32)
    query_raw = projected[:, :query_width].reshape(seq_len, group, head_size).transpose(1, 0, 2)
    key_raw = projected[:, query_width : query_width + head_size]
    values = projected[:, query_width + head_size :].astype(bf16)
    cosine_table, sine_table = rotary_tables(places, head_size)
    cosine_table, sine_table = (cosine_table[:, 0], sine_table[:, 0])
    query_normed, query_inverse = norm_forward(query_raw, query_gain)
    key_normed, key_inverse = norm_forward(key_raw, key_gain)
    queries = rotate(query_normed, cosine_table, sine_table, 1.0).astype(bf16)
    keys = rotate(key_normed, cosine_table, sine_table, 1.0).astype(bf16)
    all_grads = lax.all_gather(tie(cotangent[0], queries), both, axis=0, tiled=False)
    visible = (places[:, None] >= places[None, :])[None]
    scores = jnp.einsum("htd,kd->htk", queries, keys, preferred_element_type=f32) * score_scale
    scores = jnp.where(visible, scores, very_negative)
    peak = jnp.max(scores, axis=-1, keepdims=True)
    weights = jnp.exp(scores - peak)
    probs = weights / jnp.sum(weights, axis=-1, keepdims=True)
    probs_low = probs.astype(bf16)
    attended = jnp.einsum("htk,kd->htd", probs_low, values, preferred_element_type=f32)
    attn_low = attended.astype(bf16).transpose(1, 0, 2).reshape(seq_len, query_width)
    out_part = jnp.dot(attn_low, out_rows, preferred_element_type=f32).astype(bf16)
    own_inputs = tokens[0].astype(f32)
    residual = own_inputs + wires.scatter_plane(out_part)
    normed_post, post_inverse = norm_forward(residual, post_gain)
    mixed = normed_post.astype(bf16)
    logits = jnp.dot(mixed, router_full, preferred_element_type=f32)
    chosen = jnp.sum(chooser * logits[:, None, :], axis=-1)
    gates = jax.nn.softmax(chosen, axis=-1)
    gates_dense = jnp.sum(chooser * gates[..., None], axis=1)
    gates_mine = lax.all_to_all(gates_dense.T, both, split_axis=0, concat_axis=0, tiled=True)
    mixed_columns = wires.layers_of(mixed)
    planes = [Plane(column) for column in mixed_columns]
    planes[0].cross()
    planes[0].finish()
    planes[0].swap()
    gates_mine = tie(gates_mine, *planes[0].near)
    gates_mine = jnp.take(gates_mine, order, axis=0)
    gate_rows = jnp.sum(jnp.where(picks_true, gates_mine[:, None, :], 0.0), axis=-1)
    gate_by = gate_rows.reshape(layers, 8 * capacity, 1)

    class Back:
        def __init__(self, step, parts):
            self.step, self.near = (step, parts[:4])
            self.swapped = [wires.swap(part) for part in parts[4:]]

        def first(self, *after):
            self.leaving = [add_pairs(self.near[2:], self.swapped[2:])]
            self.halved = [wires.first(tie(self.leaving[0], *after))]

        def second(self, *after):
            half = self.halved[0].reshape(2, *self.near[0].shape)
            self.kept = [
                (
                    self.near[part].astype(f32)
                    + self.swapped[part].astype(f32)
                    + half[part].astype(f32)
                ).astype(bf16)
                for part in (0, 1)
            ]
            self.crossed = wires.second(tie(self.kept[1], *after))

        def send(self, own):
            return own if self.step == 0 else wires.to_layer(own, self.step)

        def layer(self, *after):
            own = add_low(self.kept[0], self.crossed)
            self.sum = self.send(tie(own[:tok_rows], *after))
            self.rest = own[tok_rows:]

    expert_rows, weighted, grad_pre, grad_gate_rows, backs = ([], [], [], [], [])
    out_parts = []
    if count > 1:
        planes[1].cross()
    for turn, step in enumerate(chain):
        last = turn == count - 1
        waits = []
        if 0 < turn and not last:
            waits += planes[turn + 1].near[1:]
        if 0 < turn and last:
            waits += backs[turn - 1].swapped
        if turn > 1:
            waits += backs[turn - 2].halved
            backs[turn - 2].second()
        if turn > 2:
            waits.append(backs[turn - 3].crossed)
            backs[turn - 3].layer()
        if turn > 1 and last:
            waits.append(backs[turn - 2].crossed)
            backs[turn - 2].layer()
        pieces = planes[turn].near + planes[turn].far
        found = expert_step(
            picks_by[step],
            [tie(pieces[0], *waits)] + pieces[1:],
            gate_by[step],
            pulled[turn],
            w_gate,
            w_up,
            w_down,
            turn + 2 < count,
        )
        if not last:
            pull(turn + 1, found[0])
        expert_rows.append(found[0])
        weighted.append(found[1])
        grad_pre.append(found[2:4])
        grad_gate_rows.append(found[4])
        backs.append(Back(step, found[5][:8]))
        if turn + 2 >= count:
            out_parts.append(found[5][8:])
        if not last:
            planes[turn + 1].finish()
            planes[turn + 1].swap()
            if turn + 2 < count:
                planes[turn + 2].cross(found[0])
            waits = list(planes[turn + 1].near[2:])
        if turn > 0:
            backs[turn - 1].first()
        if not last:
            planes[turn + 1].near[0] = tie(planes[turn + 1].near[0], *waits)

    backs[-1].first()
    if count > 1:
        backs[-2].swapped[0] = tie(backs[-2].swapped[0], *backs[-1].leaving)
        backs[-2].second()
    backs[-1].second()
    grad_gate_rows[-1] = tie(grad_gate_rows[-1], *backs[-1].halved)
    by_step = dict(zip(chain, grad_gate_rows))
    grad_gate_all = jnp.concatenate([by_step[step] for step in range(layers)]).reshape(
        device_count, capacity
    )
    grad_gates_back = jnp.sum(jnp.where(picks_true, grad_gate_all[..., None], 0.0), axis=1)
    numbers = jnp.arange(device_count, dtype=jnp.int32)
    inverse = jnp.sum(jnp.where(order[:, None] == numbers[None, :], numbers[:, None], 0), axis=0)
    grad_gates_back = jnp.take(grad_gates_back, inverse, axis=0)
    grad_gates_dense = lax.all_to_all(
        grad_gates_back, both, split_axis=0, concat_axis=0, tiled=True
    ).T

    weighted[-1] = tie(weighted[-1], *backs[-1].halved)
    grad_w_down = sum_of_products(weighted, grad_rows, 256)
    for turn, back in enumerate(backs):
        if not hasattr(back, "sum"):
            if turn < count - 1:
                back.layer()
            else:
                own = tie(add_low(back.kept[0], back.crossed), grad_w_down)
                back.sum = back.send(own)
    grad_mixed = sum(back.sum.astype(f32) for back in backs)
    rest = [back.rest for back in backs[:-2]]
    out_backs = []
    for back, parts in zip(backs[-2:], out_parts):
        parts[4] = tie(parts[4], *backs[-1].swapped)
        out_backs.append(Back(back.step, parts))

    def send_late(turn):
        if turn < count - 2:
            rest[turn] = backs[turn].send(tie(rest[turn], grad_residual))
        return rest[turn : turn + 1]

    upstream = cotangent[0].astype(f32)
    grad_gates = jnp.sum(chooser * grad_gates_dense[:, None, :], axis=-1)
    grad_chosen = gates * (grad_gates - jnp.sum(gates * grad_gates, axis=-1, keepdims=True))
    grad_logits = jnp.sum(chooser * grad_chosen[..., None], axis=1).astype(bf16)
    grad_mixed = grad_mixed + jnp.einsum(
        "te,de->td", grad_logits, router_full, preferred_element_type=f32
    )
    grad_w_router = jnp.einsum("td,te->ed", mixed, grad_logits, preferred_element_type=f32)
    grad_resid_norm, post_terms = norm_backward(residual, post_inverse, post_gain, grad_mixed)
    grad_residual = upstream + grad_resid_norm
    expert_rows[-1] = tie(expert_rows[-1], grad_residual)
    grad_w_gate = sum_of_products(expert_rows, [gate for gate, up in grad_pre], 256)
    resid_low = tie(wires.gather_plane(grad_residual.astype(bf16)), grad_w_gate)
    for turn, out_back in enumerate(out_backs):
        resid_low = tie(resid_low, *out_back.swapped, *send_late(turn))
        out_back.swapped[0] = tie(out_back.swapped[0], grad_residual)
        out_back.first()

    grad_w_out = jnp.einsum(
        "tc,td->cd", attn_low, resid_low, preferred_element_type=f32
    ).astype(bf16)
    shard_out = lax.psum_scatter(
        grad_w_out, expert_axes, scatter_dimension=0, tiled=True
    ).astype(f32)
    grad_attn = (
        jnp.einsum("td,cd->tc", resid_low, out_rows, preferred_element_type=f32)
        .astype(bf16)
        .reshape(seq_len, group, head_size)
        .transpose(1, 0, 2)
    )
    grad_probs = jnp.einsum("htd,kd->htk", grad_attn, values, preferred_element_type=f32)
    delta = jnp.sum(probs * grad_probs, axis=-1, keepdims=True)
    delta = tie(delta, grad_w_out, *[back.halved[0] for back in out_backs])
    for out_back in out_backs:
        out_back.second()
    grad_scores = (probs * (grad_probs - delta)).astype(bf16)
    grad_query = (
        jnp.einsum("htk,kd->htd", grad_scores, keys, preferred_element_type=f32) * score_scale
    ).astype(bf16)
    grad_key = (
        jnp.einsum("htk,htd->kd", grad_scores, queries, preferred_element_type=f32) * score_scale
    ).astype(bf16)
    grad_value = jnp.einsum(
        "htk,htd->kd", probs_low, grad_attn, preferred_element_type=f32
    ).astype(bf16)
    out_sums = []
    for out_back in out_backs:
        grad_query = tie(grad_query, out_back.crossed)
        out_sums.append(out_back.send(add_low(out_back.kept[0], out_back.crossed)))
    grad_query_raw, query_terms = norm_backward(
        query_raw,
        query_inverse,
        query_gain,
        rotate(grad_query.astype(f32), cosine_table, sine_table, -1.0),
    )
    grad_key_raw, key_terms = norm_backward(
        key_raw, key_inverse, key_gain, rotate(grad_key.astype(f32), cosine_table, sine_table, -1.0)
    )
    grad_parts = jnp.concatenate(
        [
            grad_query_raw.astype(bf16).transpose(1, 0, 2).reshape(seq_len, query_width),
            grad_key_raw.astype(bf16),
            grad_value,
        ],
        axis=1,
    )
    grad_parts = tie(grad_parts, *out_sums, shard_out)
    final = residual + sum(part.astype(f32) for part in out_sums + rest)
    activation_part = jnp.einsum("tc,dc->td", grad_parts, w_qkv, preferred_element_type=f32)
    expert_rows[-1] = tie(expert_rows[-1], activation_part)
    grad_w_up = sum_of_products(expert_rows, [up for gate, up in grad_pre], 256)
    grad_activation = wires.scatter_plane(activation_part.astype(bf16), grad_w_up)
    own_inverse = input_inverse[:tok_rows]
    grad_input_norm, unused = norm_backward(own_inputs, own_inverse, norm_gain, grad_activation)
    grad_tokens = grad_residual + grad_input_norm

    grad_w_qkv = jnp.einsum("td,tc->dc", activation, grad_parts, preferred_element_type=f32)
    column_sums = lax.psum_scatter(
        grad_w_qkv.astype(bf16)
        .reshape(context_size, expert_size, shard_rows, part_width)
        .transpose(1, 0, 2, 3)
        .reshape(model_width, part_width),
        expert_axes,
        scatter_dimension=0,
        tiled=True,
    ).reshape(context_size, shard_rows, part_width)
    shard_qkv = exchange(column_sums).transpose(1, 0, 2).astype(f32)
    shard_query = shard_qkv[:, :, :query_width].reshape(shard_rows, -1)
    shard_key = shard_qkv[:, :, query_width : query_width + head_size].reshape(shard_rows, -1)
    shard_value = shard_qkv[:, :, query_width + head_size :].reshape(shard_rows, -1)
    router_sums = wires.total(tie(grad_w_router, activation_part))
    shard_router = lax.dynamic_slice_in_dim(
        router_sums,
        (wires.context * expert_size + wires.expert) * shard_rows,
        shard_rows,
        axis=1,
    ).T
    gains = wires.total(
        jnp.concatenate(
            [
                jnp.sum(activation_part * (inputs * input_inverse), axis=0),
                jnp.sum(post_terms, axis=0),
                jnp.sum(query_terms, axis=(0, 1)),
                jnp.sum(key_terms, axis=0),
            ]
        )
    )
    gain_norm, gain_post, gain_query, gain_key = jnp.split(
        gains, [model_width, 2 * model_width, 2 * model_width + head_size]
    )
    return (
        final.astype(bf16)[None],
        grad_tokens[None],
        gain_norm,
        shard_query,
        shard_key,
        shard_value,
        gain_query,
        gain_key,
        shard_out,
        gain_post,
        shard_router,
        grad_w_gate[None],
        grad_w_up[None],
        grad_w_down[None],
    )


def shards(
    tokens,
    span_order,
    expert_ids,
    norm_gain,
    w_query,
    key_projection_weight,
    value_projection_weight,
    query_gain,
    key_gain,
    w_out,
    post_gain,
    w_router,
    w_gate,
    w_up,
    w_down,
    cotangent,
):
    tok_rows = tokens.shape[1]
    model_width = tokens.shape[2]
    head_size = query_gain.shape[0]
    top_count = expert_ids.shape[2]
    query_heads = w_query.shape[1] // head_size
    kv_heads = key_projection_weight.shape[1] // head_size
    query_group_count = query_heads // kv_heads
    context_size = lax.axis_size("context")
    device_count = lax.axis_size(("context", "expert"))
    capacity = max(2, 2 * tok_rows * top_count // device_count)
    seq_len = tok_rows * context_size
    span_rows = tok_rows // 2
    span_count = 2 * context_size
    order_row = span_order[0]
    score_scale = head_size ** (-0.5)
    bf16 = jnp.bfloat16
    f32 = jnp.float32

    def positions(first_row, row_count):
        storage = first_row + jnp.arange(row_count, dtype=jnp.int32)
        select = (storage // span_rows)[:, None] == jnp.arange(span_count, dtype=jnp.int32)[None, :]
        return (
            jnp.sum(jnp.where(select, order_row[None, :], 0), axis=1) * span_rows
            + storage % span_rows
        )

    query_places = positions(lax.axis_index("context") * tok_rows, tok_rows)
    row_places = jnp.tile(query_places, query_group_count)
    gathered = (
        lax.all_gather(w_query, ("context", "expert"), axis=0, tiled=True),
        lax.all_gather(key_projection_weight, ("context", "expert"), axis=0, tiled=True),
        lax.all_gather(value_projection_weight, ("context", "expert"), axis=0, tiled=True),
        lax.all_gather(w_out, ("context", "expert"), axis=0, tiled=True),
        lax.all_gather(w_router, ("context", "expert"), axis=0, tiled=True),
    )
    query_full, key_full, value_full, out_full, router_full = gathered
    inputs = tokens[0].astype(f32)
    normed_in, input_inverse = norm_forward(inputs, norm_gain)
    activation_output = normed_in.astype(bf16)
    query_raw = jnp.dot(activation_output, query_full, preferred_element_type=f32).reshape(
        tok_rows, query_heads, head_size
    )
    key_unrotated = jnp.dot(activation_output, key_full, preferred_element_type=f32).reshape(
        tok_rows, kv_heads, head_size
    )
    value_flat = jnp.dot(activation_output, value_full, preferred_element_type=f32).astype(bf16)
    cosine_table, sine_table = rotary_tables(query_places, head_size)
    query_normed, query_inverse = norm_forward(query_raw, query_gain)
    key_normed, key_inverse = norm_forward(key_unrotated, key_gain)
    query_prepared = rotate(query_normed, cosine_table, sine_table, 1.0).astype(bf16)
    key_flat = (
        rotate(key_normed, cosine_table, sine_table, 1.0)
        .astype(bf16)
        .reshape(tok_rows, kv_heads * head_size)
    )
    query_arr = head_rows(query_prepared, kv_heads, query_group_count)
    row_count_all = query_group_count * tok_rows
    whole_keys, whole_values = (
        lax.all_gather(key_flat, "context", axis=0, tiled=True),
        lax.all_gather(value_flat, "context", axis=0, tiled=True),
    )
    key_block = min(512, seq_len)
    block_count = seq_len // key_block
    key_blocks = whole_keys.reshape(block_count, key_block, kv_heads, head_size)
    value_blocks = whole_values.reshape(block_count, key_block, kv_heads, head_size)
    block_firsts = key_block * jnp.arange(block_count, dtype=jnp.int32)

    def block_scores(keys_now, start_now):
        scores = (
            jnp.einsum("hrd,khd->hrk", query_arr, keys_now, preferred_element_type=f32)
            * score_scale
        )
        visible = (row_places[:, None] >= positions(start_now, key_block)[None, :])[None]
        return (scores, visible)

    def stat_block(state, packed):
        keys_now, start_now = packed
        running_max, running_total = state
        scores, visible = block_scores(keys_now, start_now)
        scores = jnp.where(visible, scores, very_negative)
        new_max = jnp.maximum(running_max, jnp.max(scores, axis=-1))
        weights = jnp.where(visible, jnp.exp(scores - new_max[..., None]), 0.0)
        running_total = running_total * jnp.exp(running_max - new_max) + jnp.sum(weights, axis=-1)
        return ((new_max, running_total), None)

    (att_max, att_total), unused = lax.scan(
        stat_block,
        (
            jnp.full((kv_heads, row_count_all), very_negative, f32),
            jnp.zeros((kv_heads, row_count_all), f32),
        ),
        (key_blocks, block_firsts),
    )
    log_total = att_max + jnp.log(att_total)

    def block_probs(keys_now, start_now):
        scores, visible = block_scores(keys_now, start_now)
        return jnp.where(visible, jnp.exp(scores - log_total[..., None]), 0.0)

    def attend_block(accum, packed):
        keys_now, values_now, start_now = packed
        probs_now = block_probs(keys_now, start_now)
        accum = accum + jnp.einsum(
            "hrk,khd->hrd", probs_now.astype(bf16), values_now, preferred_element_type=f32
        )
        return (accum, None)

    attended_output, unused = lax.scan(
        attend_block,
        jnp.zeros((kv_heads, row_count_all, head_size), f32),
        (key_blocks, value_blocks, block_firsts),
    )
    attn_low = token_rows_of(attended_output, kv_heads, query_group_count, tok_rows).astype(bf16)
    residual = inputs + jnp.dot(attn_low, out_full, preferred_element_type=f32)
    normed_post, post_inverse = norm_forward(residual, post_gain)
    mixed = normed_post.astype(bf16)
    logits = jnp.dot(mixed, router_full, preferred_element_type=f32)
    local_ids = expert_ids[0]
    chooser = (
        local_ids[:, :, None] == jnp.arange(device_count, dtype=jnp.int32)[None, None, :]
    ).astype(f32)
    chosen = jnp.sum(chooser * logits[:, None, :], axis=-1)
    gates = jax.nn.softmax(chosen, axis=-1)
    flat_ids = local_ids.reshape(-1)
    pair_hot = (flat_ids[:, None] == jnp.arange(device_count, dtype=jnp.int32)[None, :]).astype(
        jnp.int32
    )
    ranks = jnp.sum(jnp.cumsum(pair_hot, axis=0) * pair_hot, axis=1) - 1
    slots = flat_ids * capacity + ranks
    pair_rows = jnp.repeat(mixed, top_count, axis=0)
    outgoing = jnp.zeros((device_count * capacity, model_width), bf16).at[slots].set(pair_rows)
    arrived = lax.all_to_all(
        outgoing.reshape(device_count, capacity, model_width),
        ("context", "expert"),
        split_axis=0,
        concat_axis=0,
        tiled=True,
    )
    expert_rows = arrived.reshape(device_count * capacity, model_width)
    gate_pre = jnp.dot(expert_rows, w_gate[0], preferred_element_type=f32)
    up_pre = jnp.dot(expert_rows, w_up[0], preferred_element_type=f32)
    activated = jax.nn.silu(gate_pre)
    hidden = (activated * up_pre).astype(bf16)
    expert_out = jnp.dot(hidden, w_down[0], preferred_element_type=f32).astype(bf16)
    returned = lax.all_to_all(
        expert_out.reshape(device_count, capacity, model_width),
        ("context", "expert"),
        split_axis=0,
        concat_axis=0,
        tiled=True,
    )
    pair_out = (
        returned.reshape(device_count * capacity, model_width)[slots]
        .reshape(tok_rows, top_count, model_width)
        .astype(f32)
    )
    final = residual + jnp.sum(gates[..., None] * pair_out, axis=1)
    again = (
        lax.all_gather(w_query, ("context", "expert"), axis=0, tiled=True),
        lax.all_gather(key_projection_weight, ("context", "expert"), axis=0, tiled=True),
        lax.all_gather(value_projection_weight, ("context", "expert"), axis=0, tiled=True),
        lax.all_gather(w_out, ("context", "expert"), axis=0, tiled=True),
        lax.all_gather(w_router, ("context", "expert"), axis=0, tiled=True),
    )
    query_back, key_back, value_back, out_back, router_back = again
    upstream = cotangent[0].astype(f32)
    grad_gates = jnp.sum(upstream[:, None, :] * pair_out, axis=-1)
    pair_grads = (
        (upstream[:, None, :] * gates[..., None])
        .astype(bf16)
        .reshape(tok_rows * top_count, model_width)
    )
    grad_outgoing = (
        jnp.zeros((device_count * capacity, model_width), bf16).at[slots].set(pair_grads)
    )
    grad_arrived = lax.all_to_all(
        grad_outgoing.reshape(device_count, capacity, model_width),
        ("context", "expert"),
        split_axis=0,
        concat_axis=0,
        tiled=True,
    ).reshape(device_count * capacity, model_width)
    grad_w_down = jnp.einsum("rf,rd->fd", hidden, grad_arrived, preferred_element_type=f32)
    grad_hidden = jnp.einsum("rd,fd->rf", grad_arrived, w_down[0], preferred_element_type=f32)
    sigmoid = jax.nn.sigmoid(gate_pre)
    grad_gate = (grad_hidden * up_pre * sigmoid * (1.0 + gate_pre * (1.0 - sigmoid))).astype(bf16)
    grad_up = (grad_hidden * activated).astype(bf16)
    grad_w_gate = jnp.einsum("rd,rf->df", expert_rows, grad_gate, preferred_element_type=f32)
    grad_w_up = jnp.einsum("rd,rf->df", expert_rows, grad_up, preferred_element_type=f32)
    grad_rows = (
        jnp.einsum("rf,df->rd", grad_gate, w_gate[0], preferred_element_type=f32)
        + jnp.einsum("rf,df->rd", grad_up, w_up[0], preferred_element_type=f32)
    ).astype(bf16)
    grad_back = lax.all_to_all(
        grad_rows.reshape(device_count, capacity, model_width),
        ("context", "expert"),
        split_axis=0,
        concat_axis=0,
        tiled=True,
    )
    grad_mixed = jnp.sum(
        grad_back.reshape(device_count * capacity, model_width)[slots]
        .reshape(tok_rows, top_count, model_width)
        .astype(f32),
        axis=1,
    )
    grad_chosen = gates * (grad_gates - jnp.sum(gates * grad_gates, axis=-1, keepdims=True))
    grad_logits = jnp.sum(chooser * grad_chosen[..., None], axis=1).astype(bf16)
    grad_mixed = grad_mixed + jnp.einsum(
        "te,de->td", grad_logits, router_back, preferred_element_type=f32
    )
    grad_w_router = jnp.einsum("td,te->de", mixed, grad_logits, preferred_element_type=f32)
    grad_resid_norm, post_terms = norm_backward(residual, post_inverse, post_gain, grad_mixed)
    grad_residual = upstream + grad_resid_norm
    resid_low = grad_residual.astype(bf16)
    grad_w_out = jnp.einsum("tc,td->cd", attn_low, resid_low, preferred_element_type=f32)
    grad_attn = jnp.einsum("td,cd->tc", resid_low, out_back, preferred_element_type=f32).astype(
        bf16
    )
    grad_arr = head_rows(
        grad_attn.reshape(tok_rows, query_heads, head_size), kv_heads, query_group_count
    )

    def delta_block(total, packed):
        keys_now, values_now, start_now = packed
        probs_now = block_probs(keys_now, start_now)
        grad_probs = jnp.einsum("hrd,khd->hrk", grad_arr, values_now, preferred_element_type=f32)
        return (total + jnp.sum(probs_now * grad_probs, axis=-1), None)

    delta, unused = lax.scan(
        delta_block,
        jnp.zeros((kv_heads, row_count_all), f32),
        (key_blocks, value_blocks, block_firsts),
    )

    def back_block(grad_query, packed):
        keys_now, values_now, start_now = packed
        probs_now = block_probs(keys_now, start_now)
        grad_probs = jnp.einsum("hrd,khd->hrk", grad_arr, values_now, preferred_element_type=f32)
        grad_scores = (probs_now * (grad_probs - delta[..., None])).astype(bf16)
        grad_query = (
            grad_query
            + jnp.einsum("hrk,khd->hrd", grad_scores, keys_now, preferred_element_type=f32)
            * score_scale
        )
        grad_keys = (
            jnp.einsum("hrk,hrd->khd", grad_scores, query_arr, preferred_element_type=f32)
            * score_scale
        )
        grad_values = jnp.einsum(
            "hrk,hrd->khd", probs_now.astype(bf16), grad_arr, preferred_element_type=f32
        )
        return (
            grad_query,
            jnp.concatenate(
                [grad_keys.reshape(key_block, -1), grad_values.reshape(key_block, -1)], axis=-1
            ),
        )

    grad_query, key_terms = lax.scan(
        back_block,
        jnp.zeros((kv_heads, row_count_all, head_size), f32),
        (key_blocks, value_blocks, block_firsts),
    )
    own_terms = lax.psum_scatter(
        key_terms.reshape(seq_len, 2 * kv_heads * head_size),
        "context",
        scatter_dimension=0,
        tiled=True,
    )
    kv_width = kv_heads * head_size
    grad_key_rot = (
        own_terms[:, :kv_width].astype(bf16).astype(f32).reshape(tok_rows, kv_heads, head_size)
    )
    grad_value_low = own_terms[:, kv_width:].astype(bf16)
    grad_query_rot = token_rows_of(
        grad_query.astype(bf16).astype(f32), kv_heads, query_group_count, tok_rows
    ).reshape(tok_rows, query_heads, head_size)
    grad_query_raw, query_terms = norm_backward(
        query_raw, query_inverse, query_gain, rotate(grad_query_rot, cosine_table, sine_table, -1.0)
    )
    grad_key_raw, key_terms_gain = norm_backward(
        key_unrotated, key_inverse, key_gain, rotate(grad_key_rot, cosine_table, sine_table, -1.0)
    )
    grad_query_low = grad_query_raw.reshape(tok_rows, query_heads * head_size).astype(bf16)
    grad_key_low = grad_key_raw.reshape(tok_rows, kv_width).astype(bf16)
    grad_activation = (
        jnp.einsum("tc,dc->td", grad_query_low, query_back, preferred_element_type=f32)
        + jnp.einsum("tc,dc->td", grad_key_low, key_back, preferred_element_type=f32)
        + jnp.einsum("tc,dc->td", grad_value_low, value_back, preferred_element_type=f32)
    )
    grad_w_query = jnp.einsum(
        "td,tc->dc", activation_output, grad_query_low, preferred_element_type=f32
    )
    grad_w_key = jnp.einsum(
        "td,tc->dc", activation_output, grad_key_low, preferred_element_type=f32
    )
    grad_w_value = jnp.einsum(
        "td,tc->dc", activation_output, grad_value_low, preferred_element_type=f32
    )
    grad_input_norm, input_terms = norm_backward(inputs, input_inverse, norm_gain, grad_activation)
    grad_tokens = grad_residual + grad_input_norm
    shard_query, shard_key, shard_value, shard_out, shard_router = (
        lax.psum_scatter(grad_w_query, ("context", "expert"), scatter_dimension=0, tiled=True),
        lax.psum_scatter(grad_w_key, ("context", "expert"), scatter_dimension=0, tiled=True),
        lax.psum_scatter(grad_w_value, ("context", "expert"), scatter_dimension=0, tiled=True),
        lax.psum_scatter(grad_w_out, ("context", "expert"), scatter_dimension=0, tiled=True),
        lax.psum_scatter(grad_w_router, ("context", "expert"), scatter_dimension=0, tiled=True),
    )
    gain_norm, gain_post, gain_query, gain_key = lax.psum(
        (
            jnp.sum(input_terms, axis=0),
            jnp.sum(post_terms, axis=0),
            jnp.sum(query_terms, axis=(0, 1)),
            jnp.sum(key_terms_gain, axis=(0, 1)),
        ),
        ("context", "expert"),
    )
    return (
        final.astype(bf16)[None],
        grad_tokens[None],
        gain_norm,
        shard_query,
        shard_key,
        shard_value,
        gain_query,
        gain_key,
        shard_out,
        gain_post,
        shard_router,
        grad_w_gate[None],
        grad_w_up[None],
        grad_w_down[None],
    )


def placements(context, expert):
    whole = (*context, *expert)
    rows = P(expert, context, None)
    shard = P(whole, None)
    experts = P(whole, None, None)
    taken = (
        rows,
        P(expert, None),
        rows,
        P(),
        shard,
        shard,
        shard,
        P(),
        P(),
        shard,
        P(),
        shard,
        experts,
        experts,
        experts,
        rows,
    )
    given = (
        rows,
        rows,
        P(),
        shard,
        shard,
        shard,
        P(),
        P(),
        shard,
        P(),
        shard,
        experts,
        experts,
        experts,
    )
    return taken, given


def solution(mesh):
    context_size, expert_size = (mesh.shape["context"], mesh.shape["expert"])

    def step(*arrays):
        key_width, head_size = (arrays[5].shape[1], arrays[7].shape[0])
        own_head = key_width == context_size * head_size
        if own_head and context_size == 4 and expert_size % 2 == 0:
            devices = mesh.devices.reshape(2, 2, expert_size // 2, 2)
            used = Mesh(devices, both)
            taken, given = placements(context_axes, expert_axes)
            body = grouped
        else:
            used, body = (mesh, shards)
            taken, given = placements(("context",), ("expert",))
        return jax.shard_map(
            body, mesh=used, in_specs=taken, out_specs=given, check_vma=False
        )(*arrays)

    return step
```

```python
import functools

import jax
import jax.numpy as jnp
from jax import lax
from jax.experimental import pallas as pl
from jax.experimental.pallas import tpu as pltpu
from jax.sharding import Mesh
from jax.sharding import PartitionSpec as P

epsilon = 1e-06
rotary_base = 1000000.0
very_negative = -1e30


def norm_forward(values, scale_gain):
    inverse = lax.rsqrt(jnp.mean(values * values, axis=-1, keepdims=True) + epsilon)
    return (values * inverse * scale_gain, inverse)


def norm_backward(values, inverse, scale_gain, upstream):
    normed = values * inverse
    weighted = upstream * scale_gain
    inner = jnp.mean(weighted * normed, axis=-1, keepdims=True)
    return (inverse * (weighted - normed * inner), upstream * normed)


def rotary_tables(token_positions, head_width):
    half_width = head_width // 2
    frequency = rotary_base ** (-jnp.arange(half_width, dtype=jnp.float32) * 2.0 / head_width)
    angles = token_positions.astype(jnp.float32)[:, None] * frequency[None, :]
    return (jnp.cos(angles)[:, None, :], jnp.sin(angles)[:, None, :])


def rotate(values, cosine_table, sine_table, direction):
    half_width = values.shape[-1] // 2
    first_half = values[..., :half_width]
    second_half = values[..., half_width:]
    return jnp.concatenate(
        [
            first_half * cosine_table - direction * second_half * sine_table,
            second_half * cosine_table + direction * first_half * sine_table,
        ],
        axis=-1,
    )


def head_rows(array_in, kv_heads, query_group_count):
    row_total = array_in.shape[0]
    return (
        array_in.reshape(row_total, kv_heads, query_group_count, -1)
        .transpose(1, 2, 0, 3)
        .reshape(kv_heads, query_group_count * row_total, -1)
    )


def token_rows_of(array_in, kv_heads, query_group_count, tok_rows):
    return (
        array_in.reshape(kv_heads, query_group_count, tok_rows, -1)
        .transpose(2, 0, 1, 3)
        .reshape(tok_rows, -1)
    )


def dense_ranks(mask):
    width = mask.shape[-1]
    before = (
        jnp.arange(width, dtype=jnp.int32)[:, None] < jnp.arange(width, dtype=jnp.int32)[None, :]
    )
    return jnp.dot(
        mask.astype(jnp.bfloat16), before.astype(jnp.bfloat16), preferred_element_type=jnp.float32
    ).astype(jnp.int32)


context_axes = ("y", "x")
expert_axes = ("z", "core")
plane_axes = ("y", "x", "core")
both = context_axes + expert_axes
bf16 = jnp.bfloat16
f32 = jnp.float32


class Wires:
    def __init__(self, expert_size):
        self.layers = expert_size // 2
        self.context = lax.axis_index(context_axes)
        self.expert = lax.axis_index(expert_axes)
        self.core = self.expert % 2
        self.layer = self.expert // 2

    def pairs(self, move):
        found = []
        for y in range(2):
            for x in range(2):
                for z in range(self.layers):
                    for core in range(2):
                        there = move(y, x, z, core)
                        found.append((self.number(y, x, z, core), self.number(*there)))
        return found

    def number(self, y, x, z, core):
        return ((y * 2 + x) * self.layers + z) * 2 + core

    def send(self, value, move):
        return lax.ppermute(value, both, self.pairs(move))

    def swap(self, value):
        return self.send(value, lambda y, x, z, core: (y, x, z, 1 - core))

    def first(self, value):
        return self.send(
            value, lambda y, x, z, core: (y, 1 - x, z, core) if core else (1 - y, x, z, core)
        )

    def second(self, value):
        return self.send(
            value, lambda y, x, z, core: (1 - y, x, z, core) if core else (y, 1 - x, z, core)
        )

    def along(self, value, flip_y, flip_x):
        return self.send(value, lambda y, x, z, core: (y ^ flip_y, x ^ flip_x, z, core))

    def layer_flip(self, value, bit):
        return self.send(value, lambda y, x, z, core: (y, x, z ^ bit, core))

    def from_layer(self, value, step):
        return self.send(value, lambda y, x, z, core: (y, x, (z - step) % self.layers, core))

    def to_layer(self, value, step):
        return self.send(value, lambda y, x, z, core: (y, x, (z + step) % self.layers, core))

    def contexts(self, core):
        index = jnp.arange(4, dtype=jnp.int32)
        one, two = (index // 2, index % 2)
        swapped = two * 2 + one
        return self.context ^ jnp.where(core == 0, index, swapped)

    def blocks(self):
        found = []
        for step in range(self.layers):
            for flip in range(2):
                core = self.core ^ flip
                layer = (self.layer + step) % self.layers
                found.append(self.contexts(core) * (2 * self.layers) + layer * 2 + core)
        return jnp.concatenate(found)

    def gather_plane(self, value):
        crossed = self.second(value)
        return jnp.concatenate(
            [value, crossed, self.first(value), self.first(crossed)], axis=0
        )

    def scatter_plane(self, value, *after):
        half = value.shape[0] // 2
        quarter = half // 2
        there = self.first(value[half:])
        mine = tie(add_low(value[quarter:half], there[quarter:]), *after)
        kept = add_low(value[:quarter], there[:quarter])
        return kept.astype(f32) + self.second(mine).astype(f32)

    def turns(self):
        others = sorted(range(1, self.layers), key=lambda step: -min(step, self.layers - step))
        return [0] + others

    def layers_of(self, value, *after):
        found = [value]
        for turn, step in enumerate(self.turns()[1:]):
            start = tie(value, *found[-1:], *(after if turn > 0 else ()))
            found.append(self.from_layer(start, step))
        return found

    def scatter_rows(self, value):
        moves = [
            (self.context // 2, lambda part: self.along(part, 1, 0)),
            (self.context % 2, lambda part: self.along(part, 0, 1)),
        ]
        bit = self.layers // 2
        while bit:
            flip = functools.partial(self.layer_flip, bit=bit)
            moves.append((self.layer // bit % 2, flip))
            bit //= 2
        moves.append((self.core, self.swap))
        for side, move in moves:
            half = value.shape[0] // 2
            kept = lax.dynamic_slice_in_dim(value, side * half, half, axis=0)
            there = lax.dynamic_slice_in_dim(value, (1 - side) * half, half, axis=0)
            value = kept + move(there)
        return value

    def total(self, value):
        value = value + self.swap(value)
        value = value + self.along(value, 1, 0)
        value = value + self.along(value, 0, 1)
        bit = 1
        while bit < self.layers:
            value = value + self.layer_flip(value, bit)
            bit *= 2
        return value


def add_low(one, two):
    return (one.astype(f32) + two.astype(f32)).astype(bf16)


def tie(value, *after):
    return lax.optimization_barrier((value, *after))[0]


def sum_of_products(lefts, rights, tile):
    rows, height = lefts[0].shape
    width = rights[0].shape[1]
    parts = len(lefts)

    def body(*refs):
        total = None
        for left, right in zip(refs[:parts], refs[parts : 2 * parts]):
            term = lax.dot_general(
                left[...], right[...], (((0,), (0,)), ((), ())), preferred_element_type=f32
            )
            total = term if total is None else total + term
        refs[2 * parts][...] = total

    return pl.pallas_call(
        body,
        grid=(height // tile,),
        in_specs=[pl.BlockSpec((rows, tile), lambda i: (0, i))] * parts
        + [pl.BlockSpec((rows, width), lambda i: (0, 0))] * parts,
        out_specs=pl.BlockSpec((tile, width), lambda i: (i, 0)),
        out_shape=jax.ShapeDtypeStruct((height, width), f32),
        cost_estimate=pl.CostEstimate(
            flops=2 * parts * rows * height * width,
            bytes_accessed=2 * parts * rows * (height + width) + 4 * height * width,
            transcendentals=0,
        ),
        name="sum_of_products",
    )(*lefts, *rights)


def estimate(flops, moved):
    return pl.CostEstimate(flops=flops, bytes_accessed=moved, transcendentals=0)


def fixed(shape):
    return pl.BlockSpec(shape, lambda *i: (0,) * len(shape))


def add_pairs(nears, fars):
    count, (rows, width) = (len(nears), nears[0].shape)
    slab = rows // 2

    def body(*refs):
        for place in range(count):
            refs[-1][place] = add_low(refs[place][...], refs[count + place][...])

    return pl.pallas_call(
        body,
        grid=(rows // slab,),
        in_specs=[pl.BlockSpec((slab, width), lambda i: (i, 0))] * (2 * count),
        out_specs=pl.BlockSpec((count, slab, width), lambda i: (0, i, 0)),
        out_shape=jax.ShapeDtypeStruct((count, rows, width), bf16),
        cost_estimate=estimate(count * rows * width, 6 * count * rows * width),
        name="add_pairs",
    )(*nears, *fars).reshape(count * rows, width)


def pull_step(places, picks, tables, w_down):
    blocks, capacity, halves = picks.shape
    width, tile = (w_down.shape[2], 256)
    rows, hidden_width = (blocks * capacity, w_down.shape[1])

    def body(places_ref, picks_ref, *refs):
        down_ref, rows_ref, pulled_ref = refs[blocks:]

        @pl.when(pl.program_id(0) == 0)
        def _():
            for block in range(blocks):
                rows_ref[pl.ds(block * capacity, capacity), :] = jnp.dot(
                    picks_ref[block], refs[block][0], preferred_element_type=f32
                ).astype(bf16)

        pulled_ref[...] = lax.dot_general(
            rows_ref[...], down_ref[0], (((1,), (1,)), ((), ())), preferred_element_type=f32
        )

    def piece(block):
        return pl.BlockSpec((1, halves, width), lambda i, places_ref: (places_ref[block], 0, 0))

    return pl.pallas_call(
        body,
        grid_spec=pltpu.PrefetchScalarGridSpec(
            num_scalar_prefetch=1,
            grid=(hidden_width // tile,),
            in_specs=[fixed(picks.shape)]
            + [piece(block) for block in range(blocks)]
            + [pl.BlockSpec((1, tile, width), lambda i, places_ref: (0, i, 0))],
            out_specs=[
                fixed((rows, width)),
                pl.BlockSpec((rows, tile), lambda i, places_ref: (0, i)),
            ],
        ),
        out_shape=[
            jax.ShapeDtypeStruct((rows, width), bf16),
            jax.ShapeDtypeStruct((rows, hidden_width), f32),
        ],
        cost_estimate=estimate(2 * rows * width * (hidden_width + 2 * halves), 4 * rows * width),
        name="pull_step",
    )(places, picks, *tables, w_down)


def expert_step(picks, pieces, gate, pulled, w_gate, w_up, w_down, joined):
    blocks, capacity, halves = picks.shape
    width, tile, slab = (w_gate.shape[1], 256, 32)
    rows, hidden_width = (blocks * capacity, w_gate.shape[2])
    count = hidden_width // tile

    wide = 512
    tail = width // wide

    def body(picks_ref, *refs):
        gate_ref, pulled_ref, w_gate_ref, w_up_ref = refs[blocks : blocks + 4]
        gate_back_ref, up_back_ref, down_ref = refs[blocks + 4 : blocks + 7]
        rows_ref, weighted_ref, grad_gate_ref, grad_up_ref, dots_ref = refs[
            blocks + 7 : blocks + 12
        ]
        back_refs, (pre_ref, up_ref) = (refs[blocks + 12 : -2], refs[-2:])
        turn = pl.program_id(0)

        @pl.when(turn == 0)
        def _():
            dots_ref[...] = jnp.zeros_like(dots_ref)
            for block in range(blocks):
                rows_ref[pl.ds(block * capacity, capacity), :] = jnp.dot(
                    picks_ref[block], refs[block][...], preferred_element_type=f32
                ).astype(bf16)

        @pl.when(turn < count)
        def _():
            pre_ref[...] = jnp.dot(rows_ref[...], w_gate_ref[0], preferred_element_type=f32)
            up_ref[...] = jnp.dot(rows_ref[...], w_up_ref[0], preferred_element_type=f32)
            columns = pl.ds(pl.multiple_of(turn * tile, tile), tile)

            @pl.loop(0, rows // slab)
            def _(place):
                at = pl.ds(pl.multiple_of(place * slab, slab), slab)
                pre, up, gates, pull = (
                    pre_ref[at, :],
                    up_ref[at, :],
                    gate_ref[at, :],
                    pulled_ref[at, :],
                )
                sigmoid = jax.nn.sigmoid(pre)
                activated = pre * sigmoid
                hidden = activated * up
                dots_ref[at, :] += jnp.sum(hidden * pull, axis=1, keepdims=True)
                weighted_ref[at, columns] = (gates * hidden).astype(bf16)
                grad_hidden = gates * pull
                grad_gate_ref[at, columns] = (
                    grad_hidden * up * sigmoid * (1.0 + pre * (1.0 - sigmoid))
                ).astype(bf16)
                grad_up_ref[at, columns] = (grad_hidden * activated).astype(bf16)

        @pl.when(turn >= count)
        def _():
            across = (((1,), (1,)), ((), ()))
            pair = lax.dot_general(
                grad_gate_ref[...], gate_back_ref[0], across, preferred_element_type=f32
            ) + lax.dot_general(
                grad_up_ref[...], up_back_ref[0], across, preferred_element_type=f32
            )
            out = jnp.dot(weighted_ref[...], down_ref[0], preferred_element_type=f32)
            for side, table in enumerate((pair.astype(bf16), out.astype(bf16))):
                for block in range(blocks):
                    found = lax.dot_general(
                        picks_ref[block],
                        table[block * capacity : (block + 1) * capacity],
                        (((0,), (0,)), ((), ())),
                        preferred_element_type=f32,
                    ).astype(bf16)
                    if joined:
                        back_refs[block][pl.ds(side * halves, halves), :] = found
                    else:
                        back_refs[side * blocks + block][...] = found

    def ahead(i):
        return jnp.minimum(i, count - 1)

    def behind(i):
        return jnp.maximum(i - count, 0)

    weights = pl.BlockSpec((1, width, tile), lambda i: (0, 0, ahead(i)))
    weights_back = pl.BlockSpec((1, wide, hidden_width), lambda i: (0, behind(i), 0))
    narrow = jax.ShapeDtypeStruct((rows, hidden_width), bf16)
    back = [((2 if joined else 1) * halves, width)] * (blocks if joined else 2 * blocks)
    found = pl.pallas_call(
        body,
        grid=(count + tail,),
        in_specs=[fixed(picks.shape)]
        + [fixed((halves, width))] * blocks
        + [
            fixed((rows, 1)),
            pl.BlockSpec((rows, tile), lambda i: (0, ahead(i))),
            weights,
            weights,
            weights_back,
            weights_back,
            pl.BlockSpec((1, hidden_width, wide), lambda i: (0, 0, behind(i))),
        ],
        out_specs=[fixed((rows, width))]
        + [fixed((rows, hidden_width))] * 3
        + [fixed((rows, 1))]
        + [pl.BlockSpec((shape[0], wide), lambda i: (0, behind(i))) for shape in back],
        out_shape=[
            jax.ShapeDtypeStruct((rows, width), bf16),
            narrow,
            narrow,
            narrow,
            jax.ShapeDtypeStruct((rows, 1), f32),
        ]
        + [jax.ShapeDtypeStruct(shape, bf16) for shape in back],
        scratch_shapes=[pltpu.VMEM((rows, tile), f32), pltpu.VMEM((rows, tile), f32)],
        cost_estimate=estimate(10 * rows * width * hidden_width, 24 * rows * width),
        name="expert_step",
    )(picks, *pieces, gate, pulled, w_gate, w_up, w_gate, w_up, w_down)
    return (*found[:5], list(found[5:]))


def grouped(
    tokens,
    span_order,
    expert_ids,
    norm_gain,
    w_query,
    key_projection_weight,
    value_projection_weight,
    query_gain,
    key_gain,
    w_out,
    post_gain,
    w_router,
    w_gate,
    w_up,
    w_down,
    cotangent,
):
    tok_rows = tokens.shape[1]
    model_width = tokens.shape[2]
    head_size = query_gain.shape[0]
    top_count = expert_ids.shape[2]
    query_heads = w_query.shape[1] // head_size
    kv_heads = key_projection_weight.shape[1] // head_size
    group = query_heads // kv_heads
    context_size = lax.axis_size(context_axes)
    expert_size = lax.axis_size(expert_axes)
    device_count = context_size * expert_size
    wires = Wires(expert_size)
    layers = wires.layers
    chain = wires.turns()
    capacity = 2 * tok_rows * top_count // device_count
    seq_len = tok_rows * context_size
    span_rows = tok_rows // 2
    span_count = 2 * context_size
    order_row = span_order[0]
    score_scale = head_size ** (-0.5)
    shard_rows = w_query.shape[0]
    query_width = group * head_size
    part_width = query_width + 2 * head_size
    hidden_width = w_gate.shape[2]

    seq_tokens = wires.gather_plane(tokens[0])
    storage = (
        wires.contexts(wires.core)[:, None] * tok_rows
        + jnp.arange(tok_rows, dtype=jnp.int32)[None, :]
    ).reshape(-1)
    select = (storage // span_rows)[:, None] == jnp.arange(span_count, dtype=jnp.int32)[None, :]
    places = (
        jnp.sum(jnp.where(select, order_row[None, :], 0), axis=1) * span_rows + storage % span_rows
    )

    packed = jnp.concatenate(
        [
            w_query.reshape(shard_rows, context_size, query_width),
            key_projection_weight.reshape(shard_rows, context_size, head_size),
            value_projection_weight.reshape(shard_rows, context_size, head_size),
        ],
        axis=2,
    ).transpose(1, 0, 2)
    flips = wires.context ^ jnp.arange(context_size, dtype=jnp.int32)

    def exchange(parts):
        facing = jnp.take(parts, flips, axis=0)
        got = [facing[0]] + [
            wires.along(facing[flip], flip // 2, flip % 2) for flip in range(1, context_size)
        ]
        return jnp.take(jnp.stack(got), flips, axis=0)

    columns = exchange(packed)
    every_column = lax.all_gather(columns, expert_axes, axis=0, tiled=False)
    order = wires.blocks()
    chooser = (
        expert_ids[0][:, :, None] == jnp.arange(device_count, dtype=jnp.int32)[None, None, :]
    ).astype(f32)
    small = lax.all_to_all(
        jnp.concatenate(
            [
                jnp.sum(chooser, axis=1).T.astype(bf16),
                jnp.broadcast_to(w_router.reshape(1, -1), (device_count, w_router.size)),
            ],
            axis=1,
        ),
        both,
        split_axis=0,
        concat_axis=0,
        tiled=True,
    )
    router_full = small[:, tok_rows:].reshape(model_width, device_count)
    mine = jnp.take(small[:, :tok_rows], order, axis=0) > 0.5
    slot_of = dense_ranks(mine)
    picks_true = (
        slot_of[:, None, :] == jnp.arange(capacity, dtype=jnp.int32)[None, :, None]
    ) & mine[:, None, :]
    picks = picks_true.astype(bf16)
    picks_by = picks.reshape(layers, 8, capacity, tok_rows)
    count = layers

    class Plane:
        def __init__(self, column):
            self.near = [column]
            self.far = []

        def cross(self, *after):
            self.near.append(wires.second(tie(self.near[0], *after)))

        def finish(self, *after):
            self.near += [wires.first(tie(part, *after)) for part in self.near[:2]]

        def swap(self):
            self.far = [wires.swap(part) for part in self.near]

    def pull(turn, *after):
        step = chain[turn]
        if step == 0:
            plane = grad_planes[0]
            tables = [part[None] for part in plane.near + plane.far]
            places = 0 * order[:8]
        else:
            tables = [all_grads] * 8
            places = order[step * 8 : step * 8 + 8]
        found = pull_step(places, tie(picks_by[step], *after), tables, w_down)
        grad_rows[turn], pulled[turn] = found

    picks_by = tie(picks_by, router_full, seq_tokens)
    pulled, grad_rows = ([None] * count, [None] * count)
    grad_planes = {0: Plane(cotangent[0])}
    grad_planes[0].cross()
    grad_planes[0].finish()
    grad_planes[0].swap()
    pull(0)
    out_rows = lax.all_gather(tie(w_out, pulled[0]), expert_axes, axis=0, tiled=True)
    inputs = seq_tokens.astype(f32)
    normed_in, input_inverse = norm_forward(inputs, norm_gain)
    activation = normed_in.astype(bf16)
    every_column = tie(every_column, activation, pulled[0])
    w_qkv = every_column.transpose(1, 0, 2, 3).reshape(model_width, part_width)
    projected = jnp.dot(activation, w_qkv, preferred_element_type=f32)
    query_raw = projected[:, :query_width].reshape(seq_len, group, head_size).transpose(1, 0, 2)
    key_raw = projected[:, query_width : query_width + head_size]
    values = projected[:, query_width + head_size :].astype(bf16)
    cosine_table, sine_table = rotary_tables(places, head_size)
    cosine_table, sine_table = (cosine_table[:, 0], sine_table[:, 0])
    query_normed, query_inverse = norm_forward(query_raw, query_gain)
    key_normed, key_inverse = norm_forward(key_raw, key_gain)
    queries = rotate(query_normed, cosine_table, sine_table, 1.0).astype(bf16)
    keys = rotate(key_normed, cosine_table, sine_table, 1.0).astype(bf16)
    all_grads = lax.all_gather(tie(cotangent[0], queries), both, axis=0, tiled=False)
    visible = (places[:, None] >= places[None, :])[None]
    scores = jnp.einsum("htd,kd->htk", queries, keys, preferred_element_type=f32) * score_scale
    scores = jnp.where(visible, scores, very_negative)
    peak = jnp.max(scores, axis=-1, keepdims=True)
    weights = jnp.exp(scores - peak)
    probs = weights / jnp.sum(weights, axis=-1, keepdims=True)
    probs_low = probs.astype(bf16)
    attended = jnp.einsum("htk,kd->htd", probs_low, values, preferred_element_type=f32)
    attn_low = attended.astype(bf16).transpose(1, 0, 2).reshape(seq_len, query_width)
    out_part = jnp.dot(attn_low, out_rows, preferred_element_type=f32).astype(bf16)
    own_inputs = tokens[0].astype(f32)
    residual = own_inputs + wires.scatter_plane(out_part)
    normed_post, post_inverse = norm_forward(residual, post_gain)
    mixed = normed_post.astype(bf16)
    logits = jnp.dot(mixed, router_full, preferred_element_type=f32)
    chosen = jnp.sum(chooser * logits[:, None, :], axis=-1)
    gates = jax.nn.softmax(chosen, axis=-1)
    gates_dense = jnp.sum(chooser * gates[..., None], axis=1)
    gates_mine = lax.all_to_all(gates_dense.T, both, split_axis=0, concat_axis=0, tiled=True)
    mixed_columns = wires.layers_of(mixed)
    planes = [Plane(column) for column in mixed_columns]
    planes[0].cross()
    planes[0].finish()
    planes[0].swap()
    gates_mine = tie(gates_mine, *planes[0].near)
    gates_mine = jnp.take(gates_mine, order, axis=0)
    gate_rows = jnp.sum(jnp.where(picks_true, gates_mine[:, None, :], 0.0), axis=-1)
    gate_by = gate_rows.reshape(layers, 8 * capacity, 1)

    class Back:
        def __init__(self, step, parts):
            self.step, self.near = (step, parts[:4])
            self.swapped = [wires.swap(part) for part in parts[4:]]

        def first(self, *after):
            self.leaving = [add_pairs(self.near[2:], self.swapped[2:])]
            self.halved = [wires.first(tie(self.leaving[0], *after))]

        def second(self, *after):
            half = self.halved[0].reshape(2, *self.near[0].shape)
            self.kept = [
                (
                    self.near[part].astype(f32)
                    + self.swapped[part].astype(f32)
                    + half[part].astype(f32)
                ).astype(bf16)
                for part in (0, 1)
            ]
            self.crossed = wires.second(tie(self.kept[1], *after))

        def send(self, own):
            return own if self.step == 0 else wires.to_layer(own, self.step)

        def layer(self, *after):
            own = add_low(self.kept[0], self.crossed)
            self.sum = self.send(tie(own[:tok_rows], *after))
            self.rest = own[tok_rows:]

    expert_rows, weighted, grad_pre, grad_gate_rows, backs = ([], [], [], [], [])
    out_parts = []
    if count > 1:
        planes[1].cross()
    for turn, step in enumerate(chain):
        last = turn == count - 1
        waits = []
        if 0 < turn and not last:
            waits += planes[turn + 1].near[1:]
        if 0 < turn and last:
            waits += backs[turn - 1].swapped
        if turn > 1:
            waits += backs[turn - 2].halved
            backs[turn - 2].second()
        if turn > 2:
            waits.append(backs[turn - 3].crossed)
            backs[turn - 3].layer()
        if turn > 1 and last:
            waits.append(backs[turn - 2].crossed)
            backs[turn - 2].layer()
        pieces = planes[turn].near + planes[turn].far
        found = expert_step(
            picks_by[step],
            [tie(pieces[0], *waits)] + pieces[1:],
            gate_by[step],
            pulled[turn],
            w_gate,
            w_up,
            w_down,
            turn + 2 < count,
        )
        if not last:
            pull(turn + 1, found[0])
        expert_rows.append(found[0])
        weighted.append(found[1])
        grad_pre.append(found[2:4])
        grad_gate_rows.append(found[4])
        backs.append(Back(step, found[5][:8]))
        if turn + 2 >= count:
            out_parts.append(found[5][8:])
        if not last:
            planes[turn + 1].finish()
            planes[turn + 1].swap()
            if turn + 2 < count:
                planes[turn + 2].cross(found[0])
            waits = list(planes[turn + 1].near[2:])
        if turn > 0:
            backs[turn - 1].first()
        if not last:
            planes[turn + 1].near[0] = tie(planes[turn + 1].near[0], *waits)

    backs[-1].first()
    if count > 1:
        backs[-2].swapped[0] = tie(backs[-2].swapped[0], *backs[-1].leaving)
        backs[-2].second()
    backs[-1].second()
    grad_gate_rows[-1] = tie(grad_gate_rows[-1], *backs[-1].halved)
    by_step = dict(zip(chain, grad_gate_rows))
    grad_gate_all = jnp.concatenate([by_step[step] for step in range(layers)]).reshape(
        device_count, capacity
    )
    grad_gates_back = jnp.sum(jnp.where(picks_true, grad_gate_all[..., None], 0.0), axis=1)
    numbers = jnp.arange(device_count, dtype=jnp.int32)
    inverse = jnp.sum(jnp.where(order[:, None] == numbers[None, :], numbers[:, None], 0), axis=0)
    grad_gates_back = jnp.take(grad_gates_back, inverse, axis=0)
    grad_gates_dense = lax.all_to_all(
        grad_gates_back, both, split_axis=0, concat_axis=0, tiled=True
    ).T

    weighted[-1] = tie(weighted[-1], *backs[-1].halved)
    grad_w_down = sum_of_products(weighted, grad_rows, 256)
    for turn, back in enumerate(backs):
        if not hasattr(back, "sum"):
            if turn < count - 1:
                back.layer()
            else:
                own = tie(add_low(back.kept[0], back.crossed), grad_w_down)
                back.sum = back.send(own)
    grad_mixed = sum(back.sum.astype(f32) for back in backs)
    rest = [back.rest for back in backs[:-2]]
    out_backs = []
    for back, parts in zip(backs[-2:], out_parts):
        parts[4] = tie(parts[4], *backs[-1].swapped)
        out_backs.append(Back(back.step, parts))

    def send_late(turn):
        if turn < count - 2:
            rest[turn] = backs[turn].send(tie(rest[turn], grad_residual))
        return rest[turn : turn + 1]

    upstream = cotangent[0].astype(f32)
    grad_gates = jnp.sum(chooser * grad_gates_dense[:, None, :], axis=-1)
    grad_chosen = gates * (grad_gates - jnp.sum(gates * grad_gates, axis=-1, keepdims=True))
    grad_logits = jnp.sum(chooser * grad_chosen[..., None], axis=1).astype(bf16)
    grad_mixed = grad_mixed + jnp.einsum(
        "te,de->td", grad_logits, router_full, preferred_element_type=f32
    )
    grad_w_router = jnp.einsum("td,te->de", mixed, grad_logits, preferred_element_type=f32)
    grad_resid_norm, post_terms = norm_backward(residual, post_inverse, post_gain, grad_mixed)
    grad_residual = upstream + grad_resid_norm
    expert_rows[-1] = tie(expert_rows[-1], grad_residual)
    grad_w_gate = sum_of_products(expert_rows, [gate for gate, up in grad_pre], 256)
    resid_low = tie(wires.gather_plane(grad_residual.astype(bf16)), grad_w_gate)
    for turn, out_back in enumerate(out_backs):
        resid_low = tie(resid_low, *out_back.swapped, *send_late(turn))
        out_back.swapped[0] = tie(out_back.swapped[0], grad_residual)
        out_back.first()

    grad_w_out = jnp.einsum(
        "tc,td->cd", attn_low, resid_low, preferred_element_type=f32
    ).astype(bf16)
    shard_out = lax.psum_scatter(
        grad_w_out, expert_axes, scatter_dimension=0, tiled=True
    ).astype(f32)
    grad_attn = (
        jnp.einsum("td,cd->tc", resid_low, out_rows, preferred_element_type=f32)
        .astype(bf16)
        .reshape(seq_len, group, head_size)
        .transpose(1, 0, 2)
    )
    grad_probs = jnp.einsum("htd,kd->htk", grad_attn, values, preferred_element_type=f32)
    delta = jnp.sum(probs * grad_probs, axis=-1, keepdims=True)
    delta = tie(delta, grad_w_out, *[back.halved[0] for back in out_backs])
    for out_back in out_backs:
        out_back.second()
    grad_scores = (probs * (grad_probs - delta)).astype(bf16)
    grad_query = (
        jnp.einsum("htk,kd->htd", grad_scores, keys, preferred_element_type=f32) * score_scale
    ).astype(bf16)
    grad_key = (
        jnp.einsum("htk,htd->kd", grad_scores, queries, preferred_element_type=f32) * score_scale
    ).astype(bf16)
    grad_value = jnp.einsum(
        "htk,htd->kd", probs_low, grad_attn, preferred_element_type=f32
    ).astype(bf16)
    out_sums = []
    for out_back in out_backs:
        grad_query = tie(grad_query, out_back.crossed)
        out_sums.append(out_back.send(add_low(out_back.kept[0], out_back.crossed)))
    grad_query_raw, query_terms = norm_backward(
        query_raw,
        query_inverse,
        query_gain,
        rotate(grad_query.astype(f32), cosine_table, sine_table, -1.0),
    )
    grad_key_raw, key_terms = norm_backward(
        key_raw, key_inverse, key_gain, rotate(grad_key.astype(f32), cosine_table, sine_table, -1.0)
    )
    grad_parts = jnp.concatenate(
        [
            grad_query_raw.astype(bf16).transpose(1, 0, 2).reshape(seq_len, query_width),
            grad_key_raw.astype(bf16),
            grad_value,
        ],
        axis=1,
    )
    grad_parts = tie(grad_parts, *out_sums, shard_out)
    final = residual + sum(part.astype(f32) for part in out_sums + rest)
    activation_part = jnp.einsum("tc,dc->td", grad_parts, w_qkv, preferred_element_type=f32)
    expert_rows[-1] = tie(expert_rows[-1], activation_part)
    grad_w_up = sum_of_products(expert_rows, [up for gate, up in grad_pre], 256)
    grad_activation = wires.scatter_plane(activation_part.astype(bf16), grad_w_up)
    own_inverse = input_inverse[:tok_rows]
    grad_input_norm, unused = norm_backward(own_inputs, own_inverse, norm_gain, grad_activation)
    grad_tokens = grad_residual + grad_input_norm

    grad_w_qkv = jnp.einsum("td,tc->dc", activation, grad_parts, preferred_element_type=f32)
    column_sums = lax.psum_scatter(
        grad_w_qkv.astype(bf16)
        .reshape(context_size, expert_size, shard_rows, part_width)
        .transpose(1, 0, 2, 3)
        .reshape(model_width, part_width),
        expert_axes,
        scatter_dimension=0,
        tiled=True,
    ).reshape(context_size, shard_rows, part_width)
    shard_qkv = exchange(column_sums).transpose(1, 0, 2).astype(f32)
    shard_query = shard_qkv[:, :, :query_width].reshape(shard_rows, -1)
    shard_key = shard_qkv[:, :, query_width : query_width + head_size].reshape(shard_rows, -1)
    shard_value = shard_qkv[:, :, query_width + head_size :].reshape(shard_rows, -1)
    shard_router = wires.scatter_rows(
        tie(grad_w_router.reshape(device_count, -1), activation_part)
    ).reshape(shard_rows, device_count)
    gains = wires.total(
        jnp.concatenate(
            [
                jnp.sum(activation_part * (inputs * input_inverse), axis=0),
                jnp.sum(post_terms, axis=0),
                jnp.sum(query_terms, axis=(0, 1)),
                jnp.sum(key_terms, axis=0),
            ]
        )
    )
    gain_norm, gain_post, gain_query, gain_key = jnp.split(
        gains, [model_width, 2 * model_width, 2 * model_width + head_size]
    )
    return (
        final.astype(bf16)[None],
        grad_tokens[None],
        gain_norm,
        shard_query,
        shard_key,
        shard_value,
        gain_query,
        gain_key,
        shard_out,
        gain_post,
        shard_router,
        grad_w_gate[None],
        grad_w_up[None],
        grad_w_down[None],
    )


def shards(
    tokens,
    span_order,
    expert_ids,
    norm_gain,
    w_query,
    key_projection_weight,
    value_projection_weight,
    query_gain,
    key_gain,
    w_out,
    post_gain,
    w_router,
    w_gate,
    w_up,
    w_down,
    cotangent,
):
    tok_rows = tokens.shape[1]
    model_width = tokens.shape[2]
    head_size = query_gain.shape[0]
    top_count = expert_ids.shape[2]
    query_heads = w_query.shape[1] // head_size
    kv_heads = key_projection_weight.shape[1] // head_size
    query_group_count = query_heads // kv_heads
    context_size = lax.axis_size("context")
    device_count = lax.axis_size(("context", "expert"))
    capacity = max(2, 2 * tok_rows * top_count // device_count)
    seq_len = tok_rows * context_size
    span_rows = tok_rows // 2
    span_count = 2 * context_size
    order_row = span_order[0]
    score_scale = head_size ** (-0.5)
    bf16 = jnp.bfloat16
    f32 = jnp.float32

    def positions(first_row, row_count):
        storage = first_row + jnp.arange(row_count, dtype=jnp.int32)
        select = (storage // span_rows)[:, None] == jnp.arange(span_count, dtype=jnp.int32)[None, :]
        return (
            jnp.sum(jnp.where(select, order_row[None, :], 0), axis=1) * span_rows
            + storage % span_rows
        )

    query_places = positions(lax.axis_index("context") * tok_rows, tok_rows)
    row_places = jnp.tile(query_places, query_group_count)
    gathered = (
        lax.all_gather(w_query, ("context", "expert"), axis=0, tiled=True),
        lax.all_gather(key_projection_weight, ("context", "expert"), axis=0, tiled=True),
        lax.all_gather(value_projection_weight, ("context", "expert"), axis=0, tiled=True),
        lax.all_gather(w_out, ("context", "expert"), axis=0, tiled=True),
        lax.all_gather(w_router, ("context", "expert"), axis=0, tiled=True),
    )
    query_full, key_full, value_full, out_full, router_full = gathered
    inputs = tokens[0].astype(f32)
    normed_in, input_inverse = norm_forward(inputs, norm_gain)
    activation_output = normed_in.astype(bf16)
    query_raw = jnp.dot(activation_output, query_full, preferred_element_type=f32).reshape(
        tok_rows, query_heads, head_size
    )
    key_unrotated = jnp.dot(activation_output, key_full, preferred_element_type=f32).reshape(
        tok_rows, kv_heads, head_size
    )
    value_flat = jnp.dot(activation_output, value_full, preferred_element_type=f32).astype(bf16)
    cosine_table, sine_table = rotary_tables(query_places, head_size)
    query_normed, query_inverse = norm_forward(query_raw, query_gain)
    key_normed, key_inverse = norm_forward(key_unrotated, key_gain)
    query_prepared = rotate(query_normed, cosine_table, sine_table, 1.0).astype(bf16)
    key_flat = (
        rotate(key_normed, cosine_table, sine_table, 1.0)
        .astype(bf16)
        .reshape(tok_rows, kv_heads * head_size)
    )
    query_arr = head_rows(query_prepared, kv_heads, query_group_count)
    row_count_all = query_group_count * tok_rows
    whole_keys, whole_values = (
        lax.all_gather(key_flat, "context", axis=0, tiled=True),
        lax.all_gather(value_flat, "context", axis=0, tiled=True),
    )
    key_block = min(512, seq_len)
    block_count = seq_len // key_block
    key_blocks = whole_keys.reshape(block_count, key_block, kv_heads, head_size)
    value_blocks = whole_values.reshape(block_count, key_block, kv_heads, head_size)
    block_firsts = key_block * jnp.arange(block_count, dtype=jnp.int32)

    def block_scores(keys_now, start_now):
        scores = (
            jnp.einsum("hrd,khd->hrk", query_arr, keys_now, preferred_element_type=f32)
            * score_scale
        )
        visible = (row_places[:, None] >= positions(start_now, key_block)[None, :])[None]
        return (scores, visible)

    def stat_block(state, packed):
        keys_now, start_now = packed
        running_max, running_total = state
        scores, visible = block_scores(keys_now, start_now)
        scores = jnp.where(visible, scores, very_negative)
        new_max = jnp.maximum(running_max, jnp.max(scores, axis=-1))
        weights = jnp.where(visible, jnp.exp(scores - new_max[..., None]), 0.0)
        running_total = running_total * jnp.exp(running_max - new_max) + jnp.sum(weights, axis=-1)
        return ((new_max, running_total), None)

    (att_max, att_total), unused = lax.scan(
        stat_block,
        (
            jnp.full((kv_heads, row_count_all), very_negative, f32),
            jnp.zeros((kv_heads, row_count_all), f32),
        ),
        (key_blocks, block_firsts),
    )
    log_total = att_max + jnp.log(att_total)

    def block_probs(keys_now, start_now):
        scores, visible = block_scores(keys_now, start_now)
        return jnp.where(visible, jnp.exp(scores - log_total[..., None]), 0.0)

    def attend_block(accum, packed):
        keys_now, values_now, start_now = packed
        probs_now = block_probs(keys_now, start_now)
        accum = accum + jnp.einsum(
            "hrk,khd->hrd", probs_now.astype(bf16), values_now, preferred_element_type=f32
        )
        return (accum, None)

    attended_output, unused = lax.scan(
        attend_block,
        jnp.zeros((kv_heads, row_count_all, head_size), f32),
        (key_blocks, value_blocks, block_firsts),
    )
    attn_low = token_rows_of(attended_output, kv_heads, query_group_count, tok_rows).astype(bf16)
    residual = inputs + jnp.dot(attn_low, out_full, preferred_element_type=f32)
    normed_post, post_inverse = norm_forward(residual, post_gain)
    mixed = normed_post.astype(bf16)
    logits = jnp.dot(mixed, router_full, preferred_element_type=f32)
    local_ids = expert_ids[0]
    chooser = (
        local_ids[:, :, None] == jnp.arange(device_count, dtype=jnp.int32)[None, None, :]
    ).astype(f32)
    chosen = jnp.sum(chooser * logits[:, None, :], axis=-1)
    gates = jax.nn.softmax(chosen, axis=-1)
    flat_ids = local_ids.reshape(-1)
    pair_hot = (flat_ids[:, None] == jnp.arange(device_count, dtype=jnp.int32)[None, :]).astype(
        jnp.int32
    )
    ranks = jnp.sum(jnp.cumsum(pair_hot, axis=0) * pair_hot, axis=1) - 1
    slots = flat_ids * capacity + ranks
    pair_rows = jnp.repeat(mixed, top_count, axis=0)
    outgoing = jnp.zeros((device_count * capacity, model_width), bf16).at[slots].set(pair_rows)
    arrived = lax.all_to_all(
        outgoing.reshape(device_count, capacity, model_width),
        ("context", "expert"),
        split_axis=0,
        concat_axis=0,
        tiled=True,
    )
    expert_rows = arrived.reshape(device_count * capacity, model_width)
    gate_pre = jnp.dot(expert_rows, w_gate[0], preferred_element_type=f32)
    up_pre = jnp.dot(expert_rows, w_up[0], preferred_element_type=f32)
    activated = jax.nn.silu(gate_pre)
    hidden = (activated * up_pre).astype(bf16)
    expert_out = jnp.dot(hidden, w_down[0], preferred_element_type=f32).astype(bf16)
    returned = lax.all_to_all(
        expert_out.reshape(device_count, capacity, model_width),
        ("context", "expert"),
        split_axis=0,
        concat_axis=0,
        tiled=True,
    )
    pair_out = (
        returned.reshape(device_count * capacity, model_width)[slots]
        .reshape(tok_rows, top_count, model_width)
        .astype(f32)
    )
    final = residual + jnp.sum(gates[..., None] * pair_out, axis=1)
    again = (
        lax.all_gather(w_query, ("context", "expert"), axis=0, tiled=True),
        lax.all_gather(key_projection_weight, ("context", "expert"), axis=0, tiled=True),
        lax.all_gather(value_projection_weight, ("context", "expert"), axis=0, tiled=True),
        lax.all_gather(w_out, ("context", "expert"), axis=0, tiled=True),
        lax.all_gather(w_router, ("context", "expert"), axis=0, tiled=True),
    )
    query_back, key_back, value_back, out_back, router_back = again
    upstream = cotangent[0].astype(f32)
    grad_gates = jnp.sum(upstream[:, None, :] * pair_out, axis=-1)
    pair_grads = (
        (upstream[:, None, :] * gates[..., None])
        .astype(bf16)
        .reshape(tok_rows * top_count, model_width)
    )
    grad_outgoing = (
        jnp.zeros((device_count * capacity, model_width), bf16).at[slots].set(pair_grads)
    )
    grad_arrived = lax.all_to_all(
        grad_outgoing.reshape(device_count, capacity, model_width),
        ("context", "expert"),
        split_axis=0,
        concat_axis=0,
        tiled=True,
    ).reshape(device_count * capacity, model_width)
    grad_w_down = jnp.einsum("rf,rd->fd", hidden, grad_arrived, preferred_element_type=f32)
    grad_hidden = jnp.einsum("rd,fd->rf", grad_arrived, w_down[0], preferred_element_type=f32)
    sigmoid = jax.nn.sigmoid(gate_pre)
    grad_gate = (grad_hidden * up_pre * sigmoid * (1.0 + gate_pre * (1.0 - sigmoid))).astype(bf16)
    grad_up = (grad_hidden * activated).astype(bf16)
    grad_w_gate = jnp.einsum("rd,rf->df", expert_rows, grad_gate, preferred_element_type=f32)
    grad_w_up = jnp.einsum("rd,rf->df", expert_rows, grad_up, preferred_element_type=f32)
    grad_rows = (
        jnp.einsum("rf,df->rd", grad_gate, w_gate[0], preferred_element_type=f32)
        + jnp.einsum("rf,df->rd", grad_up, w_up[0], preferred_element_type=f32)
    ).astype(bf16)
    grad_back = lax.all_to_all(
        grad_rows.reshape(device_count, capacity, model_width),
        ("context", "expert"),
        split_axis=0,
        concat_axis=0,
        tiled=True,
    )
    grad_mixed = jnp.sum(
        grad_back.reshape(device_count * capacity, model_width)[slots]
        .reshape(tok_rows, top_count, model_width)
        .astype(f32),
        axis=1,
    )
    grad_chosen = gates * (grad_gates - jnp.sum(gates * grad_gates, axis=-1, keepdims=True))
    grad_logits = jnp.sum(chooser * grad_chosen[..., None], axis=1).astype(bf16)
    grad_mixed = grad_mixed + jnp.einsum(
        "te,de->td", grad_logits, router_back, preferred_element_type=f32
    )
    grad_w_router = jnp.einsum("td,te->de", mixed, grad_logits, preferred_element_type=f32)
    grad_resid_norm, post_terms = norm_backward(residual, post_inverse, post_gain, grad_mixed)
    grad_residual = upstream + grad_resid_norm
    resid_low = grad_residual.astype(bf16)
    grad_w_out = jnp.einsum("tc,td->cd", attn_low, resid_low, preferred_element_type=f32)
    grad_attn = jnp.einsum("td,cd->tc", resid_low, out_back, preferred_element_type=f32).astype(
        bf16
    )
    grad_arr = head_rows(
        grad_attn.reshape(tok_rows, query_heads, head_size), kv_heads, query_group_count
    )

    def delta_block(total, packed):
        keys_now, values_now, start_now = packed
        probs_now = block_probs(keys_now, start_now)
        grad_probs = jnp.einsum("hrd,khd->hrk", grad_arr, values_now, preferred_element_type=f32)
        return (total + jnp.sum(probs_now * grad_probs, axis=-1), None)

    delta, unused = lax.scan(
        delta_block,
        jnp.zeros((kv_heads, row_count_all), f32),
        (key_blocks, value_blocks, block_firsts),
    )

    def back_block(grad_query, packed):
        keys_now, values_now, start_now = packed
        probs_now = block_probs(keys_now, start_now)
        grad_probs = jnp.einsum("hrd,khd->hrk", grad_arr, values_now, preferred_element_type=f32)
        grad_scores = (probs_now * (grad_probs - delta[..., None])).astype(bf16)
        grad_query = (
            grad_query
            + jnp.einsum("hrk,khd->hrd", grad_scores, keys_now, preferred_element_type=f32)
            * score_scale
        )
        grad_keys = (
            jnp.einsum("hrk,hrd->khd", grad_scores, query_arr, preferred_element_type=f32)
            * score_scale
        )
        grad_values = jnp.einsum(
            "hrk,hrd->khd", probs_now.astype(bf16), grad_arr, preferred_element_type=f32
        )
        return (
            grad_query,
            jnp.concatenate(
                [grad_keys.reshape(key_block, -1), grad_values.reshape(key_block, -1)], axis=-1
            ),
        )

    grad_query, key_terms = lax.scan(
        back_block,
        jnp.zeros((kv_heads, row_count_all, head_size), f32),
        (key_blocks, value_blocks, block_firsts),
    )
    own_terms = lax.psum_scatter(
        key_terms.reshape(seq_len, 2 * kv_heads * head_size),
        "context",
        scatter_dimension=0,
        tiled=True,
    )
    kv_width = kv_heads * head_size
    grad_key_rot = (
        own_terms[:, :kv_width].astype(bf16).astype(f32).reshape(tok_rows, kv_heads, head_size)
    )
    grad_value_low = own_terms[:, kv_width:].astype(bf16)
    grad_query_rot = token_rows_of(
        grad_query.astype(bf16).astype(f32), kv_heads, query_group_count, tok_rows
    ).reshape(tok_rows, query_heads, head_size)
    grad_query_raw, query_terms = norm_backward(
        query_raw, query_inverse, query_gain, rotate(grad_query_rot, cosine_table, sine_table, -1.0)
    )
    grad_key_raw, key_terms_gain = norm_backward(
        key_unrotated, key_inverse, key_gain, rotate(grad_key_rot, cosine_table, sine_table, -1.0)
    )
    grad_query_low = grad_query_raw.reshape(tok_rows, query_heads * head_size).astype(bf16)
    grad_key_low = grad_key_raw.reshape(tok_rows, kv_width).astype(bf16)
    grad_activation = (
        jnp.einsum("tc,dc->td", grad_query_low, query_back, preferred_element_type=f32)
        + jnp.einsum("tc,dc->td", grad_key_low, key_back, preferred_element_type=f32)
        + jnp.einsum("tc,dc->td", grad_value_low, value_back, preferred_element_type=f32)
    )
    grad_w_query = jnp.einsum(
        "td,tc->dc", activation_output, grad_query_low, preferred_element_type=f32
    )
    grad_w_key = jnp.einsum(
        "td,tc->dc", activation_output, grad_key_low, preferred_element_type=f32
    )
    grad_w_value = jnp.einsum(
        "td,tc->dc", activation_output, grad_value_low, preferred_element_type=f32
    )
    grad_input_norm, input_terms = norm_backward(inputs, input_inverse, norm_gain, grad_activation)
    grad_tokens = grad_residual + grad_input_norm
    shard_query, shard_key, shard_value, shard_out, shard_router = (
        lax.psum_scatter(grad_w_query, ("context", "expert"), scatter_dimension=0, tiled=True),
        lax.psum_scatter(grad_w_key, ("context", "expert"), scatter_dimension=0, tiled=True),
        lax.psum_scatter(grad_w_value, ("context", "expert"), scatter_dimension=0, tiled=True),
        lax.psum_scatter(grad_w_out, ("context", "expert"), scatter_dimension=0, tiled=True),
        lax.psum_scatter(grad_w_router, ("context", "expert"), scatter_dimension=0, tiled=True),
    )
    gain_norm, gain_post, gain_query, gain_key = lax.psum(
        (
            jnp.sum(input_terms, axis=0),
            jnp.sum(post_terms, axis=0),
            jnp.sum(query_terms, axis=(0, 1)),
            jnp.sum(key_terms_gain, axis=(0, 1)),
        ),
        ("context", "expert"),
    )
    return (
        final.astype(bf16)[None],
        grad_tokens[None],
        gain_norm,
        shard_query,
        shard_key,
        shard_value,
        gain_query,
        gain_key,
        shard_out,
        gain_post,
        shard_router,
        grad_w_gate[None],
        grad_w_up[None],
        grad_w_down[None],
    )


def placements(context, expert):
    whole = (*context, *expert)
    rows = P(expert, context, None)
    shard = P(whole, None)
    experts = P(whole, None, None)
    taken = (
        rows,
        P(expert, None),
        rows,
        P(),
        shard,
        shard,
        shard,
        P(),
        P(),
        shard,
        P(),
        shard,
        experts,
        experts,
        experts,
        rows,
    )
    given = (
        rows,
        rows,
        P(),
        shard,
        shard,
        shard,
        P(),
        P(),
        shard,
        P(),
        shard,
        experts,
        experts,
        experts,
    )
    return taken, given


def solution(mesh):
    context_size, expert_size = (mesh.shape["context"], mesh.shape["expert"])

    def step(*arrays):
        key_width, head_size = (arrays[5].shape[1], arrays[7].shape[0])
        own_head = key_width == context_size * head_size
        if own_head and context_size == 4 and expert_size % 2 == 0:
            devices = mesh.devices.reshape(2, 2, expert_size // 2, 2)
            used = Mesh(devices, both)
            taken, given = placements(context_axes, expert_axes)
            body = grouped
        else:
            used, body = (mesh, shards)
            taken, given = placements(("context",), ("expert",))
        return jax.shard_map(
            body, mesh=used, in_specs=taken, out_specs=given, check_vma=False
        )(*arrays)

    return step
```
